256 devices in a mesh: dom: 64 (over z, y, core), edge: 4 (over x).
Axes of the slice: x: 4, y: 4, z: 8, core: 2. Of those that a mesh axis runs over, the one named last changes fastest.
Arguments:
- fine_nodes: bfloat16 [524288, 128], P('dom'), may hold values from -6 to 6
- fine_edges: bfloat16 [1048576, 128], P(('dom', 'edge')), may hold values from -6 to 6
- fine_senders: int32 [1048576], P(('dom', 'edge')), may hold values from 0 to 12287, as said below
- fine_receivers: int32 [1048576], P(('dom', 'edge')), may hold values from 0 to 8191
- fine_halo: int32 [64, 64, 64], P('dom'), may hold values from 0 to 8191
- coarse_edges: bfloat16 [262144, 128], P(('dom', 'edge')), may hold values from -6 to 6
- coarse_senders: int32 [262144], P(('dom', 'edge')), may hold values from 0 to 4095, as said below
- coarse_receivers: int32 [262144], P(('dom', 'edge')), may hold values from 0 to 2047
- coarse_halo: int32 [64, 64, 32], P('dom'), may hold values from 0 to 2047
- pool_send: int32 [64, 64, 192], P('dom'), may hold values from 0 to 8191, as said below
- pool_dest: int32 [64, 64, 192], P('dom'), may hold values from 0 to 2048, as said below
- unpool_slot: int32 [524288], P('dom'), may hold values from 0 to 12287, as said below
- edge_in_weight: bfloat16 [2, 384, 128], replicated, may hold values from -0.3125 to 0.3125
- edge_out_weight: bfloat16 [2, 128, 128], replicated, may hold values from -0.5 to 0.5
- node_in_weight: bfloat16 [2, 256, 128], replicated, may hold values from -0.375 to 0.375
- node_out_weight: bfloat16 [2, 128, 128], replicated, may hold values from -0.5 to 0.5
- edge_gain: float32 [2, 128], replicated, may hold values from 0.5 to 1.5
- node_gain: float32 [2, 128], replicated, may hold values from 0.5 to 1.5
Outputs:
- fine_out: bfloat16 [524288, 128], P('dom')
- coarse_out: bfloat16 [131072, 128], P('dom')
The draws below stay inside these ranges and needn't reach their ends.
Inputs may be any that keep to these rules, and one draw needn't show every extreme that they name: `fine_senders`: an entry below 8192 is a row of the edge's own partition; an entry 8192 + d * 64 + s names slot s of fine_halo[d, p] for the edge's partition p. `coarse_senders`: an entry below 2048 is a row of the edge's own coarse partition; an entry 2048 + d * 32 + s names slot s of coarse_halo[d, p]. pool_send[d, p, s] is a row of partition d. For each pair (d, p) the slots that carry data come first and number at most 192; in every draw some p receives 192 from every d. Every row of partition d is carried exactly once over all p and s; empty slots hold 0. pool_dest[p, d, s] is 2048 exactly where slot s of pool_send[d, p] is empty, else a row of coarse partition p. `unpool_slot`: row r of partition d holds p * 192 + s for the one carrying slot with pool_send[d, p, s] = r.
All inputs are finite; a program needn't handle non-finite values.
Results may differ from the reference program's by a relative error of at most 0.0068.
Values may be sent and summed in bfloat16 or wider, within the bound.
A program may use at most 64 MiB of HBM per device.

```python
import jax
import jax.numpy as jnp
from jax import lax

H = 128
FINE_DEV = 8192
EDGE_DEV = 4096
COARSE = 2048
CEDGE_DEV = 1024
HALO = 64
CHALO = 32
GHOSTS = 4096
CGHOSTS = 2048
PS = 192
NF = 524288
NE = 1048576
NCE = 262144
N_DOM = 64
N_EDGE = 4


def sender_mix(key, rows, ghosts, total):
    first, second, third = jax.random.split(key, 3)
    near = jax.random.randint(first, (total,), 0, rows, dtype=jnp.int32)
    far = rows + jax.random.randint(second, (total,), 0, ghosts, dtype=jnp.int32)
    pick = jax.random.randint(third, (total,), 0, 4, dtype=jnp.int32)
    return jnp.where(pick == 0, far, near).astype(jnp.int32)


def draw_fine_senders(key, part):
    return sender_mix(jax.random.fold_in(key, 11), FINE_DEV, GHOSTS, EDGE_DEV * N_DOM * N_EDGE)


def draw_coarse_senders(key, part):
    return sender_mix(jax.random.fold_in(key, 12), COARSE, CGHOSTS, CEDGE_DEV * N_DOM * N_EDGE)


def pool_layout(key):
    base_key = jax.random.fold_in(key, 7)
    first, second, third, fourth = jax.random.split(base_key, 4)
    pairs = N_DOM // 2
    base = FINE_DEV // N_DOM
    small = base // 2
    chosen = jax.random.randint(first, (), 0, pairs, dtype=jnp.int32)
    flips = jax.random.randint(second, (N_DOM, pairs), 0, 2, dtype=jnp.int32)
    flips = jnp.where(jnp.arange(pairs, dtype=jnp.int32)[None, :] == chosen, 1, flips)
    even_count = jnp.where(flips == 1, PS, small)
    odd_count = jnp.where(flips == 1, small, PS)
    counts = jnp.stack([even_count, odd_count], axis=-1).reshape(N_DOM, N_DOM).astype(jnp.int32)
    starts = (jnp.cumsum(counts, axis=1) - counts).astype(jnp.int32)
    orders = jax.vmap(lambda k: jax.random.permutation(k, jnp.arange(FINE_DEV, dtype=jnp.int32)))(jax.random.split(third, N_DOM))
    slots = jnp.arange(PS, dtype=jnp.int32)
    valid = slots[None, None, :] < counts[:, :, None]
    spots = jnp.minimum(starts[:, :, None] + slots[None, None, :], FINE_DEV - 1)
    picked = jax.vmap(lambda order, spot: order[spot])(orders, spots)
    send = jnp.where(valid, picked, 0).astype(jnp.int32)
    ranks = jnp.arange(FINE_DEV, dtype=jnp.int32)

    def slot_of(start, order):
        owner = (jnp.sum((start[None, :] <= ranks[:, None]).astype(jnp.int32), axis=1) - 1).astype(jnp.int32)
        offset = ranks - start[owner]
        value = (owner * PS + offset).astype(jnp.int32)
        return jnp.zeros((FINE_DEV,), jnp.int32).at[order].set(value)
    unpool = jax.vmap(slot_of)(starts, orders).reshape(-1).astype(jnp.int32)
    places = jax.random.randint(fourth, (N_DOM, N_DOM, PS), 0, COARSE, dtype=jnp.int32)
    dest = jnp.where(jnp.transpose(valid, (1, 0, 2)), places, COARSE).astype(jnp.int32)
    return (send, dest, unpool)


def draw_pool_send(key, part):
    return pool_layout(key)[0]


def draw_pool_dest(key, part):
    return pool_layout(key)[1]


def draw_unpool_slot(key, part):
    return pool_layout(key)[2]


def touch_ends(drawn, rng, low, top_value):
    dims = drawn.shape
    spot = [jax.random.randint(jax.random.fold_in(rng, axis), (), 0, dims[axis]) for axis in range(len(dims))]
    drawn = drawn.at[tuple(spot)].set(low)
    longest = dims.index(max(dims))
    spot[longest] = (spot[longest] + 1) % dims[longest]
    return drawn.at[tuple(spot)].set(top_value)


def steps_of(stream_key, shape, pieces, least, high):
    level = 1.0
    for axis_at, blocks in pieces:
        draws = jax.random.uniform(jax.random.fold_in(jax.random.fold_in(stream_key, 6), axis_at), (blocks,), jnp.float32, least / len(pieces), high / len(pieces))
        level = level * jnp.repeat(jnp.exp(draws), shape[axis_at] // blocks).reshape((-1,) + (1,) * (len(shape) - 1 - axis_at))
    return level


def noise(rng, shape, scale, limit, shards=(), kind=jnp.bfloat16):
    entries = scale * jax.random.normal(rng, shape, jnp.float32)
    if shards:
        entries = entries * steps_of(rng, shape, shards, -0.22, 0.18)
    return jnp.clip(entries, -limit, limit).astype(kind)


def setup_inputs(seed: int = 0) -> dict:
    key_list = jax.random.split(jax.random.key(seed), 19)
    fine_nodes = noise(key_list[0], (NF, H), 1.0, 6.0, ((0, 64),))
    fine_edges = noise(key_list[1], (NE, H), 1.0, 6.0, ((0, 256),))
    fine_senders = draw_fine_senders(jax.random.fold_in(key_list[18], 71), 0)
    fine_receivers = touch_ends(jax.random.randint(key_list[3], (NE,), 0, FINE_DEV), jax.random.fold_in(key_list[3], 1), 0, FINE_DEV - 1).astype(jnp.int32)
    fine_halo = touch_ends(jax.random.randint(key_list[4], (N_DOM, N_DOM, HALO), 0, FINE_DEV), jax.random.fold_in(key_list[4], 1), 0, FINE_DEV - 1).astype(jnp.int32)
    coarse_edges = noise(key_list[5], (NCE, H), 1.0, 6.0, ((0, 256),))
    coarse_senders = draw_coarse_senders(jax.random.fold_in(key_list[18], 71), 0)
    coarse_receivers = touch_ends(jax.random.randint(key_list[7], (NCE,), 0, COARSE), jax.random.fold_in(key_list[7], 1), 0, COARSE - 1).astype(jnp.int32)
    coarse_halo = touch_ends(jax.random.randint(key_list[8], (N_DOM, N_DOM, CHALO), 0, COARSE), jax.random.fold_in(key_list[8], 1), 0, COARSE - 1).astype(jnp.int32)
    pool_send = draw_pool_send(jax.random.fold_in(key_list[18], 71), 0)
    pool_dest = draw_pool_dest(jax.random.fold_in(key_list[18], 71), 0)
    unpool_slot = draw_unpool_slot(jax.random.fold_in(key_list[18], 71), 0)
    edge_in_weight = noise(key_list[12], (2, 3 * H, H), (3 * H) ** -0.5, 0.3125)
    edge_out_weight = noise(key_list[13], (2, H, H), H ** -0.5, 0.5)
    node_in_weight = noise(key_list[14], (2, 2 * H, H), (2 * H) ** -0.5, 0.375)
    node_out_weight = noise(key_list[15], (2, H, H), H ** -0.5, 0.5)
    edge_gain = jnp.clip(1.0 + 0.1 * jax.random.normal(key_list[16], (2, H), jnp.float32), 0.5, 1.5)
    node_gain = jnp.clip(1.0 + 0.1 * jax.random.normal(key_list[17], (2, H), jnp.float32), 0.5, 1.5)
    return {"fine_nodes": fine_nodes, "fine_edges": fine_edges, "fine_senders": fine_senders, "fine_receivers": fine_receivers, "fine_halo": fine_halo, "coarse_edges": coarse_edges, "coarse_senders": coarse_senders, "coarse_receivers": coarse_receivers, "coarse_halo": coarse_halo, "pool_send": pool_send, "pool_dest": pool_dest, "unpool_slot": unpool_slot, "edge_in_weight": edge_in_weight, "edge_out_weight": edge_out_weight, "node_in_weight": node_in_weight, "node_out_weight": node_out_weight, "edge_gain": edge_gain, "node_gain": node_gain}


def layer_norm(values, gain):
    center = values - lax.optimization_barrier(jnp.mean(values, axis=-1, keepdims=True))
    spread = lax.optimization_barrier(jnp.mean(center * center, axis=-1, keepdims=True))
    return center * lax.rsqrt(spread + 1e-05) * gain

def node_update(rows, summed, w_first, w_second, gain):
    inputs = jnp.concatenate([rows, summed.astype(jnp.bfloat16)], axis=1)
    hidden = jax.nn.silu(jnp.dot(inputs, w_first, preferred_element_type=jnp.float32)).astype(jnp.bfloat16)
    result = layer_norm(jnp.dot(hidden, w_second, preferred_element_type=jnp.float32), gain)
    return (rows.astype(jnp.float32) + result).astype(jnp.bfloat16)

def graph_layer(nodes, edges, senders, receivers, border, level, weights):
    edge_in_weight, edge_out_weight, node_in_weight, node_out_weight, edge_gain, node_gain = weights
    width = nodes.shape[-1]
    parts = nodes.reshape(N_DOM, -1, width)
    row_count = parts.shape[1]
    sent = jax.vmap(lambda rows, index: rows[index])(parts, border)
    ghosts = jnp.transpose(sent, (1, 0, 2, 3)).reshape(N_DOM, -1, width)
    edge_parts = edges.reshape(N_DOM, -1, width)
    send_parts = senders.reshape(N_DOM, -1)
    recv_parts = receivers.reshape(N_DOM, -1)

    def one_part(items):
        rows, ghost, edge_rows, sender, receiver = items
        table = jnp.concatenate([rows, ghost], axis=0)
        inputs = jnp.concatenate([table[sender], rows[receiver], edge_rows], axis=1)
        hidden = jax.nn.silu(jnp.dot(inputs, edge_in_weight[level], preferred_element_type=jnp.float32)).astype(jnp.bfloat16)
        message = layer_norm(jnp.dot(hidden, edge_out_weight[level], preferred_element_type=jnp.float32), edge_gain[level])
        summed = jax.ops.segment_sum(message, receiver, num_segments=row_count)
        return node_update(rows, summed, node_in_weight[level], node_out_weight[level], node_gain[level])
    result = lax.map(one_part, (parts, ghosts, edge_parts, send_parts, recv_parts))
    return result.reshape(-1, width)

def reference(fine_nodes, fine_edges, fine_senders, fine_receivers, fine_halo, coarse_edges, coarse_senders, coarse_receivers, coarse_halo, pool_send, pool_dest, unpool_slot, edge_in_weight, edge_out_weight, node_in_weight, node_out_weight, edge_gain, node_gain):
    weights = (edge_in_weight, edge_out_weight, node_in_weight, node_out_weight, edge_gain, node_gain)
    width = fine_nodes.shape[-1]
    fine_mid = graph_layer(fine_nodes, fine_edges, fine_senders, fine_receivers, fine_halo, 0, weights)
    mid_parts = fine_mid.reshape(N_DOM, -1, width)

    def pool_one(target):
        rows = jax.vmap(lambda part, index: part[index])(mid_parts, pool_send[:, target, :])
        places = pool_dest[target].reshape(-1)
        sums = jax.ops.segment_sum(rows.reshape(-1, width).astype(jnp.float32), places, num_segments=COARSE + 1)[:COARSE]
        counts = jax.ops.segment_sum(jnp.ones_like(places), places, num_segments=COARSE + 1)[:COARSE]
        return (sums / jnp.maximum(counts, 1).astype(jnp.float32)[:, None]).astype(jnp.bfloat16)
    coarse_in = lax.map(pool_one, jnp.arange(N_DOM, dtype=jnp.int32)).reshape(-1, width)
    coarse_out = graph_layer(coarse_in, coarse_edges, coarse_senders, coarse_receivers, coarse_halo, 1, weights)
    source = (jnp.arange(NF, dtype=jnp.int32) // FINE_DEV).astype(jnp.int32)
    target = (unpool_slot // PS).astype(jnp.int32)
    within = (unpool_slot % PS).astype(jnp.int32)
    place = pool_dest[target, source, within]
    parents = coarse_out[(target * COARSE + place).astype(jnp.int32)]
    fine_out = (fine_mid.astype(jnp.float32) + parents.astype(jnp.float32)).astype(jnp.bfloat16)
    return (fine_out, coarse_out)
```

```python
import functools

import jax
import jax.numpy as jnp
from jax import lax
from jax.experimental import pallas as pl
from jax.experimental.pallas import tpu as pltpu
from jax.sharding import PartitionSpec as P

F32, BF16 = jnp.float32, jnp.bfloat16
VMEM = pl.BlockSpec(memory_space=pltpu.VMEM)
SMEM = pl.BlockSpec(memory_space=pltpu.SMEM)
LANES = 128


def silu(v):
    return v / (1.0 + jnp.exp(-v))


def normed(v, gain):
    center = v - jnp.mean(v, axis=-1, keepdims=True)
    spread = jnp.mean(center * center, axis=-1, keepdims=True)
    return center * lax.rsqrt(spread + 1e-05) * gain


def dot(a, b):
    return jnp.dot(a, b, preferred_element_type=F32)


def node_mlp(rows, summed, w_in, w_out, gain):
    pre = dot(rows, w_in[0:LANES, :]) + dot(summed.astype(BF16), w_in[LANES : 2 * LANES, :])
    hidden = silu(pre).astype(BF16)
    return (rows.astype(F32) + normed(dot(hidden, w_out), gain)).astype(BF16)


def row_loop(total, step, body):
    def run(i, carry):
        body(pl.multiple_of(i * step, step))
        return carry

    lax.fori_loop(0, total // step, run, 0)


def widen(src, dst, step=512):
    def body(at):
        dst[pl.ds(at, step), :] = src[pl.ds(at, step), :].astype(F32)

    row_loop(src.shape[0], step, body)


def gather_rows(index, table, dst, count, unroll=16):
    def body(at):
        for j in range(unroll):
            dst[pl.ds(at + j, 1), :] = table[pl.ds(index[at + j], 1), :]

    row_loop(count, unroll, body)


def clear_all(accs, step=512):
    def body(at):
        for acc in accs:
            acc[pl.ds(at, step), :] = jnp.zeros((step, LANES), F32)

    row_loop(accs[0].shape[0] // step * step, step, body)


def add_rows(where, values, count, accs, unroll=16):
    def body(at):
        for j in range(0, unroll, 2):
            acc = accs[(j // 2) % len(accs)]
            first, second = where(at + j), where(at + j + 1)
            value = acc[pl.ds(first, 1), :] + values[pl.ds(at + j, 1), :]
            other = acc[pl.ds(second, 1), :]
            other = jnp.where(first == second, value, other) + values[pl.ds(at + j + 1, 1), :]
            acc[pl.ds(first, 1), :] = value
            acc[pl.ds(second, 1), :] = other

    row_loop(count, unroll, body)


def sum_accs(accs, out, step=512):
    def body(at):
        value = accs[0][pl.ds(at, step), :]
        for acc in accs[1:]:
            value = value + acc[pl.ds(at, step), :]
        out[pl.ds(at, step), :] = value.astype(BF16)

    row_loop(out.shape[0], step, body)


def premultiply(rows, weight, dst, base=0, step=512):
    def body(at):
        dst[pl.ds(pl.multiple_of(base + at, step), step), :] = dot(rows[pl.ds(at, step), :], weight)

    row_loop(rows.shape[0], step, body)


def edge_mlp(msg, w_out, gain, out, step=512):
    def body(at):
        hidden = silu(msg[pl.ds(at, step), :]).astype(BF16)
        out[pl.ds(at, step), :] = normed(dot(hidden, w_out), gain)

    row_loop(msg.shape[0], step, body)


def coarse_edge_kernel(senders, receivers, nodes, ghosts, edges, w_in, w_out, gain, out, table_s, table_r, msg, *accs):
    rows, count = nodes.shape[0], edges.shape[0]
    w = w_in[1]
    premultiply(nodes, w[0:LANES, :], table_s)
    premultiply(nodes, w[LANES : 2 * LANES, :], table_r)
    premultiply(ghosts, w[0:LANES, :], table_s, rows)
    premultiply(edges, w[2 * LANES :, :], msg)
    clear_all(accs)

    def gather(at):
        for j in range(32):
            msg[pl.ds(at + j, 1), :] = msg[pl.ds(at + j, 1), :] + (
                table_s[pl.ds(senders[at + j], 1), :] + table_r[pl.ds(receivers[at + j], 1), :]
            )

    row_loop(count, 32, gather)
    edge_mlp(msg, w_out[1], gain[1:2, :], msg)
    add_rows(lambda j: receivers[j], msg, count, accs)
    sum_accs(accs, out)


def coarse_edge_stage(senders, receivers, nodes, ghosts, edges, w_in, w_out, gain):
    rows, far, count = nodes.shape[0], ghosts.shape[0], edges.shape[0]
    return pl.pallas_call(
        coarse_edge_kernel,
        out_shape=jax.ShapeDtypeStruct((rows, LANES), BF16),
        in_specs=[SMEM] * 2 + [VMEM] * 6,
        out_specs=VMEM,
        scratch_shapes=[
            pltpu.VMEM((rows + far, LANES), F32),
            pltpu.VMEM((rows, LANES), F32),
            pltpu.VMEM((count, LANES), F32),
        ]
        + [pltpu.VMEM((rows, LANES), F32)] * 2,
        name="coarse_edge_stage",
    )(senders, receivers, nodes, ghosts, edges, w_in, w_out, gain)


def sum_kernel(receivers, place, msg, out, *accs):
    clear_all(accs)
    add_rows(lambda j: place[receivers[j]], msg, msg.shape[0], accs)
    sum_accs(accs, out)


def sum_stage(receivers, place, msg, slots):
    return pl.pallas_call(
        sum_kernel,
        out_shape=jax.ShapeDtypeStruct((slots, LANES), BF16),
        in_specs=[SMEM, SMEM, VMEM],
        out_specs=VMEM,
        scratch_shapes=[pltpu.VMEM((slots, LANES), F32)] * 2,
        name="sum_stage",
    )(receivers, place, msg)


def pool_kernel(dest, arrived, out, wide, *accs):
    clear_all(accs)
    widen(arrived, wide)
    add_rows(lambda j: dest[j], wide, arrived.shape[0], accs)
    sum_accs(accs, out)


def pool_stage(dest, arrived, rows):
    return pl.pallas_call(
        pool_kernel,
        out_shape=jax.ShapeDtypeStruct((rows, LANES), BF16),
        in_specs=[SMEM, VMEM],
        out_specs=VMEM,
        scratch_shapes=[pltpu.VMEM(arrived.shape, F32)] + [pltpu.VMEM((rows + 8, LANES), F32)] * 2,
        name="pool_stage",
    )(dest, arrived)


def final_kernel(index, table, out, wide, rows):
    widen(table, wide)
    gather_rows(index, wide, rows, out.shape[0], 64)

    def pack(at):
        out[pl.ds(at, 512), :] = rows[pl.ds(at, 512), :].astype(BF16)

    row_loop(out.shape[0], 512, pack)


def final_stage(index, table):
    count = index.shape[0]
    return pl.pallas_call(
        final_kernel,
        out_shape=jax.ShapeDtypeStruct((count, LANES), BF16),
        in_specs=[SMEM, VMEM],
        out_specs=VMEM,
        scratch_shapes=[pltpu.VMEM(table.shape, F32), pltpu.VMEM((count, LANES), F32)],
        name="final_stage",
    )(index, table)


class Net:
    def __init__(self, doms, groups):
        self.doms, self.groups, self.per = doms, groups, doms // groups
        self.me = lax.axis_index("dom")
        self.e = lax.axis_index("edge")
        self.group = self.me // self.per
        self.local = lax.rem(self.me, self.per)
        self.right = lax.rem(self.e + 1, 4)
        self.left = lax.rem(self.e + 3, 4)
        self.opp = lax.rem(self.e + 2, 4)

    def greet(self):
        sem = pltpu.get_barrier_semaphore()
        pl.semaphore_signal(sem, 1, device_id={"edge": self.right})
        pl.semaphore_signal(sem, 1, device_id={"edge": self.left})

        def signal(k, carry):
            pl.semaphore_signal(sem, 1, device_id={"dom": lax.rem(self.me + k, self.doms)})
            return carry

        lax.fori_loop(1, self.doms, signal, 0)

    def meet(self):
        pl.semaphore_wait(pltpu.get_barrier_semaphore(), self.doms + 1)

    def offset(self, t):
        odd = lax.rem(t, 2)
        return odd * ((t + 1) // 2) + (1 - odd) * lax.rem(self.groups - t // 2, self.groups)

    def ahead(self, t):
        return lax.rem(self.group + self.offset(t), self.groups) * self.per

    def behind(self, t):
        return lax.rem(self.group + self.groups - self.offset(t), self.groups) * self.per


class Exchange:
    def __init__(self, net, first, source, target, landed, sems):
        self.net, self.first, self.source, self.target, self.landed = net, first, source, target, landed
        self.send_sem, self.recv_sem, self.own_sem = sems

    def copy(self, t, i):
        net = self.net
        local = lax.rem(net.local + i, net.per)
        peer = self.first(t) + local
        return pltpu.make_async_remote_copy(
            src_ref=self.source(t, peer),
            dst_ref=self.target(t),
            send_sem=self.send_sem.at[t * net.per + local],
            recv_sem=self.recv_sem.at[t * net.per + net.local],
            device_id={"dom": peer},
        )

    def own(self):
        return pltpu.make_async_copy(self.source(0, self.net.me), self.target(0), self.own_sem)

    def each(self, t, body):
        def run(i, carry):
            body(i)
            return carry

        lax.fori_loop(jnp.where(t == 0, 1, 0), self.net.per, run, 0)

    def send(self, t):
        self.each(t, lambda i: self.copy(t, i).start())

    def receive(self, t):
        net = self.net

        def wait(i):
            local = lax.rem(net.local + i, net.per)
            pltpu.make_async_remote_copy(
                src_ref=self.landed(t, local),
                dst_ref=self.landed(t, local),
                send_sem=self.send_sem.at[t * net.per + local],
                recv_sem=self.recv_sem.at[t * net.per + local],
                device_id={"dom": self.first(t) + local},
            ).wait_recv()

        self.each(t, wait)

    def loop(self, body):
        def run(t, carry):
            body(t)
            return carry

        lax.fori_loop(0, self.net.groups, run, 0)

    def finish(self):
        self.own().wait()
        self.loop(lambda t: self.each(t, lambda i: self.copy(t, i).wait_send()))


def exchange_sems(doms):
    return [pltpu.SemaphoreType.DMA((doms,)), pltpu.SemaphoreType.DMA((doms,)), pltpu.SemaphoreType.DMA]


def edge_copy(src, dst, sems, which, slot, to):
    return pltpu.make_async_remote_copy(
        src_ref=src,
        dst_ref=dst,
        send_sem=sems[0].at[which, slot],
        recv_sem=sems[1].at[which, slot],
        device_id={"edge": to},
    )


class Relay:
    def __init__(self, net, out, sems, pieces):
        self.net, self.out, self.sems, self.pieces = net, out, sems, pieces
        self.size = out.shape[1] // pieces

    def copy(self, which, owner, s, half, to):
        if half is None:
            at = pl.ds(s * self.size, self.size)
        else:
            at = pl.ds(s * self.size + half * (self.size // 2), self.size // 2)
        piece = self.out.at[owner, at]
        return edge_copy(piece, piece, self.sems, which, s, to)

    def first(self, s):
        n = self.net
        self.copy(0, n.e, s, None, n.right).start()
        self.copy(1, n.e, s, None, n.left).start()

    def second(self, s):
        n = self.net
        self.copy(0, n.left, s, None, n.right).wait_recv()
        self.copy(2, n.left, s, 0, n.right).start()
        self.copy(1, n.right, s, None, n.left).wait_recv()
        self.copy(3, n.right, s, 1, n.left).start()

    def finish(self, s):
        n = self.net
        self.copy(2, n.opp, s, 0, n.right).wait_recv()
        self.copy(3, n.opp, s, 1, n.left).wait_recv()
        self.copy(0, n.e, s, None, n.right).wait_send()
        self.copy(1, n.e, s, None, n.left).wait_send()
        self.copy(2, n.left, s, 0, n.right).wait_send()
        self.copy(3, n.right, s, 1, n.left).wait_send()

    def run(self, ready=lambda s: None, work=lambda s: None):
        for s in range(self.pieces):
            ready(s)
            self.first(s)
            if s:
                self.second(s - 1)
            work(s)
        self.second(self.pieces - 1)
        for s in range(self.pieces):
            self.finish(s)


def relay_sems(pieces):
    return [pltpu.SemaphoreType.DMA((4, pieces)), pltpu.SemaphoreType.DMA((4, pieces))]


class Reduce:
    def __init__(self, net, part, hop, passed, near, sems, chunks):
        self.net, self.part, self.hop, self.passed, self.near = net, part, hop, passed, near
        self.sems, self.chunks = sems, chunks
        self.half = part.shape[1] // 2
        self.size = self.half // chunks

    def a(self, c):
        return pl.ds(pl.multiple_of(c * self.size, self.size), self.size)

    def b(self, c):
        return pl.ds(pl.multiple_of(self.half + c * self.size, self.size), self.size)

    def hop_right(self, c):
        return edge_copy(self.part.at[self.net.opp, self.a(c)], self.hop.at[0, self.a(c)], self.sems, 0, c, self.net.right)

    def hop_left(self, c):
        return edge_copy(self.part.at[self.net.opp, self.b(c)], self.hop.at[1, self.a(c)], self.sems, 1, c, self.net.left)

    def raw_right(self, c):
        return edge_copy(self.part.at[self.net.right, self.b(c)], self.near.at[0, self.b(c)], self.sems, 2, c, self.net.right)

    def raw_left(self, c):
        return edge_copy(self.part.at[self.net.left, self.a(c)], self.near.at[1, self.a(c)], self.sems, 3, c, self.net.left)

    def sum_right(self, c):
        return edge_copy(self.passed.at[0, self.a(c)], self.near.at[0, self.a(c)], self.sems, 4, c, self.net.right)

    def sum_left(self, c):
        return edge_copy(self.passed.at[1, self.a(c)], self.near.at[1, self.b(c)], self.sems, 5, c, self.net.left)

    def loop(self, body):
        def run(c, carry):
            body(c)
            return carry

        lax.fori_loop(0, self.chunks, run, 0)

    def start(self, c):
        self.hop_right(c).start()
        self.hop_left(c).start()
        self.raw_right(c).start()
        self.raw_left(c).start()

    def through(self, c):
        net = self.net
        self.hop_right(c).wait_recv()
        self.passed[0, self.a(c)] = (
            self.hop[0, self.a(c)].astype(F32) + self.part[net.right, self.a(c)].astype(F32)
        ).astype(BF16)
        self.hop_left(c).wait_recv()
        self.passed[1, self.a(c)] = (
            self.hop[1, self.a(c)].astype(F32) + self.part[net.left, self.b(c)].astype(F32)
        ).astype(BF16)
        self.hop_right(c).wait_send()
        self.hop_left(c).wait_send()
        self.sum_right(c).start()
        self.sum_left(c).start()

    def finish(self, c):
        for copy in (self.raw_right(c), self.raw_left(c), self.sum_right(c), self.sum_left(c)):
            copy.wait()

    def run(self, use=lambda c: None):
        self.start(0)
        for c in range(self.chunks):
            if c + 1 < self.chunks:
                self.start(c + 1)
            self.through(c)
            if c:
                self.finish(c - 1)
                use(c - 1)
        self.finish(self.chunks - 1)
        use(self.chunks - 1)

    def value(self, rows):
        return (
            self.part[self.net.e, rows].astype(F32)
            + self.near[0, rows].astype(F32)
            + self.near[1, rows].astype(F32)
        )


def reduce_scratch(rows, chunks):
    return [
        pltpu.VMEM((2, rows // 2, LANES), BF16),
        pltpu.VMEM((2, rows // 2, LANES), BF16),
        pltpu.VMEM((2, rows, LANES), BF16),
        pltpu.SemaphoreType.DMA((6, chunks)),
        pltpu.SemaphoreType.DMA((6, chunks)),
    ]


def gather_blocks(index, base, table, rows, dst, blocks):
    size = dst.shape[1]

    def body(i, carry):
        k = blocks[0] + i
        start, at = base(k), pl.multiple_of(k * size, size)
        for j in range(size):
            rows[pl.ds(at + j, 1), :] = table[pl.ds(index[start + j], 1), :]
        dst[k] = rows[pl.ds(at, size), :].astype(BF16)
        return carry

    lax.fori_loop(0, blocks[1], body, 0)


def message_kernel(
    groups, pieces, halo, pool_send, senders, receivers, nodes, edges, w_in, w_out, gain,
    out, own_nodes, ghosts, wide, rows, send, table_s, table_r, msg, s0, s1, s2, r0, r1,
):
    doms, size, own_size = ghosts.shape[1], ghosts.shape[2], own_nodes.shape[1]
    count, near = edges.shape[0], nodes.shape[0]
    net = Net(doms, groups)
    net.greet()
    widen(nodes, wide)
    gather_blocks(halo, lambda k: k * (4 * size) + net.e * size, wide, rows, send, (0, doms))
    net.meet()
    land = ghosts.at[net.e]
    exchange = Exchange(
        net, net.ahead,
        lambda t, peer: send.at[peer],
        lambda t: land.at[t * net.per + net.local],
        lambda t, l: land.at[t * net.per + l],
        (s0, s1, s2),
    )
    exchange.own().start()
    exchange.loop(exchange.send)
    w = w_in[0]
    premultiply(nodes, w[LANES : 2 * LANES, :], table_r)
    premultiply(edges, w[2 * LANES :, :], msg)

    def gather_near(at):
        for j in range(32):
            msg[pl.ds(at + j, 1), :] = msg[pl.ds(at + j, 1), :] + table_r[pl.ds(receivers[at + j], 1), :]

    row_loop(count, 32, gather_near)
    each = groups // pieces

    def ready(s):
        def run(t, carry):
            exchange.receive(t)
            return carry

        lax.fori_loop(s * each, (s + 1) * each, run, 0)
        if s == 0:
            exchange.own().wait()

    def base(k):
        p = net.behind(k // net.per) + lax.rem(k, net.per)
        return p * (4 * own_size) + net.e * own_size

    def work(s):
        gather_blocks(pool_send, base, wide, rows, own_nodes, (s * (doms // pieces), doms // pieces))
        if s == pieces - 1:
            premultiply(nodes, w[0:LANES, :], table_s)

    Relay(net, ghosts, (r0, r1), pieces).run(ready, work)
    for owner in range(4):
        block = ghosts[owner].reshape(doms * size, LANES)
        table_s[pl.ds(near + owner * doms * size, doms * size), :] = dot(block, w[0:LANES, :])

    def gather_far(at):
        for j in range(32):
            msg[pl.ds(at + j, 1), :] = msg[pl.ds(at + j, 1), :] + table_s[pl.ds(senders[at + j], 1), :]

    row_loop(count, 32, gather_far)
    edge_mlp(msg, w_out[0], gain[0:1, :], out)
    exchange.loop(lambda t: exchange.each(t, lambda i: exchange.copy(t, i).wait_send()))


def comm_params(collective_id):
    return pltpu.CompilerParams(collective_id=collective_id, has_side_effects=True)


def message_stage(doms, groups, halo, pool_send, senders, receivers, nodes, edges, w_in, w_out, gain, pieces=2):
    size, own_size = halo.shape[0] // doms // 4, pool_send.shape[0] // doms // 4
    near, count = nodes.shape[0], edges.shape[0]
    return pl.pallas_call(
        functools.partial(message_kernel, groups, pieces),
        out_shape=(
            jax.ShapeDtypeStruct((count, LANES), F32),
            jax.ShapeDtypeStruct((doms, own_size, LANES), BF16),
        ),
        in_specs=[SMEM] * 4 + [VMEM] * 5,
        out_specs=(VMEM, VMEM),
        scratch_shapes=[
            pltpu.VMEM((4, doms, size, LANES), BF16),
            pltpu.VMEM(nodes.shape, F32),
            pltpu.VMEM((doms * own_size, LANES), F32),
            pltpu.VMEM((doms, size, LANES), BF16),
            pltpu.VMEM((near + 4 * doms * size, LANES), F32),
            pltpu.VMEM((near, LANES), F32),
            pltpu.VMEM((count, LANES), F32),
        ]
        + exchange_sems(doms)
        + relay_sems(pieces),
        compiler_params=comm_params(0),
        name="message_stage",
    )(halo, pool_send, senders, receivers, nodes, edges, w_in, w_out, gain)


def fine_kernel(groups, part, nodes, w_in, w_out, gain, mid, arrived, hop, passed, near, c0, c1, s0, s1, s2):
    doms, size = mid.shape[0], mid.shape[1]
    net = Net(doms, groups)
    net.greet()
    net.meet()
    reduce = Reduce(net, part, hop, passed, near, (c0, c1), groups // 2)
    exchange = Exchange(
        net, net.behind,
        lambda t, peer: mid.at[t * net.per + lax.rem(peer, net.per)],
        lambda t: arrived.at[net.me],
        lambda t, l: arrived.at[net.ahead(t) + l],
        (s0, s1, s2),
    )
    span = net.per * size

    def use(c):
        units = (c, groups // 2 + c)
        for u in units:
            own = nodes[u * net.per : (u + 1) * net.per].reshape(span, LANES)
            result = node_mlp(own, reduce.value(pl.ds(u * span, span)), w_in[0], w_out[0], gain[0:1, :])
            mid[u * net.per : (u + 1) * net.per] = result.reshape(net.per, size, LANES)
        if c == 0:
            exchange.own().start()
        for u in units:
            exchange.send(u)

    reduce.run(use)
    exchange.loop(exchange.receive)
    exchange.finish()


def fine_stage(groups, part, nodes, w_in, w_out, gain):
    return pl.pallas_call(
        functools.partial(fine_kernel, groups),
        out_shape=(jax.ShapeDtypeStruct(nodes.shape, BF16), jax.ShapeDtypeStruct(nodes.shape, BF16)),
        in_specs=[VMEM] * 5,
        out_specs=(VMEM, VMEM),
        scratch_shapes=reduce_scratch(part.shape[1], groups // 2) + exchange_sems(nodes.shape[0]),
        compiler_params=comm_params(1),
        name="fine_stage",
    )(part, nodes, w_in, w_out, gain)


def coarse_border_kernel(
    groups, chunks, halo, part, count, full, out, wide, rows, send, hop, passed, near, c0, c1, g0, g1, s0, s1, s2, r0, r1
):
    doms, size = out.shape[1], out.shape[2]
    net = Net(doms, groups)
    net.greet()
    net.meet()
    reduce = Reduce(net, part, hop, passed, near, (c0, c1), chunks)
    reduce.run()
    quarter = part.shape[1]
    full[net.e] = (reduce.value(pl.ds(0, quarter)) / count[...]).astype(BF16)
    Relay(net, full, (g0, g1), 1).run()
    for q in range(4):
        wide[pl.ds(q * quarter, quarter), :] = full[q].astype(F32)
    gather_blocks(halo, lambda k: k * (4 * size) + net.e * size, wide, rows, send, (0, doms))
    land = out.at[net.e]
    exchange = Exchange(
        net, net.ahead,
        lambda t, peer: send.at[peer],
        lambda t: land.at[t * net.per + net.local],
        lambda t, l: land.at[t * net.per + l],
        (s0, s1, s2),
    )
    exchange.own().start()
    exchange.loop(exchange.send)
    exchange.loop(exchange.receive)
    exchange.finish()
    Relay(net, out, (r0, r1), 1).run()


def coarse_border_stage(doms, groups, halo, part, count, chunks=2):
    quarter, size = part.shape[1], halo.shape[0] // doms // 4
    return pl.pallas_call(
        functools.partial(coarse_border_kernel, groups, chunks),
        out_shape=(
            jax.ShapeDtypeStruct(part.shape, BF16),
            jax.ShapeDtypeStruct((4, doms, size, LANES), BF16),
        ),
        in_specs=[SMEM, VMEM, VMEM],
        out_specs=(VMEM, VMEM),
        scratch_shapes=[
            pltpu.VMEM((4 * quarter, LANES), F32),
            pltpu.VMEM((doms * size, LANES), F32),
            pltpu.VMEM((doms, size, LANES), BF16),
        ]
        + reduce_scratch(quarter, chunks)
        + relay_sems(1)
        + exchange_sems(doms)
        + relay_sems(1),
        compiler_params=comm_params(2),
        name="coarse_border_stage",
    )(halo, part, count)


def unpool_kernel(
    groups, chunks, pieces, index, part, nodes, mid, w_in, w_out, gain,
    full, out, wide, rows, send, land, hop, passed, near, c0, c1, g0, g1, s0, s1, s2, r0, r1,
):
    doms, size = mid.shape[0], mid.shape[1]
    net = Net(doms, groups)
    net.greet()
    net.meet()
    reduce = Reduce(net, part, hop, passed, near, (c0, c1), chunks)
    reduce.run()
    quarter = part.shape[1]
    full[net.e] = node_mlp(
        nodes[net.e], reduce.value(pl.ds(0, quarter)), w_in[1], w_out[1], gain[1:2, :]
    )
    wide[pl.ds(4 * quarter, 8), :] = jnp.zeros((8, LANES), F32)
    Relay(net, full, (g0, g1), 1).run()
    for q in range(4):
        wide[pl.ds(q * quarter, quarter), :] = full[q].astype(F32)
    exchange = Exchange(
        net, net.ahead,
        lambda t, peer: send.at[peer],
        lambda t: land.at[t * net.per + net.local],
        lambda t, l: land.at[t * net.per + l],
        (s0, s1, s2),
    )

    def start(t):
        gather_blocks(index, lambda k: k * size, wide, rows, send, (net.ahead(t), net.per))
        exchange.send(t)

    exchange.loop(start)
    exchange.own().start()
    each = groups // pieces

    def ready(s):
        def run(t, carry):
            exchange.receive(t)
            return carry

        lax.fori_loop(s * each, (s + 1) * each, run, 0)
        if s == 0:
            exchange.own().wait()
        span = each * net.per
        block = slice(s * span, (s + 1) * span)
        out[net.e, block] = (land[block].astype(F32) + mid[block].astype(F32)).astype(BF16)

    Relay(net, out, (r0, r1), pieces).run(ready)
    exchange.loop(lambda t: exchange.each(t, lambda i: exchange.copy(t, i).wait_send()))


def unpool_stage(groups, index, part, nodes, mid, w_in, w_out, gain, chunks=2, pieces=4):
    quarter, (doms, size, _) = part.shape[1], mid.shape
    pieces = min(pieces, groups)
    return pl.pallas_call(
        functools.partial(unpool_kernel, groups, chunks, pieces),
        out_shape=(
            jax.ShapeDtypeStruct(part.shape, BF16),
            jax.ShapeDtypeStruct((4,) + mid.shape, BF16),
        ),
        in_specs=[SMEM] + [VMEM] * 6,
        out_specs=(VMEM, VMEM),
        scratch_shapes=[
            pltpu.VMEM((4 * quarter + 8, LANES), F32),
            pltpu.VMEM((doms * size, LANES), F32),
            pltpu.VMEM(mid.shape, BF16),
            pltpu.VMEM(mid.shape, BF16),
        ]
        + reduce_scratch(quarter, chunks)
        + relay_sems(1)
        + exchange_sems(doms)
        + relay_sems(pieces),
        compiler_params=comm_params(3),
        name="unpool_stage",
    )(index, part, nodes, mid, w_in, w_out, gain)


def child_counts(dest, rows):
    high, low = dest // LANES, lax.rem(dest, LANES)
    left = (lax.broadcasted_iota(jnp.int32, (rows // LANES, dest.shape[0]), 0) == high[None, :]).astype(BF16)
    right = (lax.broadcasted_iota(jnp.int32, (LANES, dest.shape[0]), 0) == low[None, :]).astype(BF16)
    return lax.dot_general(left, right, (((1,), (1,)), ((), ())), preferred_element_type=F32)


def shards(groups, coarse_rows, *args):
    (
        fine_nodes, fine_edges, fine_senders, fine_receivers, fine_halo,
        coarse_edges, coarse_senders, coarse_receivers, coarse_halo,
        pool_send, pool_dest, unpool_slot,
        edge_in_weight, edge_out_weight, node_in_weight, node_out_weight, edge_gain, node_gain,
    ) = args
    e, me = lax.axis_index("edge"), lax.axis_index("dom")
    doms = fine_halo.shape[1]
    per = doms // groups

    def nearby(p):
        away = lax.rem(me // per + groups - p // per, groups)
        step = jnp.where(2 * away <= groups, jnp.maximum(2 * away - 1, 0), 2 * (groups - away))
        return step * per + lax.rem(p, per)

    def moved(senders, rows, width):
        far = senders - rows
        size = width // 4
        owner, slot = far // width, lax.rem(far, width)
        there = rows + (slot // size) * (doms * size) + nearby(owner) * size + lax.rem(slot, size)
        return jnp.where(senders < rows, senders, there)

    slots = pool_dest.shape[2]
    own_size = slots // 4
    slot = lax.rem(unpool_slot, slots)
    place = (slot // own_size) * (doms * own_size) + nearby(unpool_slot // slots) * own_size + lax.rem(slot, own_size)
    dest = lax.dynamic_slice_in_dim(pool_dest[0], e * own_size, own_size, axis=1).reshape(-1)
    senders = moved(fine_senders, fine_nodes.shape[0], fine_halo.shape[2])
    far_senders = moved(coarse_senders, coarse_rows, coarse_halo.shape[2])
    counts = child_counts(pool_dest[0].reshape(-1), coarse_rows).reshape(4, -1)
    counts = jnp.maximum(lax.dynamic_index_in_dim(counts, e, keepdims=False), 1.0)
    counts = jnp.broadcast_to(counts[:, None], (coarse_rows // 4, LANES))

    msg, own_nodes = message_stage(
        doms, groups, fine_halo.reshape(-1), pool_send.reshape(-1), senders, fine_receivers,
        fine_nodes, fine_edges, edge_in_weight, edge_out_weight, edge_gain,
    )
    part = sum_stage(fine_receivers, place, msg, doms * slots)
    mid, arrived = fine_stage(
        groups, part.reshape(4, -1, LANES), own_nodes, node_in_weight, node_out_weight, node_gain
    )
    pooled = pool_stage(dest, arrived.reshape(-1, LANES), coarse_rows)
    coarse_in, coarse_ghosts = coarse_border_stage(
        doms, groups, coarse_halo.reshape(-1), pooled.reshape(4, -1, LANES), counts
    )
    part = coarse_edge_stage(
        far_senders, coarse_receivers, coarse_in.reshape(-1, LANES), coarse_ghosts.reshape(-1, LANES),
        coarse_edges, edge_in_weight, edge_out_weight, edge_gain,
    )
    coarse_out, table = unpool_stage(
        groups, dest, part.reshape(4, -1, LANES), coarse_in, mid, node_in_weight, node_out_weight, node_gain
    )
    fine_out = final_stage(place, table.reshape(-1, LANES))
    return fine_out, coarse_out.reshape(-1, LANES)


def solution(mesh, groups=8, coarse_rows=2048):
    placed = (
        P("dom", None),
        P(("dom", "edge"), None),
        P(("dom", "edge")),
        P(("dom", "edge")),
        P("dom", None, None),
        P(("dom", "edge"), None),
        P(("dom", "edge")),
        P(("dom", "edge")),
        P("dom", None, None),
        P("dom", None, None),
        P("dom", None, None),
        P("dom"),
        P(),
        P(),
        P(),
        P(),
        P(),
        P(),
    )
    return jax.shard_map(
        functools.partial(shards, groups, coarse_rows),
        mesh=mesh,
        in_specs=placed,
        out_specs=(P("dom", None), P("dom", None)),
        check_vma=False,
    )
```

```python
import functools

import jax
import jax.numpy as jnp
from jax import lax
from jax.experimental import pallas as pl
from jax.experimental.pallas import tpu as pltpu
from jax.sharding import PartitionSpec as P

F32, BF16 = jnp.float32, jnp.bfloat16
VMEM = pl.BlockSpec(memory_space=pltpu.VMEM)
SMEM = pl.BlockSpec(memory_space=pltpu.SMEM)
LANES = 128


def silu(v):
    return v / (1.0 + jnp.exp(-v))


def normed(v, gain):
    center = v - jnp.mean(v, axis=-1, keepdims=True)
    spread = jnp.mean(center * center, axis=-1, keepdims=True)
    return center * lax.rsqrt(spread + 1e-05) * gain


def dot(a, b):
    return jnp.dot(a, b, preferred_element_type=F32)


def node_mlp(rows, summed, w_in, w_out, gain):
    pre = dot(rows, w_in[0:LANES, :]) + dot(summed.astype(BF16), w_in[LANES : 2 * LANES, :])
    hidden = silu(pre).astype(BF16)
    return (rows.astype(F32) + normed(dot(hidden, w_out), gain)).astype(BF16)


def row_loop(total, step, body):
    def run(i, carry):
        body(pl.multiple_of(i * step, step))
        return carry

    lax.fori_loop(0, total // step, run, 0)


def widen(src, dst, step=512):
    def body(at):
        dst[pl.ds(at, step), :] = src[pl.ds(at, step), :].astype(F32)

    row_loop(src.shape[0], step, body)


def gather_rows(index, table, dst, count, unroll=16):
    def body(at):
        for j in range(unroll):
            dst[pl.ds(at + j, 1), :] = table[pl.ds(index[at + j], 1), :]

    row_loop(count, unroll, body)


def clear_all(accs, step=512):
    def body(at):
        for acc in accs:
            acc[pl.ds(at, step), :] = jnp.zeros((step, LANES), F32)

    row_loop(accs[0].shape[0] // step * step, step, body)


def add_rows(where, values, count, accs, unroll=32):
    def body(at):
        for j in range(unroll):
            acc, row = accs[j % len(accs)], where(at + j)
            acc[pl.ds(row, 1), :] = acc[pl.ds(row, 1), :] + values[pl.ds(at + j, 1), :]

    row_loop(count, unroll, body)


def sum_accs(accs, out, step=512):
    def body(at):
        value = accs[0][pl.ds(at, step), :]
        for acc in accs[1:]:
            value = value + acc[pl.ds(at, step), :]
        out[pl.ds(at, step), :] = value.astype(BF16)

    row_loop(out.shape[0], step, body)


def premultiply(rows, weight, dst, base=0, step=512):
    def body(at):
        dst[pl.ds(pl.multiple_of(base + at, step), step), :] = dot(rows[pl.ds(at, step), :], weight)

    row_loop(rows.shape[0], step, body)


def edge_mlp(msg, w_out, gain, out, step=512):
    def body(at):
        hidden = silu(msg[pl.ds(at, step), :]).astype(BF16)
        out[pl.ds(at, step), :] = normed(dot(hidden, w_out), gain)

    row_loop(msg.shape[0], step, body)


def sum_kernel(receivers, place, msg, out, *accs):
    clear_all(accs)
    add_rows(lambda j: place[receivers[j]], msg, msg.shape[0], accs)
    sum_accs(accs, out)


def sum_stage(receivers, place, msg, slots):
    return pl.pallas_call(
        sum_kernel,
        out_shape=jax.ShapeDtypeStruct((slots, LANES), BF16),
        in_specs=[SMEM, SMEM, VMEM],
        out_specs=VMEM,
        scratch_shapes=[pltpu.VMEM((slots, LANES), F32)] * 3,
        name="sum_stage",
    )(receivers, place, msg)


def final_kernel(index, table, out, wide, rows):
    widen(table, wide)
    gather_rows(index, wide, rows, out.shape[0], 64)

    def pack(at):
        out[pl.ds(at, 512), :] = rows[pl.ds(at, 512), :].astype(BF16)

    row_loop(out.shape[0], 512, pack)


def final_stage(index, table):
    count = index.shape[0]
    return pl.pallas_call(
        final_kernel,
        out_shape=jax.ShapeDtypeStruct((count, LANES), BF16),
        in_specs=[SMEM, VMEM],
        out_specs=VMEM,
        scratch_shapes=[pltpu.VMEM(table.shape, F32), pltpu.VMEM((count, LANES), F32)],
        name="final_stage",
    )(index, table)


class Net:
    def __init__(self, doms, groups):
        self.doms, self.groups, self.per = doms, groups, doms // groups
        self.me = lax.axis_index("dom")
        self.e = lax.axis_index("edge")
        self.group = self.me // self.per
        self.local = lax.rem(self.me, self.per)
        self.right = lax.rem(self.e + 1, 4)
        self.left = lax.rem(self.e + 3, 4)
        self.opp = lax.rem(self.e + 2, 4)

    def greet(self):
        sem = pltpu.get_barrier_semaphore()
        pl.semaphore_signal(sem, 1, device_id={"edge": self.right})
        pl.semaphore_signal(sem, 1, device_id={"edge": self.left})

        def signal(k, carry):
            pl.semaphore_signal(sem, 1, device_id={"dom": lax.rem(self.me + k, self.doms)})
            return carry

        lax.fori_loop(1, self.doms, signal, 0)

    def meet(self):
        pl.semaphore_wait(pltpu.get_barrier_semaphore(), self.doms + 1)

    def offset(self, t):
        odd = lax.rem(t, 2)
        return odd * ((t + 1) // 2) + (1 - odd) * lax.rem(self.groups - t // 2, self.groups)

    def ahead(self, t):
        return lax.rem(self.group + self.offset(t), self.groups) * self.per

    def behind(self, t):
        return lax.rem(self.group + self.groups - self.offset(t), self.groups) * self.per


class Exchange:
    def __init__(self, net, first, source, target, landed, sems):
        self.net, self.first, self.source, self.target, self.landed = net, first, source, target, landed
        self.send_sem, self.recv_sem, self.own_sem = sems

    def copy(self, t, i):
        net = self.net
        local = lax.rem(net.local + i, net.per)
        peer = self.first(t) + local
        return pltpu.make_async_remote_copy(
            src_ref=self.source(t, peer),
            dst_ref=self.target(t),
            send_sem=self.send_sem.at[t * net.per + local],
            recv_sem=self.recv_sem.at[t * net.per + net.local],
            device_id={"dom": peer},
        )

    def own(self):
        return pltpu.make_async_copy(self.source(0, self.net.me), self.target(0), self.own_sem)

    def each(self, t, body):
        def run(i, carry):
            body(i)
            return carry

        lax.fori_loop(jnp.where(t == 0, 1, 0), self.net.per, run, 0)

    def send(self, t):
        self.each(t, lambda i: self.copy(t, i).start())

    def receive(self, t):
        net = self.net

        def wait(i):
            local = lax.rem(net.local + i, net.per)
            pltpu.make_async_remote_copy(
                src_ref=self.landed(t, local),
                dst_ref=self.landed(t, local),
                send_sem=self.send_sem.at[t * net.per + local],
                recv_sem=self.recv_sem.at[t * net.per + local],
                device_id={"dom": self.first(t) + local},
            ).wait_recv()

        self.each(t, wait)

    def loop(self, body):
        def run(t, carry):
            body(t)
            return carry

        lax.fori_loop(0, self.net.groups, run, 0)

    def finish(self):
        self.own().wait()
        self.loop(lambda t: self.each(t, lambda i: self.copy(t, i).wait_send()))


def exchange_sems(doms):
    return [pltpu.SemaphoreType.DMA((doms,)), pltpu.SemaphoreType.DMA((doms,)), pltpu.SemaphoreType.DMA]


def edge_copy(src, dst, sems, which, slot, to):
    return pltpu.make_async_remote_copy(
        src_ref=src,
        dst_ref=dst,
        send_sem=sems[0].at[which, slot],
        recv_sem=sems[1].at[which, slot],
        device_id={"edge": to},
    )


class Relay:
    def __init__(self, net, out, sems, pieces):
        self.net, self.out, self.sems, self.pieces = net, out, sems, pieces
        self.size = out.shape[1] // pieces

    def copy(self, which, owner, s, half, to):
        if half is None:
            at = pl.ds(s * self.size, self.size)
        else:
            at = pl.ds(s * self.size + half * (self.size // 2), self.size // 2)
        piece = self.out.at[owner, at]
        return edge_copy(piece, piece, self.sems, which, s, to)

    def first(self, s):
        n = self.net
        self.copy(0, n.e, s, None, n.right).start()
        self.copy(1, n.e, s, None, n.left).start()

    def second(self, s):
        n = self.net
        self.copy(0, n.left, s, None, n.right).wait_recv()
        self.copy(2, n.left, s, 0, n.right).start()
        self.copy(1, n.right, s, None, n.left).wait_recv()
        self.copy(3, n.right, s, 1, n.left).start()

    def finish(self, s):
        n = self.net
        self.copy(2, n.opp, s, 0, n.right).wait_recv()
        self.copy(3, n.opp, s, 1, n.left).wait_recv()
        self.copy(0, n.e, s, None, n.right).wait_send()
        self.copy(1, n.e, s, None, n.left).wait_send()
        self.copy(2, n.left, s, 0, n.right).wait_send()
        self.copy(3, n.right, s, 1, n.left).wait_send()

    def run(self, ready=lambda s: None, work=lambda s: None):
        for s in range(self.pieces):
            ready(s)
            self.first(s)
            if s:
                self.second(s - 1)
            work(s)
        self.second(self.pieces - 1)
        for s in range(self.pieces):
            self.finish(s)


def relay_sems(pieces):
    return [pltpu.SemaphoreType.DMA((4, pieces)), pltpu.SemaphoreType.DMA((4, pieces))]


class Reduce:
    def __init__(self, net, part, hop, passed, near, sems, chunks):
        self.net, self.part, self.hop, self.passed, self.near = net, part, hop, passed, near
        self.sems, self.chunks = sems, chunks
        self.half = part.shape[1] // 2
        self.size = self.half // chunks

    def a(self, c):
        return pl.ds(pl.multiple_of(c * self.size, self.size), self.size)

    def b(self, c):
        return pl.ds(pl.multiple_of(self.half + c * self.size, self.size), self.size)

    def hop_right(self, c):
        return edge_copy(self.part.at[self.net.opp, self.a(c)], self.hop.at[0, self.a(c)], self.sems, 0, c, self.net.right)

    def hop_left(self, c):
        return edge_copy(self.part.at[self.net.opp, self.b(c)], self.hop.at[1, self.a(c)], self.sems, 1, c, self.net.left)

    def raw_right(self, c):
        return edge_copy(self.part.at[self.net.right, self.b(c)], self.near.at[0, self.b(c)], self.sems, 2, c, self.net.right)

    def raw_left(self, c):
        return edge_copy(self.part.at[self.net.left, self.a(c)], self.near.at[1, self.a(c)], self.sems, 3, c, self.net.left)

    def sum_right(self, c):
        return edge_copy(self.passed.at[0, self.a(c)], self.near.at[0, self.a(c)], self.sems, 4, c, self.net.right)

    def sum_left(self, c):
        return edge_copy(self.passed.at[1, self.a(c)], self.near.at[1, self.b(c)], self.sems, 5, c, self.net.left)

    def loop(self, body):
        def run(c, carry):
            body(c)
            return carry

        lax.fori_loop(0, self.chunks, run, 0)

    def start(self, c):
        self.hop_right(c).start()
        self.hop_left(c).start()
        self.raw_right(c).start()
        self.raw_left(c).start()

    def through(self, c):
        net = self.net
        self.hop_right(c).wait_recv()
        self.passed[0, self.a(c)] = (
            self.hop[0, self.a(c)].astype(F32) + self.part[net.right, self.a(c)].astype(F32)
        ).astype(BF16)
        self.hop_left(c).wait_recv()
        self.passed[1, self.a(c)] = (
            self.hop[1, self.a(c)].astype(F32) + self.part[net.left, self.b(c)].astype(F32)
        ).astype(BF16)
        self.hop_right(c).wait_send()
        self.hop_left(c).wait_send()
        self.sum_right(c).start()
        self.sum_left(c).start()

    def finish(self, c):
        for copy in (self.raw_right(c), self.raw_left(c), self.sum_right(c), self.sum_left(c)):
            copy.wait()

    def run(self, use=lambda c: None, aside=lambda: None):
        order = list(reversed(range(self.chunks)))
        self.start(order[0])
        for k, c in enumerate(order):
            if k + 1 < self.chunks:
                self.start(order[k + 1])
            if k == 0:
                aside()
            self.through(c)
            if k:
                self.finish(order[k - 1])
                use(order[k - 1])
        self.finish(order[-1])
        use(order[-1])

    def value(self, rows):
        return (
            self.part[self.net.e, rows].astype(F32)
            + self.near[0, rows].astype(F32)
            + self.near[1, rows].astype(F32)
        )


def reduce_scratch(rows, chunks):
    return [
        pltpu.VMEM((2, rows // 2, LANES), BF16),
        pltpu.VMEM((2, rows // 2, LANES), BF16),
        pltpu.VMEM((2, rows, LANES), BF16),
        pltpu.SemaphoreType.DMA((6, chunks)),
        pltpu.SemaphoreType.DMA((6, chunks)),
    ]


def gather_blocks(index, base, table, rows, dst, blocks):
    size = dst.shape[1]

    def body(i, carry):
        k = blocks[0] + i
        start, at = base(k), pl.multiple_of(k * size, size)
        for j in range(size):
            rows[pl.ds(at + j, 1), :] = table[pl.ds(index[start + j], 1), :]
        dst[k] = rows[pl.ds(at, size), :].astype(BF16)
        return carry

    lax.fori_loop(0, blocks[1], body, 0)


def message_kernel(
    groups, pieces, halo, pool_send, senders, receivers, nodes, edges, w_in, w_out, gain,
    out, own_nodes, ghosts, wide, rows, send, table_s, table_r, msg, s0, s1, s2, r0, r1,
):
    doms, size, own_size = ghosts.shape[1], ghosts.shape[2], own_nodes.shape[1]
    count, near = edges.shape[0], nodes.shape[0]
    net = Net(doms, groups)
    net.greet()
    widen(nodes, wide)
    gather_blocks(halo, lambda k: k * (4 * size) + net.e * size, wide, rows, send, (0, doms))
    net.meet()
    land = ghosts.at[net.e]
    exchange = Exchange(
        net, net.ahead,
        lambda t, peer: send.at[peer],
        lambda t: land.at[t * net.per + net.local],
        lambda t, l: land.at[t * net.per + l],
        (s0, s1, s2),
    )
    exchange.own().start()
    exchange.loop(exchange.send)
    w = w_in[0]
    premultiply(nodes, w[LANES : 2 * LANES, :], table_r)
    premultiply(edges, w[2 * LANES :, :], msg)

    def gather_near(at):
        for j in range(32):
            msg[pl.ds(at + j, 1), :] = msg[pl.ds(at + j, 1), :] + table_r[pl.ds(receivers[at + j], 1), :]

    row_loop(count, 32, gather_near)
    each = groups // pieces

    def ready(s):
        def run(t, carry):
            exchange.receive(t)
            return carry

        lax.fori_loop(s * each, (s + 1) * each, run, 0)
        if s == 0:
            exchange.own().wait()

    def base(k):
        p = net.behind(k // net.per) + lax.rem(k, net.per)
        return p * (4 * own_size) + net.e * own_size

    def work(s):
        gather_blocks(pool_send, base, wide, rows, own_nodes, (s * (doms // pieces), doms // pieces))
        if s == pieces - 1:
            premultiply(nodes, w[0:LANES, :], table_s)

    Relay(net, ghosts, (r0, r1), pieces).run(ready, work)
    for owner in range(4):
        block = ghosts[owner].reshape(doms * size, LANES)
        table_s[pl.ds(near + owner * doms * size, doms * size), :] = dot(block, w[0:LANES, :])

    def gather_far(at):
        for j in range(32):
            msg[pl.ds(at + j, 1), :] = msg[pl.ds(at + j, 1), :] + table_s[pl.ds(senders[at + j], 1), :]

    row_loop(count, 32, gather_far)
    edge_mlp(msg, w_out[0], gain[0:1, :], out)
    exchange.loop(lambda t: exchange.each(t, lambda i: exchange.copy(t, i).wait_send()))


def comm_params(collective_id):
    return pltpu.CompilerParams(collective_id=collective_id, has_side_effects=True)


def message_stage(doms, groups, halo, pool_send, senders, receivers, nodes, edges, w_in, w_out, gain, pieces=2):
    size, own_size = halo.shape[0] // doms // 4, pool_send.shape[0] // doms // 4
    near, count = nodes.shape[0], edges.shape[0]
    return pl.pallas_call(
        functools.partial(message_kernel, groups, pieces),
        out_shape=(
            jax.ShapeDtypeStruct((count, LANES), F32),
            jax.ShapeDtypeStruct((doms, own_size, LANES), BF16),
        ),
        in_specs=[SMEM] * 4 + [VMEM] * 5,
        out_specs=(VMEM, VMEM),
        scratch_shapes=[
            pltpu.VMEM((4, doms, size, LANES), BF16),
            pltpu.VMEM(nodes.shape, F32),
            pltpu.VMEM((doms * own_size, LANES), F32),
            pltpu.VMEM((doms, size, LANES), BF16),
            pltpu.VMEM((near + 4 * doms * size, LANES), F32),
            pltpu.VMEM((near, LANES), F32),
            pltpu.VMEM((count, LANES), F32),
        ]
        + exchange_sems(doms)
        + relay_sems(pieces),
        compiler_params=comm_params(0),
        name="message_stage",
    )(halo, pool_send, senders, receivers, nodes, edges, w_in, w_out, gain)


def child_counts(all_dest, first, counts, step=128):
    lines = all_dest.shape[0]

    def rows(at):
        target = lax.broadcasted_iota(jnp.int32, (step, LANES), 0) + (first + at)

        def line(i, total):
            for j in range(8):
                hit = all_dest[pl.ds(i * 8 + j, 1), :] == target
                total = total + jnp.where(hit, 1.0, 0.0)
            return total

        total = lax.fori_loop(0, lines // 8, line, jnp.zeros((step, LANES), F32))
        counts[pl.ds(at, step), :] = jnp.broadcast_to(jnp.sum(total, axis=1, keepdims=True), (step, LANES))

    row_loop(counts.shape[0], step, rows)


def one_hot(index, first, rows):
    at = lax.broadcasted_iota(jnp.int32, (rows, index.shape[1]), 0) + first
    return jnp.where(at == index, 1.0, 0.0).astype(BF16)


def main_kernel(
    groups, pieces, halo, dest, senders, receivers, all_dest, group_dest, line_receivers,
    part, nodes, edges, edge_in, edge_out, node_in, node_out, edge_gain, node_gain,
    coarse_out, table,
    hop, passed, near, mid, arrived, counts, pooled, coarse_part, coarse_hop, coarse_passed, coarse_near,
    coarse_in, ghosts, wide, rows, border, table_s, table_r, msg, send, land,
    f0, f1, p0, p1, e0, e1, a0, a1, b0, b1, g0, g1, h0, h1, i0, i1, i2, j0, j1, j2, k0, k1, k2,
):
    doms, size = mid.shape[0], mid.shape[1]
    quarter, border_size = coarse_in.shape[1], ghosts.shape[2]
    coarse_rows, count = 4 * quarter, edges.shape[0]
    net = Net(doms, groups)
    net.greet()
    premultiply(edges, edge_in[1, 2 * LANES :, :], msg)
    net.meet()

    reduce = Reduce(net, part, hop, passed, near, (f0, f1), groups // 2)
    pool = Exchange(
        net, net.behind,
        lambda t, peer: mid.at[t * net.per + lax.rem(peer, net.per)],
        lambda t: arrived.at[net.me],
        lambda t, l: arrived.at[net.ahead(t) + l],
        (i0, i1, i2),
    )
    span = net.per * size

    def use(c):
        units = (groups // 2 + c, c)
        for u in units:
            own = nodes[u * net.per : (u + 1) * net.per].reshape(span, LANES)
            result = node_mlp(own, reduce.value(pl.ds(u * span, span)), node_in[0], node_out[0], node_gain[0:1, :])
            mid[u * net.per : (u + 1) * net.per] = result.reshape(net.per, size, LANES)
        if c == 0:
            pool.own().start()
        for u in units:
            pool.send(u)

    def aside():
        pooled[...] = jnp.zeros_like(pooled)
        child_counts(all_dest, net.e * quarter, counts)

    reduce.run(use, aside)

    def gathered(k, carry):
        c = groups // 2 - 1 - k // 2
        t = c + (1 - lax.rem(k, 2)) * (groups // 2)
        pool.receive(t)

        @pl.when(t == 0)
        def _():
            pool.own().wait()

        first = net.ahead(t)
        block = arrived[pl.ds(first, net.per)].reshape(span, LANES)
        index = group_dest[pl.ds(first // net.per, 1), :]
        for q in range(4):
            at = pl.ds(q * quarter, quarter)
            pooled[at, :] = pooled[at, :] + dot(one_hot(index, q * quarter, quarter), block)
        return carry

    lax.fori_loop(0, groups, gathered, 0)
    for owner in (net.opp, net.right, net.left, net.e):
        at = pl.ds(pl.multiple_of(owner * quarter, quarter), quarter)
        coarse_part[owner] = pooled[at, :].astype(BF16)
    pool.loop(lambda t: pool.each(t, lambda i: pool.copy(t, i).wait_send()))

    reduce = Reduce(net, coarse_part, coarse_hop, coarse_passed, coarse_near, (p0, p1), p0.shape[1])
    reduce.run()
    mean = reduce.value(pl.ds(0, quarter)) / jnp.maximum(counts[...], 1.0)
    coarse_in[net.e] = mean.astype(BF16)
    Relay(net, coarse_in, (g0, g1), 1).run()
    for q in range(4):
        wide[pl.ds(q * quarter, quarter), :] = coarse_in[q].astype(F32)
    gather_blocks(halo, lambda k: k * (4 * border_size) + net.e * border_size, wide, rows, border, (0, doms))
    here = ghosts.at[net.e]
    exchange = Exchange(
        net, net.ahead,
        lambda t, peer: border.at[peer],
        lambda t: here.at[t * net.per + net.local],
        lambda t, l: here.at[t * net.per + l],
        (j0, j1, j2),
    )
    exchange.own().start()
    exchange.loop(exchange.send)
    w = edge_in[1]
    for q in range(4):
        table_r[pl.ds(q * quarter, quarter), :] = dot(coarse_in[q], w[LANES : 2 * LANES, :])
        table_s[pl.ds(q * quarter, quarter), :] = dot(coarse_in[q], w[0:LANES, :])

    def gather_near(at):
        for j in range(32):
            msg[pl.ds(at + j, 1), :] = msg[pl.ds(at + j, 1), :] + table_r[pl.ds(receivers[at + j], 1), :]

    row_loop(count, 32, gather_near)
    exchange.loop(exchange.receive)
    exchange.finish()
    Relay(net, ghosts, (h0, h1), 1).run()
    for owner in range(4):
        block = ghosts[owner].reshape(doms * border_size, LANES)
        at = pl.ds(coarse_rows + owner * doms * border_size, doms * border_size)
        table_s[at, :] = dot(block, w[0:LANES, :])

    def gather_far(at):
        for j in range(32):
            msg[pl.ds(at + j, 1), :] = msg[pl.ds(at + j, 1), :] + table_s[pl.ds(senders[at + j], 1), :]

    row_loop(count, 32, gather_far)
    edge_mlp(msg, edge_out[1], edge_gain[1:2, :], msg)
    high = msg[...].astype(BF16)
    low = (msg[...] - high.astype(F32)).astype(BF16)
    both = jnp.concatenate([high, low], axis=1)
    for owner in (net.opp, net.right, net.left, net.e):
        sums = dot(one_hot(line_receivers[...], owner * quarter, quarter), both)
        coarse_part[owner] = (sums[:, 0:LANES] + sums[:, LANES:]).astype(BF16)

    reduce = Reduce(net, coarse_part, coarse_hop, coarse_passed, coarse_near, (e0, e1), e0.shape[1])
    reduce.run()
    coarse_out[net.e] = node_mlp(
        coarse_in[net.e], reduce.value(pl.ds(0, quarter)), node_in[1], node_out[1], node_gain[1:2, :]
    )
    wide[pl.ds(coarse_rows, 8), :] = jnp.zeros((8, LANES), F32)
    Relay(net, coarse_out, (a0, a1), 1).run()
    for q in range(4):
        wide[pl.ds(q * quarter, quarter), :] = coarse_out[q].astype(F32)
    back = Exchange(
        net, net.ahead,
        lambda t, peer: send.at[peer],
        lambda t: land.at[t * net.per + net.local],
        lambda t, l: land.at[t * net.per + l],
        (k0, k1, k2),
    )

    def start(t):
        gather_blocks(dest, lambda k: k * size, wide, rows, send, (net.ahead(t), net.per))
        back.send(t)

    back.loop(start)
    back.own().start()
    each = groups // pieces

    def ready(s):
        def run(t, carry):
            back.receive(t)
            return carry

        lax.fori_loop(s * each, (s + 1) * each, run, 0)
        if s == 0:
            back.own().wait()
        block = slice(s * each * net.per, (s + 1) * each * net.per)
        table[net.e, block] = (land[block].astype(F32) + mid[block].astype(F32)).astype(BF16)

    Relay(net, table, (b0, b1), pieces).run(ready)
    back.loop(lambda t: back.each(t, lambda i: back.copy(t, i).wait_send()))


def main_stage(groups, coarse_rows, ints, part, nodes, edges, weights, pieces=4):
    doms, size, _ = nodes.shape
    pieces, quarter = min(pieces, groups), coarse_rows // 4
    border_size, count = ints[0].shape[0] // doms // 4, edges.shape[0]
    vmem = pltpu.VMEM
    return pl.pallas_call(
        functools.partial(main_kernel, groups, pieces),
        out_shape=(
            jax.ShapeDtypeStruct((4, quarter, LANES), BF16),
            jax.ShapeDtypeStruct((4,) + nodes.shape, BF16),
        ),
        in_specs=[SMEM] * 4 + [VMEM] * 12,
        out_specs=(VMEM, VMEM),
        scratch_shapes=reduce_scratch(part.shape[1], 1)[:3]
        + [
            vmem(nodes.shape, BF16),
            vmem(nodes.shape, BF16),
            vmem((quarter, LANES), F32),
            vmem((coarse_rows, LANES), F32),
            vmem((4, quarter, LANES), BF16),
        ]
        + reduce_scratch(quarter, 1)[:3]
        + [
            vmem((4, quarter, LANES), BF16),
            vmem((4, doms, border_size, LANES), BF16),
            vmem((coarse_rows + 8, LANES), F32),
            vmem((doms * size, LANES), F32),
            vmem((doms, border_size, LANES), BF16),
            vmem((coarse_rows + 4 * doms * border_size, LANES), F32),
            vmem((coarse_rows, LANES), F32),
            vmem((count, LANES), F32),
            vmem(nodes.shape, BF16),
            vmem(nodes.shape, BF16),
        ]
        + reduce_scratch(quarter, groups // 2)[3:]
        + reduce_scratch(quarter, 2)[3:]
        + reduce_scratch(quarter, 2)[3:]
        + relay_sems(1)
        + relay_sems(pieces)
        + relay_sems(1)
        + relay_sems(1)
        + exchange_sems(doms)
        + exchange_sems(doms)
        + exchange_sems(doms),
        compiler_params=comm_params(1),
        name="main_stage",
    )(*ints, part, nodes, edges, *weights)


def shards(groups, coarse_rows, *args):
    (
        fine_nodes, fine_edges, fine_senders, fine_receivers, fine_halo,
        coarse_edges, coarse_senders, coarse_receivers, coarse_halo,
        pool_send, pool_dest, unpool_slot,
        edge_in_weight, edge_out_weight, node_in_weight, node_out_weight, edge_gain, node_gain,
    ) = args
    e, me = lax.axis_index("edge"), lax.axis_index("dom")
    doms = fine_halo.shape[1]
    per = doms // groups

    def nearby(p):
        away = lax.rem(me // per + groups - p // per, groups)
        step = jnp.where(2 * away <= groups, jnp.maximum(2 * away - 1, 0), 2 * (groups - away))
        return step * per + lax.rem(p, per)

    def moved(senders, rows, width):
        far = senders - rows
        size = width // 4
        owner, slot = far // width, lax.rem(far, width)
        there = rows + (slot // size) * (doms * size) + nearby(owner) * size + lax.rem(slot, size)
        return jnp.where(senders < rows, senders, there)

    slots = pool_dest.shape[2]
    own_size = slots // 4
    slot = lax.rem(unpool_slot, slots)
    place = (slot // own_size) * (doms * own_size) + nearby(unpool_slot // slots) * own_size + lax.rem(slot, own_size)
    dest = lax.dynamic_slice_in_dim(pool_dest[0], e * own_size, own_size, axis=1).reshape(-1)
    senders = moved(fine_senders, fine_nodes.shape[0], fine_halo.shape[2])
    far_senders = moved(coarse_senders, coarse_rows, coarse_halo.shape[2])

    msg, own_nodes = message_stage(
        doms, groups, fine_halo.reshape(-1), pool_send.reshape(-1), senders, fine_receivers,
        fine_nodes, fine_edges, edge_in_weight, edge_out_weight, edge_gain,
    )
    part = sum_stage(fine_receivers, place, msg, doms * slots)
    ints = (
        coarse_halo.reshape(-1), dest, far_senders, coarse_receivers,
        pool_dest.reshape(-1, LANES), dest.reshape(groups, -1), coarse_receivers.reshape(1, -1),
    )
    weights = (edge_in_weight, edge_out_weight, node_in_weight, node_out_weight, edge_gain, node_gain)
    coarse_out, table = main_stage(
        groups, coarse_rows, ints, part.reshape(4, -1, LANES), own_nodes, coarse_edges, weights
    )
    fine_out = final_stage(place, table.reshape(-1, LANES))
    return fine_out, coarse_out.reshape(-1, LANES)


def solution(mesh, groups=8, coarse_rows=2048):
    placed = (
        P("dom", None),
        P(("dom", "edge"), None),
        P(("dom", "edge")),
        P(("dom", "edge")),
        P("dom", None, None),
        P(("dom", "edge"), None),
        P(("dom", "edge")),
        P(("dom", "edge")),
        P("dom", None, None),
        P("dom", None, None),
        P("dom", None, None),
        P("dom"),
        P(),
        P(),
        P(),
        P(),
        P(),
        P(),
    )
    return jax.shard_map(
        functools.partial(shards, groups, coarse_rows),
        mesh=mesh,
        in_specs=placed,
        out_specs=(P("dom", None), P("dom", None)),
        check_vma=False,
    )
```

```python
import functools

import jax
import jax.numpy as jnp
from jax import lax
from jax.experimental import pallas as pl
from jax.experimental.pallas import tpu as pltpu
from jax.sharding import PartitionSpec as P

F32, BF16 = jnp.float32, jnp.bfloat16
VMEM = pl.BlockSpec(memory_space=pltpu.VMEM)
SMEM = pl.BlockSpec(memory_space=pltpu.SMEM)
ANY = pl.BlockSpec(memory_space=pl.ANY)
LANES = 128


def silu(v):
    return v / (1.0 + jnp.exp(-v))


def normed(v, gain):
    center = v - jnp.mean(v, axis=-1, keepdims=True)
    spread = jnp.mean(center * center, axis=-1, keepdims=True)
    return center * lax.rsqrt(spread + 1e-05) * gain


def dot(a, b):
    return jnp.dot(a, b, preferred_element_type=F32)


def node_mlp(rows, summed, w_in, w_out, gain):
    pre = dot(rows, w_in[0:LANES, :]) + dot(summed.astype(BF16), w_in[LANES : 2 * LANES, :])
    hidden = silu(pre).astype(BF16)
    return (rows.astype(F32) + normed(dot(hidden, w_out), gain)).astype(BF16)


def row_loop(total, step, body):
    def run(i, carry):
        body(pl.multiple_of(i * step, step))
        return carry

    lax.fori_loop(0, total // step, run, 0)


def widen(src, dst, step=512):
    def body(at):
        dst[pl.ds(at, step), :] = src[pl.ds(at, step), :].astype(F32)

    row_loop(src.shape[0], step, body)


def gather_rows(index, table, dst, count, unroll=16):
    def body(at):
        for j in range(unroll):
            dst[pl.ds(at + j, 1), :] = table[pl.ds(index[at + j], 1), :]

    row_loop(count, unroll, body)


def clear_all(accs, step=512):
    def body(at):
        for acc in accs:
            acc[pl.ds(at, step), :] = jnp.zeros((step, LANES), F32)

    row_loop(accs[0].shape[0] // step * step, step, body)


def add_rows(where, values, count, accs, unroll=32):
    def body(at):
        for j in range(unroll):
            acc, row = accs[j % len(accs)], where(at + j)
            acc[pl.ds(row, 1), :] = acc[pl.ds(row, 1), :] + values[pl.ds(at + j, 1), :]

    row_loop(count, unroll, body)


def sum_accs(accs, out, step=512):
    def body(at):
        value = accs[0][pl.ds(at, step), :]
        for acc in accs[1:]:
            value = value + acc[pl.ds(at, step), :]
        out[pl.ds(at, step), :] = value.astype(BF16)

    row_loop(out.shape[0], step, body)


def premultiply(rows, weight, dst, base=0, step=512):
    def body(at):
        dst[pl.ds(pl.multiple_of(base + at, step), step), :] = dot(rows[pl.ds(at, step), :], weight)

    row_loop(rows.shape[0], step, body)


def edge_mlp(msg, w_out, gain, out, step=512):
    def body(at):
        hidden = silu(msg[pl.ds(at, step), :]).astype(BF16)
        out[pl.ds(at, step), :] = normed(dot(hidden, w_out), gain)

    row_loop(msg.shape[0], step, body)


def sum_kernel(receivers, place, msg, out, held, total, sem_in, sem_out, *accs):
    load = pltpu.make_async_copy(msg, held, sem_in)
    load.start()
    clear_all(accs)
    load.wait()
    add_rows(lambda j: place[receivers[j]], held, held.shape[0], accs)
    size = out.shape[0] // 4

    def store(q):
        at = pl.ds(q * size, size)
        return pltpu.make_async_copy(total.at[at], out.at[at], sem_out.at[q])

    for q in range(4):
        at = pl.ds(q * size, size)
        sum_accs([acc.at[at] for acc in accs], total.at[at])
        store(q).start()
    for q in range(4):
        store(q).wait()


def sum_stage(receivers, place, msg, slots):
    return pl.pallas_call(
        sum_kernel,
        out_shape=jax.ShapeDtypeStruct((slots, LANES), BF16),
        in_specs=[SMEM, SMEM, ANY],
        out_specs=ANY,
        scratch_shapes=[
            pltpu.VMEM(msg.shape, F32),
            pltpu.VMEM((slots, LANES), BF16),
            pltpu.SemaphoreType.DMA,
            pltpu.SemaphoreType.DMA((4,)),
        ]
        + [pltpu.VMEM((slots, LANES), F32)] * 3,
        name="sum_stage",
    )(receivers, place, msg)


def place_kernel(groups, widths, senders, far_senders, slots, out, far_out, place):
    me = lax.axis_index("dom")
    doms, rows, width, coarse_rows, coarse_width, slot_count = widths
    per = doms // groups

    def over(value, divisor):
        shift = (divisor & -divisor).bit_length() - 1
        left = divisor >> shift
        value = lax.shift_right_logical(value, shift)
        if left == 1:
            return value
        return lax.shift_right_logical(value * ((1 << 16) // left + 1), 16)

    def split(value, divisor):
        high = over(value, divisor)
        return high, value - high * divisor

    def nearby(p):
        group, local = split(p, per)
        away = me // per + groups - group
        away = jnp.where(away >= groups, away - groups, away)
        step = jnp.where(2 * away <= groups, jnp.maximum(2 * away - 1, 0), 2 * (groups - away))
        return step * per + local

    def moved(value, near, wide):
        size = wide // 4
        owner, slot = split(jnp.maximum(value - near, 0), wide)
        quarter, inner = split(slot, size)
        there = near + quarter * (doms * size) + nearby(owner) * size + inner
        return jnp.where(value < near, value, there)

    out[...] = moved(senders[...], rows, width)
    far_out[...] = moved(far_senders[...], coarse_rows, coarse_width)
    owner, slot = split(slots[...], slot_count)
    size = slot_count // 4
    quarter, inner = split(slot, size)
    place[...] = quarter * (doms * size) + nearby(owner) * size + inner


def place_stage(groups, widths, *ints):
    shaped = [x.reshape(-1, LANES) for x in ints]
    results = pl.pallas_call(
        functools.partial(place_kernel, groups, widths),
        out_shape=[jax.ShapeDtypeStruct(x.shape, jnp.int32) for x in shaped],
        in_specs=[VMEM] * 3,
        out_specs=[VMEM] * 3,
        name="place_stage",
    )(*shaped)
    return [x.reshape(-1) for x in results]


def final_kernel(index, table, out, wide, rows):
    widen(table, wide)
    gather_rows(index, wide, rows, out.shape[0], 64)

    def pack(at):
        out[pl.ds(at, 512), :] = rows[pl.ds(at, 512), :].astype(BF16)

    row_loop(out.shape[0], 512, pack)


def final_stage(index, table):
    count = index.shape[0]
    return pl.pallas_call(
        final_kernel,
        out_shape=jax.ShapeDtypeStruct((count, LANES), BF16),
        in_specs=[SMEM, VMEM],
        out_specs=VMEM,
        scratch_shapes=[pltpu.VMEM(table.shape, F32), pltpu.VMEM((count, LANES), F32)],
        name="final_stage",
    )(index, table)


class Net:
    def __init__(self, doms, groups):
        self.doms, self.groups, self.per = doms, groups, doms // groups
        self.me = lax.axis_index("dom")
        self.e = lax.axis_index("edge")
        self.group = self.me // self.per
        self.local = lax.rem(self.me, self.per)
        self.right = lax.rem(self.e + 1, 4)
        self.left = lax.rem(self.e + 3, 4)
        self.opp = lax.rem(self.e + 2, 4)

    def greet(self):
        sem = pltpu.get_barrier_semaphore()
        pl.semaphore_signal(sem, 1, device_id={"edge": self.right})
        pl.semaphore_signal(sem, 1, device_id={"edge": self.left})

        def signal(k, carry):
            pl.semaphore_signal(sem, 1, device_id={"dom": lax.rem(self.me + k, self.doms)})
            return carry

        lax.fori_loop(1, self.doms, signal, 0)

    def meet(self):
        pl.semaphore_wait(pltpu.get_barrier_semaphore(), self.doms + 1)

    def offset(self, t):
        odd = lax.rem(t, 2)
        return odd * ((t + 1) // 2) + (1 - odd) * lax.rem(self.groups - t // 2, self.groups)

    def ahead(self, t):
        return lax.rem(self.group + self.offset(t), self.groups) * self.per

    def behind(self, t):
        return lax.rem(self.group + self.groups - self.offset(t), self.groups) * self.per


class Exchange:
    def __init__(self, net, first, source, target, landed, sems):
        self.net, self.first, self.source, self.target, self.landed = net, first, source, target, landed
        self.send_sem, self.recv_sem, self.own_sem = sems

    def copy(self, t, i):
        net = self.net
        local = lax.rem(net.local + i, net.per)
        peer = self.first(t) + local
        return pltpu.make_async_remote_copy(
            src_ref=self.source(t, peer),
            dst_ref=self.target(t),
            send_sem=self.send_sem.at[t * net.per + local],
            recv_sem=self.recv_sem.at[t * net.per + net.local],
            device_id={"dom": peer},
        )

    def own(self):
        return pltpu.make_async_copy(self.source(0, self.net.me), self.target(0), self.own_sem)

    def each(self, t, body):
        def run(i, carry):
            body(i)
            return carry

        lax.fori_loop(jnp.where(t == 0, 1, 0), self.net.per, run, 0)

    def send(self, t):
        self.each(t, lambda i: self.copy(t, i).start())

    def receive(self, t):
        net = self.net

        def wait(i):
            local = lax.rem(net.local + i, net.per)
            pltpu.make_async_remote_copy(
                src_ref=self.landed(t, local),
                dst_ref=self.landed(t, local),
                send_sem=self.send_sem.at[t * net.per + local],
                recv_sem=self.recv_sem.at[t * net.per + local],
                device_id={"dom": self.first(t) + local},
            ).wait_recv()

        self.each(t, wait)

    def loop(self, body):
        def run(t, carry):
            body(t)
            return carry

        lax.fori_loop(0, self.net.groups, run, 0)

    def finish(self):
        self.own().wait()
        self.loop(lambda t: self.each(t, lambda i: self.copy(t, i).wait_send()))


def exchange_sems(doms):
    return [pltpu.SemaphoreType.DMA((doms,)), pltpu.SemaphoreType.DMA((doms,)), pltpu.SemaphoreType.DMA]


def edge_copy(src, dst, sems, which, slot, to):
    return pltpu.make_async_remote_copy(
        src_ref=src,
        dst_ref=dst,
        send_sem=sems[0].at[which, slot],
        recv_sem=sems[1].at[which, slot],
        device_id={"edge": to},
    )


class Relay:
    def __init__(self, net, out, sems, pieces):
        self.net, self.out, self.sems, self.pieces = net, out, sems, pieces
        self.size = out.shape[1] // pieces

    def copy(self, which, owner, s, half, to):
        if half is None:
            at = pl.ds(s * self.size, self.size)
        else:
            at = pl.ds(s * self.size + half * (self.size // 2), self.size // 2)
        piece = self.out.at[owner, at]
        return edge_copy(piece, piece, self.sems, which, s, to)

    def first(self, s):
        n = self.net
        self.copy(0, n.e, s, None, n.right).start()
        self.copy(1, n.e, s, None, n.left).start()

    def second(self, s):
        n = self.net
        self.copy(0, n.left, s, None, n.right).wait_recv()
        self.copy(2, n.left, s, 0, n.right).start()
        self.copy(1, n.right, s, None, n.left).wait_recv()
        self.copy(3, n.right, s, 1, n.left).start()

    def finish(self, s):
        n = self.net
        self.copy(2, n.opp, s, 0, n.right).wait_recv()
        self.copy(3, n.opp, s, 1, n.left).wait_recv()
        self.copy(0, n.e, s, None, n.right).wait_send()
        self.copy(1, n.e, s, None, n.left).wait_send()
        self.copy(2, n.left, s, 0, n.right).wait_send()
        self.copy(3, n.right, s, 1, n.left).wait_send()

    def run(self, ready=lambda s: None, work=lambda s: None):
        for s in range(self.pieces):
            ready(s)
            self.first(s)
            if s:
                self.second(s - 1)
            work(s)
        self.second(self.pieces - 1)
        work(self.pieces)
        for s in range(self.pieces):
            self.finish(s)


def relay_sems(pieces):
    return [pltpu.SemaphoreType.DMA((4, pieces)), pltpu.SemaphoreType.DMA((4, pieces))]


class Reduce:
    def __init__(self, net, part, hop, passed, near, sems, chunks):
        self.net, self.part, self.hop, self.passed, self.near = net, part, hop, passed, near
        self.sems, self.chunks = sems, chunks
        self.half = part.shape[1] // 2
        self.size = self.half // chunks

    def a(self, c):
        return pl.ds(pl.multiple_of(c * self.size, self.size), self.size)

    def b(self, c):
        return pl.ds(pl.multiple_of(self.half + c * self.size, self.size), self.size)

    def hop_right(self, c):
        return edge_copy(self.part.at[self.net.opp, self.a(c)], self.hop.at[0, self.a(c)], self.sems, 0, c, self.net.right)

    def hop_left(self, c):
        return edge_copy(self.part.at[self.net.opp, self.b(c)], self.hop.at[1, self.a(c)], self.sems, 1, c, self.net.left)

    def raw_right(self, c):
        return edge_copy(self.part.at[self.net.right, self.b(c)], self.near.at[0, self.b(c)], self.sems, 2, c, self.net.right)

    def raw_left(self, c):
        return edge_copy(self.part.at[self.net.left, self.a(c)], self.near.at[1, self.a(c)], self.sems, 3, c, self.net.left)

    def sum_right(self, c):
        return edge_copy(self.passed.at[0, self.a(c)], self.near.at[0, self.a(c)], self.sems, 4, c, self.net.right)

    def sum_left(self, c):
        return edge_copy(self.passed.at[1, self.a(c)], self.near.at[1, self.b(c)], self.sems, 5, c, self.net.left)

    def loop(self, body):
        def run(c, carry):
            body(c)
            return carry

        lax.fori_loop(0, self.chunks, run, 0)

    def start(self, c):
        self.hop_right(c).start()
        self.hop_left(c).start()
        self.raw_right(c).start()
        self.raw_left(c).start()

    def through(self, c):
        net = self.net
        self.hop_right(c).wait_recv()
        self.passed[0, self.a(c)] = (
            self.hop[0, self.a(c)].astype(F32) + self.part[net.right, self.a(c)].astype(F32)
        ).astype(BF16)
        self.hop_left(c).wait_recv()
        self.passed[1, self.a(c)] = (
            self.hop[1, self.a(c)].astype(F32) + self.part[net.left, self.b(c)].astype(F32)
        ).astype(BF16)
        self.hop_right(c).wait_send()
        self.hop_left(c).wait_send()
        self.sum_right(c).start()
        self.sum_left(c).start()

    def finish(self, c):
        for copy in (self.raw_right(c), self.raw_left(c), self.sum_right(c), self.sum_left(c)):
            copy.wait()

    def run(self, use=lambda c: None):
        order = list(reversed(range(self.chunks)))
        self.start(order[0])
        for k, c in enumerate(order):
            if k + 1 < self.chunks:
                self.start(order[k + 1])
            self.through(c)
            if k:
                self.finish(order[k - 1])
                use(order[k - 1])
        self.finish(order[-1])
        use(order[-1])

    def value(self, rows):
        return (
            self.part[self.net.e, rows].astype(F32)
            + self.near[0, rows].astype(F32)
            + self.near[1, rows].astype(F32)
        )


def reduce_scratch(rows, chunks):
    return [
        pltpu.VMEM((2, rows // 2, LANES), BF16),
        pltpu.VMEM((2, rows // 2, LANES), BF16),
        pltpu.VMEM((2, rows, LANES), BF16),
        pltpu.SemaphoreType.DMA((6, chunks)),
        pltpu.SemaphoreType.DMA((6, chunks)),
    ]


def gather_blocks(index, base, table, rows, dst, blocks):
    size = dst.shape[1]

    def body(i, carry):
        k = blocks[0] + i
        (line, start), at = base(k), pl.multiple_of(k * size, size)
        for j in range(size):
            rows[pl.ds(at + j, 1), :] = table[pl.ds(index[line, start + j], 1), :]
        dst[k] = rows[pl.ds(at, size), :].astype(BF16)
        return carry

    lax.fori_loop(0, blocks[1], body, 0)


def message_kernel(
    groups, pieces, halo, pool_send, senders, receivers, nodes, edges, w_in, w_out, gain,
    out, own_nodes, ghosts, wide, rows, send, table_s, table_r, msg, s0, s1, s2, r0, r1,
):
    doms, size, own_size = ghosts.shape[1], ghosts.shape[2], own_nodes.shape[1]
    count, near = edges.shape[0], nodes.shape[0]
    net = Net(doms, groups)
    net.greet()
    widen(nodes, wide)
    gather_blocks(halo, lambda k: (k, net.e * size), wide, rows, send, (0, doms))
    net.meet()
    land = ghosts.at[net.e]
    exchange = Exchange(
        net, net.ahead,
        lambda t, peer: send.at[peer],
        lambda t: land.at[t * net.per + net.local],
        lambda t, l: land.at[t * net.per + l],
        (s0, s1, s2),
    )
    exchange.own().start()
    exchange.loop(exchange.send)
    w = w_in[0]
    premultiply(nodes, w[LANES : 2 * LANES, :], table_r)
    premultiply(edges, w[2 * LANES :, :], msg)

    def gather_near(at):
        for j in range(32):
            msg[pl.ds(at + j, 1), :] = msg[pl.ds(at + j, 1), :] + table_r[pl.ds(receivers[at + j], 1), :]

    row_loop(count, 32, gather_near)
    premultiply(nodes, w[0:LANES, :], table_s)
    each = groups // pieces

    def ready(s):
        def run(t, carry):
            exchange.receive(t)
            return carry

        lax.fori_loop(s * each, (s + 1) * each, run, 0)
        if s == 0:
            exchange.own().wait()

    def base(k):
        p = net.behind(k // net.per) + lax.rem(k, net.per)
        return p, net.e * own_size

    part = doms // (pieces + 1) if doms % (pieces + 1) == 0 else doms // (2 * pieces)

    def work(s):
        first = s * part
        gather_blocks(pool_send, base, wide, rows, own_nodes, (first, part if s < pieces else doms - first))

    Relay(net, ghosts, (r0, r1), pieces).run(ready, work)
    for owner in range(4):
        block = ghosts[owner].reshape(doms * size, LANES)
        table_s[pl.ds(near + owner * doms * size, doms * size), :] = dot(block, w[0:LANES, :])

    def gather_far(at):
        for j in range(32):
            msg[pl.ds(at + j, 1), :] = msg[pl.ds(at + j, 1), :] + table_s[pl.ds(senders[at + j], 1), :]

    row_loop(count, 32, gather_far)
    edge_mlp(msg, w_out[0], gain[0:1, :], out)
    exchange.loop(lambda t: exchange.each(t, lambda i: exchange.copy(t, i).wait_send()))


def comm_params(collective_id):
    return pltpu.CompilerParams(collective_id=collective_id, has_side_effects=True)


def message_stage(doms, groups, halo, pool_send, senders, receivers, nodes, edges, w_in, w_out, gain, pieces=2):
    size, own_size = halo.shape[1] // 4, pool_send.shape[1] // 4
    near, count = nodes.shape[0], edges.shape[0]
    return pl.pallas_call(
        functools.partial(message_kernel, groups, pieces),
        out_shape=(
            jax.ShapeDtypeStruct((count, LANES), F32),
            jax.ShapeDtypeStruct((doms, own_size, LANES), BF16),
        ),
        in_specs=[SMEM] * 4 + [VMEM] * 5,
        out_specs=(VMEM, VMEM),
        scratch_shapes=[
            pltpu.VMEM((4, doms, size, LANES), BF16),
            pltpu.VMEM(nodes.shape, F32),
            pltpu.VMEM((doms * own_size, LANES), F32),
            pltpu.VMEM((doms, size, LANES), BF16),
            pltpu.VMEM((near + 4 * doms * size, LANES), F32),
            pltpu.VMEM((near, LANES), F32),
            pltpu.VMEM((count, LANES), F32),
        ]
        + exchange_sems(doms)
        + relay_sems(pieces),
        compiler_params=comm_params(0),
        name="message_stage",
    )(halo, pool_send, senders, receivers, nodes, edges, w_in, w_out, gain)


def child_counts(all_dest, first, counts, step=128):
    lines, width = all_dest.shape

    def rows(at):
        target = lax.broadcasted_iota(jnp.int32, (step, width), 0) + (first + at)

        def line(i, total):
            for j in range(4):
                hit = all_dest[pl.ds(i * 4 + j, 1), :] == target
                total = total + jnp.where(hit, 1.0, 0.0)
            return total

        total = lax.fori_loop(0, lines // 4, line, jnp.zeros((step, width), F32))
        counts[pl.ds(at, step), :] = jnp.broadcast_to(jnp.sum(total, axis=1, keepdims=True), (step, LANES))

    row_loop(counts.shape[0], step, rows)


def one_hot(index, first, rows):
    at = lax.broadcasted_iota(jnp.int32, (rows, index.shape[1]), 0) + first
    return jnp.where(at == index, 1.0, 0.0).astype(BF16)


def main_kernel(
    groups, pieces, halo, dest, senders, receivers, all_dest, group_dest, line_receivers,
    part_there, nodes_there, edges, edge_in, edge_out, node_in, node_out, edge_gain, node_gain,
    coarse_out, table,
    part, nodes, load_sems, hop, passed, near, mid, arrived, counts, pooled, coarse_part, coarse_hop, coarse_passed, coarse_near,
    coarse_in, ghosts, wide, rows, border, table_s, table_r, msg, send, land,
    f0, f1, p0, p1, e0, e1, a0, a1, b0, b1, g0, g1, h0, h1, i0, i1, i2, j0, j1, j2, k0, k1, k2,
):
    doms, size = mid.shape[0], mid.shape[1]
    quarter, border_size = coarse_in.shape[1], ghosts.shape[2]
    coarse_rows, count = 4 * quarter, edges.shape[0]
    net = Net(doms, groups)
    load_part = pltpu.make_async_copy(part_there, part, load_sems.at[0])
    load_nodes = pltpu.make_async_copy(nodes_there, nodes, load_sems.at[1])
    load_part.start()
    load_nodes.start()
    net.greet()
    premultiply(edges, edge_in[1, 2 * LANES :, :], msg)
    child_counts(all_dest, net.e * quarter, counts)
    pooled[...] = jnp.zeros_like(pooled)
    load_part.wait()
    load_nodes.wait()
    net.meet()

    reduce = Reduce(net, part, hop, passed, near, (f0, f1), groups // 2)
    pool = Exchange(
        net, net.behind,
        lambda t, peer: mid.at[t * net.per + lax.rem(peer, net.per)],
        lambda t: arrived.at[net.me],
        lambda t, l: arrived.at[net.ahead(t) + l],
        (i0, i1, i2),
    )
    span = net.per * size

    def use(c):
        units = (groups // 2 + c, c)
        for u in units:
            own = nodes[u * net.per : (u + 1) * net.per].reshape(span, LANES)
            result = node_mlp(own, reduce.value(pl.ds(u * span, span)), node_in[0], node_out[0], node_gain[0:1, :])
            mid[u * net.per : (u + 1) * net.per] = result.reshape(net.per, size, LANES)
        if c == 0:
            pool.own().start()
        for u in units:
            pool.send(u)

    reduce.run(use)

    def gathered(k, carry):
        c = groups // 2 - 1 - k // 2
        t = c + (1 - lax.rem(k, 2)) * (groups // 2)
        pool.receive(t)

        @pl.when(t == 0)
        def _():
            pool.own().wait()

        first = net.ahead(t)
        block = arrived[pl.ds(first, net.per)].reshape(span, LANES)
        index = group_dest[pl.ds(first // net.per, 1), :]
        for q in range(4):
            at = pl.ds(q * quarter, quarter)
            pooled[at, :] = pooled[at, :] + dot(one_hot(index, q * quarter, quarter), block)
        return carry

    lax.fori_loop(0, groups, gathered, 0)
    for owner in (net.opp, net.right, net.left, net.e):
        at = pl.ds(pl.multiple_of(owner * quarter, quarter), quarter)
        coarse_part[owner] = pooled[at, :].astype(BF16)
    pool.loop(lambda t: pool.each(t, lambda i: pool.copy(t, i).wait_send()))

    reduce = Reduce(net, coarse_part, coarse_hop, coarse_passed, coarse_near, (p0, p1), p0.shape[1])
    reduce.run()
    mean = reduce.value(pl.ds(0, quarter)) / jnp.maximum(counts[...], 1.0)
    coarse_in[net.e] = mean.astype(BF16)
    Relay(net, coarse_in, (g0, g1), 1).run()
    for q in range(4):
        wide[pl.ds(q * quarter, quarter), :] = coarse_in[q].astype(F32)
    gather_blocks(halo, lambda k: (k, net.e * border_size), wide, rows, border, (0, doms))
    here = ghosts.at[net.e]
    exchange = Exchange(
        net, net.ahead,
        lambda t, peer: border.at[peer],
        lambda t: here.at[t * net.per + net.local],
        lambda t, l: here.at[t * net.per + l],
        (j0, j1, j2),
    )
    exchange.own().start()
    exchange.loop(exchange.send)
    w = edge_in[1]
    for q in range(4):
        table_r[pl.ds(q * quarter, quarter), :] = dot(coarse_in[q], w[LANES : 2 * LANES, :])
        table_s[pl.ds(q * quarter, quarter), :] = dot(coarse_in[q], w[0:LANES, :])

    def gather_near(at):
        for j in range(32):
            msg[pl.ds(at + j, 1), :] = msg[pl.ds(at + j, 1), :] + table_r[pl.ds(receivers[at + j], 1), :]

    row_loop(count, 32, gather_near)

    def ready(s):
        def run(t, carry):
            exchange.receive(t)
            return carry

        lax.fori_loop(s * (groups // 2), (s + 1) * (groups // 2), run, 0)
        if s == 0:
            exchange.own().wait()

    Relay(net, ghosts, (h0, h1), 2).run(ready)
    exchange.loop(lambda t: exchange.each(t, lambda i: exchange.copy(t, i).wait_send()))
    for owner in range(4):
        block = ghosts[owner].reshape(doms * border_size, LANES)
        at = pl.ds(coarse_rows + owner * doms * border_size, doms * border_size)
        table_s[at, :] = dot(block, w[0:LANES, :])

    def gather_far(at):
        for j in range(32):
            msg[pl.ds(at + j, 1), :] = msg[pl.ds(at + j, 1), :] + table_s[pl.ds(senders[at + j], 1), :]

    row_loop(count, 32, gather_far)
    edge_mlp(msg, edge_out[1], edge_gain[1:2, :], msg)
    high = msg[...].astype(BF16)
    low = (msg[...] - high.astype(F32)).astype(BF16)
    both = jnp.concatenate([high, low], axis=1)
    for owner in (net.opp, net.right, net.left, net.e):
        sums = dot(one_hot(line_receivers[...], owner * quarter, quarter), both)
        coarse_part[owner] = (sums[:, 0:LANES] + sums[:, LANES:]).astype(BF16)

    reduce = Reduce(net, coarse_part, coarse_hop, coarse_passed, coarse_near, (e0, e1), e0.shape[1])
    reduce.run()
    coarse_out[net.e] = node_mlp(
        coarse_in[net.e], reduce.value(pl.ds(0, quarter)), node_in[1], node_out[1], node_gain[1:2, :]
    )
    wide[pl.ds(coarse_rows, 8), :] = jnp.zeros((8, LANES), F32)
    Relay(net, coarse_out, (a0, a1), 1).run()
    for q in range(4):
        wide[pl.ds(q * quarter, quarter), :] = coarse_out[q].astype(F32)
    back = Exchange(
        net, net.ahead,
        lambda t, peer: send.at[peer],
        lambda t: land.at[t * net.per + net.local],
        lambda t, l: land.at[t * net.per + l],
        (k0, k1, k2),
    )

    def start(t):
        gather_blocks(dest, lambda k: (k, net.e * size), wide, rows, send, (net.ahead(t), net.per))
        back.send(t)

    back.loop(start)
    back.own().start()
    each = groups // pieces

    def ready(s):
        def run(t, carry):
            back.receive(t)
            return carry

        lax.fori_loop(s * each, (s + 1) * each, run, 0)
        if s == 0:
            back.own().wait()
        block = slice(s * each * net.per, (s + 1) * each * net.per)
        table[net.e, block] = (land[block].astype(F32) + mid[block].astype(F32)).astype(BF16)

    Relay(net, table, (b0, b1), pieces).run(ready)
    back.loop(lambda t: back.each(t, lambda i: back.copy(t, i).wait_send()))


def main_stage(groups, coarse_rows, ints, part, nodes, edges, weights, pieces=4):
    doms, size, _ = nodes.shape
    pieces, quarter = min(pieces, groups), coarse_rows // 4
    border_size, count = ints[0].shape[1] // 4, edges.shape[0]
    vmem = pltpu.VMEM
    return pl.pallas_call(
        functools.partial(main_kernel, groups, pieces),
        out_shape=(
            jax.ShapeDtypeStruct((4, quarter, LANES), BF16),
            jax.ShapeDtypeStruct((4,) + nodes.shape, BF16),
        ),
        in_specs=[SMEM] * 4 + [VMEM] * 3 + [ANY] * 2 + [VMEM] * 7,
        out_specs=(VMEM, VMEM),
        scratch_shapes=[vmem(part.shape, BF16), vmem(nodes.shape, BF16), pltpu.SemaphoreType.DMA((2,))]
        + reduce_scratch(part.shape[1], 1)[:3]
        + [
            vmem(nodes.shape, BF16),
            vmem(nodes.shape, BF16),
            vmem((quarter, LANES), F32),
            vmem((coarse_rows, LANES), F32),
            vmem((4, quarter, LANES), BF16),
        ]
        + reduce_scratch(quarter, 1)[:3]
        + [
            vmem((4, quarter, LANES), BF16),
            vmem((4, doms, border_size, LANES), BF16),
            vmem((coarse_rows + 8, LANES), F32),
            vmem((doms * size, LANES), F32),
            vmem((doms, border_size, LANES), BF16),
            vmem((coarse_rows + 4 * doms * border_size, LANES), F32),
            vmem((coarse_rows, LANES), F32),
            vmem((count, LANES), F32),
            vmem(nodes.shape, BF16),
            vmem(nodes.shape, BF16),
        ]
        + reduce_scratch(quarter, groups // 2)[3:]
        + reduce_scratch(quarter, 2)[3:]
        + reduce_scratch(quarter, 2)[3:]
        + relay_sems(1)
        + relay_sems(pieces)
        + relay_sems(1)
        + relay_sems(2)
        + exchange_sems(doms)
        + exchange_sems(doms)
        + exchange_sems(doms),
        compiler_params=comm_params(1),
        name="main_stage",
    )(*ints, part, nodes, edges, *weights)


def shards(groups, coarse_rows, *args):
    (
        fine_nodes, fine_edges, fine_senders, fine_receivers, fine_halo,
        coarse_edges, coarse_senders, coarse_receivers, coarse_halo,
        pool_send, pool_dest, unpool_slot,
        edge_in_weight, edge_out_weight, node_in_weight, node_out_weight, edge_gain, node_gain,
    ) = args
    e = lax.axis_index("edge")
    doms = fine_halo.shape[1]
    slots = pool_dest.shape[2]
    group_dest = lax.dynamic_slice_in_dim(pool_dest[0], e * (slots // 4), slots // 4, axis=1).reshape(groups, -1)
    widths = (doms, fine_nodes.shape[0], fine_halo.shape[2], coarse_rows, coarse_halo.shape[2], slots)
    senders, far_senders, place = place_stage(groups, widths, fine_senders, coarse_senders, unpool_slot)

    msg, own_nodes = message_stage(
        doms, groups, fine_halo[0], pool_send[0], senders, fine_receivers,
        fine_nodes, fine_edges, edge_in_weight, edge_out_weight, edge_gain,
    )
    part = sum_stage(fine_receivers, place, msg, doms * slots)
    ints = (
        coarse_halo[0], pool_dest[0], far_senders, coarse_receivers,
        pool_dest[0], group_dest, coarse_receivers.reshape(1, -1),
    )
    weights = (edge_in_weight, edge_out_weight, node_in_weight, node_out_weight, edge_gain, node_gain)
    coarse_out, table = main_stage(
        groups, coarse_rows, ints, part.reshape(4, -1, LANES), own_nodes, coarse_edges, weights
    )
    fine_out = final_stage(place, table.reshape(-1, LANES))
    return fine_out, coarse_out.reshape(-1, LANES)


def solution(mesh, groups=8, coarse_rows=2048):
    placed = (
        P("dom", None),
        P(("dom", "edge"), None),
        P(("dom", "edge")),
        P(("dom", "edge")),
        P("dom", None, None),
        P(("dom", "edge"), None),
        P(("dom", "edge")),
        P(("dom", "edge")),
        P("dom", None, None),
        P("dom", None, None),
        P("dom", None, None),
        P("dom"),
        P(),
        P(),
        P(),
        P(),
        P(),
        P(),
    )
    return jax.shard_map(
        functools.partial(shards, groups, coarse_rows),
        mesh=mesh,
        in_specs=placed,
        out_specs=(P("dom", None), P("dom", None)),
        check_vma=False,
    )
```

```python
import functools

import jax
import jax.numpy as jnp
from jax import lax
from jax.experimental import pallas as pl
from jax.experimental.pallas import tpu as pltpu
from jax.sharding import PartitionSpec as P

F32, BF16 = jnp.float32, jnp.bfloat16
VMEM = pl.BlockSpec(memory_space=pltpu.VMEM)
SMEM = pl.BlockSpec(memory_space=pltpu.SMEM)
ANY = pl.BlockSpec(memory_space=pl.ANY)
LANES = 128


def silu(v):
    return v / (1.0 + jnp.exp(-v))


def normed(v, gain):
    center = v - jnp.mean(v, axis=-1, keepdims=True)
    spread = jnp.mean(center * center, axis=-1, keepdims=True)
    return center * lax.rsqrt(spread + 1e-05) * gain


def dot(a, b):
    return jnp.dot(a, b, preferred_element_type=F32)


def node_mlp(rows, summed, w_in, w_out, gain):
    pre = dot(rows, w_in[0:LANES, :]) + dot(summed.astype(BF16), w_in[LANES : 2 * LANES, :])
    hidden = silu(pre).astype(BF16)
    return (rows.astype(F32) + normed(dot(hidden, w_out), gain)).astype(BF16)


def row_loop(total, step, body):
    def run(i, carry):
        body(pl.multiple_of(i * step, step))
        return carry

    lax.fori_loop(0, total // step, run, 0)


def widen(src, dst, step=512):
    def body(at):
        dst[pl.ds(at, step), :] = src[pl.ds(at, step), :].astype(F32)

    row_loop(src.shape[0], step, body)


def clear_all(accs, step=512):
    def body(at):
        for acc in accs:
            acc[pl.ds(at, step), :] = jnp.zeros((step, LANES), F32)

    row_loop(accs[0].shape[0] // step * step, step, body)


def add_rows(where, values, count, accs, unroll=32):
    def body(at):
        for j in range(unroll):
            acc, row = accs[j % len(accs)], where(at + j)
            acc[pl.ds(row, 1), :] = acc[pl.ds(row, 1), :] + values[pl.ds(at + j, 1), :]

    row_loop(count, unroll, body)


def sum_accs(accs, out, step=512):
    def body(at):
        value = accs[0][pl.ds(at, step), :]
        for acc in accs[1:]:
            value = value + acc[pl.ds(at, step), :]
        out[pl.ds(at, step), :] = value.astype(BF16)

    row_loop(out.shape[0], step, body)


def premultiply(rows, weight, dst, base=0, step=512):
    def body(at):
        dst[pl.ds(pl.multiple_of(base + at, step), step), :] = dot(rows[pl.ds(at, step), :], weight)

    row_loop(rows.shape[0], step, body)


def edge_mlp(msg, w_out, gain, out, step=512):
    def body(at):
        hidden = silu(msg[pl.ds(at, step), :]).astype(BF16)
        out[pl.ds(at, step), :] = normed(dot(hidden, w_out), gain)

    row_loop(msg.shape[0], step, body)


def sum_kernel(receivers, place, msg, out, held, total, sem_in, sem_out, *accs):
    load = pltpu.make_async_copy(msg, held, sem_in)
    load.start()
    clear_all(accs)
    load.wait()
    add_rows(lambda j: place[receivers[j]], held, held.shape[0], accs)
    size = out.shape[0] // 4

    def store(q):
        at = pl.ds(q * size, size)
        return pltpu.make_async_copy(total.at[at], out.at[at], sem_out.at[q])

    for q in range(4):
        at = pl.ds(q * size, size)
        sum_accs([acc.at[at] for acc in accs], total.at[at])
        store(q).start()
    for q in range(4):
        store(q).wait()


def sum_stage(receivers, place, msg, slots):
    return pl.pallas_call(
        sum_kernel,
        out_shape=jax.ShapeDtypeStruct((slots, LANES), BF16),
        in_specs=[SMEM, SMEM, ANY],
        out_specs=ANY,
        scratch_shapes=[
            pltpu.VMEM(msg.shape, F32),
            pltpu.VMEM((slots, LANES), BF16),
            pltpu.SemaphoreType.DMA,
            pltpu.SemaphoreType.DMA((4,)),
        ]
        + [pltpu.VMEM((slots, LANES), F32)] * 3,
        name="sum_stage",
    )(receivers, place, msg)


def place_kernel(groups, widths, senders, far_senders, slots, out, far_out, place):
    me = lax.axis_index("dom")
    doms, rows, width, coarse_rows, coarse_width, slot_count = widths
    per = doms // groups

    def over(value, divisor):
        shift = (divisor & -divisor).bit_length() - 1
        left = divisor >> shift
        value = lax.shift_right_logical(value, shift)
        if left == 1:
            return value
        return lax.shift_right_logical(value * ((1 << 16) // left + 1), 16)

    def split(value, divisor):
        high = over(value, divisor)
        return high, value - high * divisor

    def nearby(p):
        group, local = split(p, per)
        away = me // per + groups - group
        away = jnp.where(away >= groups, away - groups, away)
        step = jnp.where(2 * away <= groups, jnp.maximum(2 * away - 1, 0), 2 * (groups - away))
        return step * per + local

    def moved(value, near, wide):
        size = wide // 4
        owner, slot = split(jnp.maximum(value - near, 0), wide)
        quarter, inner = split(slot, size)
        there = near + quarter * (doms * size) + nearby(owner) * size + inner
        return jnp.where(value < near, value, there)

    out[...] = moved(senders[...], rows, width)
    far_out[...] = moved(far_senders[...], coarse_rows, coarse_width)
    owner, slot = split(slots[...], slot_count)
    size = slot_count // 4
    quarter, inner = split(slot, size)
    place[...] = quarter * (doms * size) + nearby(owner) * size + inner


def place_stage(groups, widths, *ints):
    shaped = [x.reshape(-1, LANES) for x in ints]
    results = pl.pallas_call(
        functools.partial(place_kernel, groups, widths),
        out_shape=[jax.ShapeDtypeStruct(x.shape, jnp.int32) for x in shaped],
        in_specs=[VMEM] * 3,
        out_specs=[VMEM] * 3,
        name="place_stage",
    )(*shaped)
    return [x.reshape(-1) for x in results]


class Net:
    def __init__(self, doms, groups):
        self.doms, self.groups, self.per = doms, groups, doms // groups
        self.me = lax.axis_index("dom")
        self.e = lax.axis_index("edge")
        self.group = self.me // self.per
        self.local = lax.rem(self.me, self.per)
        self.right = lax.rem(self.e + 1, 4)
        self.left = lax.rem(self.e + 3, 4)
        self.opp = lax.rem(self.e + 2, 4)

    def greet(self):
        sem = pltpu.get_barrier_semaphore()
        pl.semaphore_signal(sem, 1, device_id={"edge": self.right})
        pl.semaphore_signal(sem, 1, device_id={"edge": self.left})

        def signal(k, carry):
            pl.semaphore_signal(sem, 1, device_id={"dom": lax.rem(self.me + k, self.doms)})
            return carry

        lax.fori_loop(1, self.doms, signal, 0)

    def meet(self):
        pl.semaphore_wait(pltpu.get_barrier_semaphore(), self.doms + 1)

    def offset(self, t):
        odd = lax.rem(t, 2)
        return odd * ((t + 1) // 2) + (1 - odd) * lax.rem(self.groups - t // 2, self.groups)

    def ahead(self, t):
        return lax.rem(self.group + self.offset(t), self.groups) * self.per

    def behind(self, t):
        return lax.rem(self.group + self.groups - self.offset(t), self.groups) * self.per


class Exchange:
    def __init__(self, net, first, source, target, landed, sems):
        self.net, self.first, self.source, self.target, self.landed = net, first, source, target, landed
        self.send_sem, self.recv_sem, self.own_sem = sems

    def copy(self, t, i):
        net = self.net
        local = lax.rem(net.local + i, net.per)
        peer = self.first(t) + local
        return pltpu.make_async_remote_copy(
            src_ref=self.source(t, peer),
            dst_ref=self.target(t),
            send_sem=self.send_sem.at[t * net.per + local],
            recv_sem=self.recv_sem.at[t * net.per + net.local],
            device_id={"dom": peer},
        )

    def own(self):
        return pltpu.make_async_copy(self.source(0, self.net.me), self.target(0), self.own_sem)

    def each(self, t, body):
        def run(i, carry):
            body(i)
            return carry

        lax.fori_loop(jnp.where(t == 0, 1, 0), self.net.per, run, 0)

    def send(self, t):
        self.each(t, lambda i: self.copy(t, i).start())

    def receive(self, t):
        net = self.net

        def wait(i):
            local = lax.rem(net.local + i, net.per)
            pltpu.make_async_remote_copy(
                src_ref=self.landed(t, local),
                dst_ref=self.landed(t, local),
                send_sem=self.send_sem.at[t * net.per + local],
                recv_sem=self.recv_sem.at[t * net.per + local],
                device_id={"dom": self.first(t) + local},
            ).wait_recv()

        self.each(t, wait)

    def loop(self, body):
        def run(t, carry):
            body(t)
            return carry

        lax.fori_loop(0, self.net.groups, run, 0)

    def finish(self):
        self.own().wait()
        self.loop(lambda t: self.each(t, lambda i: self.copy(t, i).wait_send()))


def exchange_sems(doms):
    return [pltpu.SemaphoreType.DMA((doms,)), pltpu.SemaphoreType.DMA((doms,)), pltpu.SemaphoreType.DMA]


def edge_copy(src, dst, sems, which, slot, to):
    return pltpu.make_async_remote_copy(
        src_ref=src,
        dst_ref=dst,
        send_sem=sems[0].at[which, slot],
        recv_sem=sems[1].at[which, slot],
        device_id={"edge": to},
    )


class Relay:
    def __init__(self, net, out, sems, sizes):
        self.net, self.out, self.sems, self.sizes = net, out, sems, sizes
        self.pieces = len(sizes)

    def range(self, s):
        return sum(self.sizes[:s]), self.sizes[s]

    def copy(self, which, owner, s, half, to):
        first, size = self.range(s)
        if half is None:
            at = pl.ds(first, size)
        else:
            at = pl.ds(first + half * (size // 2), size // 2)
        piece = self.out.at[owner, at]
        return edge_copy(piece, piece, self.sems, which, s, to)

    def first(self, s):
        n = self.net
        self.copy(0, n.e, s, None, n.right).start()
        self.copy(1, n.e, s, None, n.left).start()

    def second(self, s):
        n = self.net
        self.copy(0, n.left, s, None, n.right).wait_recv()
        self.copy(2, n.left, s, 0, n.right).start()
        self.copy(1, n.right, s, None, n.left).wait_recv()
        self.copy(3, n.right, s, 1, n.left).start()

    def finish(self, s):
        n = self.net
        self.copy(2, n.opp, s, 0, n.right).wait_recv()
        self.copy(3, n.opp, s, 1, n.left).wait_recv()
        self.copy(0, n.e, s, None, n.right).wait_send()
        self.copy(1, n.e, s, None, n.left).wait_send()
        self.copy(2, n.left, s, 0, n.right).wait_send()
        self.copy(3, n.right, s, 1, n.left).wait_send()

    def run(self, ready=lambda s: None, work=lambda s: None, got=lambda owner, s: None):
        n, last = self.net, self.pieces - 1
        for s in range(self.pieces + 1):
            if s <= last:
                ready(s)
                self.first(s)
            if s:
                self.second(s - 1)
            work(s)
            if s <= last:
                got(n.e, s)
            if s:
                got(n.left, s - 1)
                got(n.right, s - 1)
        for s in range(self.pieces):
            self.finish(s)
            got(n.opp, s)


def relay_sems(pieces):
    return [pltpu.SemaphoreType.DMA((4, pieces)), pltpu.SemaphoreType.DMA((4, pieces))]


class Reduce:
    def __init__(self, net, part, hop, passed, near, sems, chunks):
        self.net, self.part, self.hop, self.passed, self.near = net, part, hop, passed, near
        self.sems, self.chunks = sems, chunks
        self.half = part.shape[1] // 2
        self.size = self.half // chunks

    def a(self, c):
        return pl.ds(pl.multiple_of(c * self.size, self.size), self.size)

    def b(self, c):
        return pl.ds(pl.multiple_of(self.half + c * self.size, self.size), self.size)

    def hop_right(self, c):
        return edge_copy(self.part.at[self.net.opp, self.a(c)], self.hop.at[0, self.a(c)], self.sems, 0, c, self.net.right)

    def hop_left(self, c):
        return edge_copy(self.part.at[self.net.opp, self.b(c)], self.hop.at[1, self.a(c)], self.sems, 1, c, self.net.left)

    def raw_right(self, c):
        return edge_copy(self.part.at[self.net.right, self.b(c)], self.near.at[0, self.b(c)], self.sems, 2, c, self.net.right)

    def raw_left(self, c):
        return edge_copy(self.part.at[self.net.left, self.a(c)], self.near.at[1, self.a(c)], self.sems, 3, c, self.net.left)

    def sum_right(self, c):
        return edge_copy(self.passed.at[0, self.a(c)], self.near.at[0, self.a(c)], self.sems, 4, c, self.net.right)

    def sum_left(self, c):
        return edge_copy(self.passed.at[1, self.a(c)], self.near.at[1, self.b(c)], self.sems, 5, c, self.net.left)

    def loop(self, body):
        def run(c, carry):
            body(c)
            return carry

        lax.fori_loop(0, self.chunks, run, 0)

    def start(self, c):
        self.hop_right(c).start()
        self.hop_left(c).start()
        self.raw_right(c).start()
        self.raw_left(c).start()

    def through(self, c):
        net = self.net
        self.hop_right(c).wait_recv()
        self.passed[0, self.a(c)] = (
            self.hop[0, self.a(c)].astype(F32) + self.part[net.right, self.a(c)].astype(F32)
        ).astype(BF16)
        self.hop_left(c).wait_recv()
        self.passed[1, self.a(c)] = (
            self.hop[1, self.a(c)].astype(F32) + self.part[net.left, self.b(c)].astype(F32)
        ).astype(BF16)
        self.hop_right(c).wait_send()
        self.hop_left(c).wait_send()
        self.sum_right(c).start()
        self.sum_left(c).start()

    def finish(self, c):
        for copy in (self.raw_right(c), self.raw_left(c), self.sum_right(c), self.sum_left(c)):
            copy.wait()

    def run(self, use=lambda c: None):
        order = list(reversed(range(self.chunks)))
        self.start(order[0])
        for k, c in enumerate(order):
            if k + 1 < self.chunks:
                self.start(order[k + 1])
            self.through(c)
            if k:
                self.finish(order[k - 1])
                use(order[k - 1])
        self.finish(order[-1])
        use(order[-1])

    def value(self, rows):
        return (
            self.part[self.net.e, rows].astype(F32)
            + self.near[0, rows].astype(F32)
            + self.near[1, rows].astype(F32)
        )


def reduce_scratch(rows, chunks):
    return [
        pltpu.VMEM((2, rows // 2, LANES), BF16),
        pltpu.VMEM((2, rows // 2, LANES), BF16),
        pltpu.VMEM((2, rows, LANES), BF16),
        pltpu.SemaphoreType.DMA((6, chunks)),
        pltpu.SemaphoreType.DMA((6, chunks)),
    ]


def gather_blocks(index, base, table, rows, dst, blocks):
    size = dst.shape[1]

    def body(i, carry):
        k = blocks[0] + i
        line, at = base(k), pl.multiple_of(k * size, size)
        for j in range(size):
            rows[pl.ds(at + j, 1), :] = table[pl.ds(index[line, j], 1), :]
        dst[k] = rows[pl.ds(at, size), :].astype(BF16)
        return carry

    lax.fori_loop(0, blocks[1], body, 0)


def message_kernel(
    groups, pieces, halo, pool_send, senders, receivers, nodes, edges, w_in, w_out, gain,
    out, own_nodes, ghosts, wide, rows, send, table_s, table_r, msg, s0, s1, s2, r0, r1,
):
    doms, size, own_size = ghosts.shape[1], ghosts.shape[2], own_nodes.shape[1]
    count, near = edges.shape[0], nodes.shape[0]
    net = Net(doms, groups)
    net.greet()
    widen(nodes, wide)
    gather_blocks(halo, lambda k: k, wide, rows, send, (0, doms))
    net.meet()
    land = ghosts.at[net.e]
    exchange = Exchange(
        net, net.ahead,
        lambda t, peer: send.at[peer],
        lambda t: land.at[t * net.per + net.local],
        lambda t, l: land.at[t * net.per + l],
        (s0, s1, s2),
    )
    exchange.own().start()
    exchange.loop(exchange.send)
    w = w_in[0]
    premultiply(nodes, w[LANES : 2 * LANES, :], table_r)
    premultiply(edges, w[2 * LANES :, :], msg)

    def gather_near(at):
        for j in range(32):
            msg[pl.ds(at + j, 1), :] = msg[pl.ds(at + j, 1), :] + table_r[pl.ds(receivers[at + j], 1), :]

    row_loop(count, 32, gather_near)
    premultiply(nodes, w[0:LANES, :], table_s)
    each = groups // pieces

    def ready(s):
        def run(t, carry):
            exchange.receive(t)
            return carry

        lax.fori_loop(s * each, (s + 1) * each, run, 0)
        if s == 0:
            exchange.own().wait()

    def base(k):
        p = net.behind(k // net.per) + lax.rem(k, net.per)
        return p

    part = doms // (pieces + 1) if doms % (pieces + 1) == 0 else doms // (2 * pieces)

    def work(s):
        first = s * part
        gather_blocks(pool_send, base, wide, rows, own_nodes, (first, part if s < pieces else doms - first))

    Relay(net, ghosts, (r0, r1), [doms // pieces] * pieces).run(ready, work)
    for owner in range(4):
        block = ghosts[owner].reshape(doms * size, LANES)
        table_s[pl.ds(near + owner * doms * size, doms * size), :] = dot(block, w[0:LANES, :])

    def gather_far(at):
        for j in range(32):
            msg[pl.ds(at + j, 1), :] = msg[pl.ds(at + j, 1), :] + table_s[pl.ds(senders[at + j], 1), :]

    row_loop(count, 32, gather_far)
    edge_mlp(msg, w_out[0], gain[0:1, :], out)
    exchange.loop(lambda t: exchange.each(t, lambda i: exchange.copy(t, i).wait_send()))


def comm_params(collective_id):
    return pltpu.CompilerParams(collective_id=collective_id, has_side_effects=True)


def message_stage(doms, groups, halo, pool_send, senders, receivers, nodes, edges, w_in, w_out, gain, pieces=2):
    size, own_size = halo.shape[1], pool_send.shape[1]
    near, count = nodes.shape[0], edges.shape[0]
    return pl.pallas_call(
        functools.partial(message_kernel, groups, pieces),
        out_shape=(
            jax.ShapeDtypeStruct((count, LANES), F32),
            jax.ShapeDtypeStruct((doms, own_size, LANES), BF16),
        ),
        in_specs=[SMEM] * 4 + [VMEM] * 5,
        out_specs=(VMEM, VMEM),
        scratch_shapes=[
            pltpu.VMEM((4, doms, size, LANES), BF16),
            pltpu.VMEM(nodes.shape, F32),
            pltpu.VMEM((doms * own_size, LANES), F32),
            pltpu.VMEM((doms, size, LANES), BF16),
            pltpu.VMEM((near + 4 * doms * size, LANES), F32),
            pltpu.VMEM((near, LANES), F32),
            pltpu.VMEM((count, LANES), F32),
        ]
        + exchange_sems(doms)
        + relay_sems(pieces),
        compiler_params=comm_params(0),
        name="message_stage",
    )(halo, pool_send, senders, receivers, nodes, edges, w_in, w_out, gain)


def child_counts(all_dest, first, counts, step=128):
    lines, width = all_dest.shape

    def rows(at):
        target = lax.broadcasted_iota(jnp.int32, (step, width), 0) + (first + at)

        def line(i, total):
            for j in range(4):
                hit = all_dest[pl.ds(i * 4 + j, 1), :] == target
                total = total + jnp.where(hit, 1.0, 0.0)
            return total

        total = lax.fori_loop(0, lines // 4, line, jnp.zeros((step, width), F32))
        counts[pl.ds(at, step), :] = jnp.broadcast_to(jnp.sum(total, axis=1, keepdims=True), (step, LANES))

    row_loop(counts.shape[0], step, rows)


def one_hot(index, first, rows):
    at = lax.broadcasted_iota(jnp.int32, (rows, index.shape[1]), 0) + first
    return jnp.where(at == index, 1.0, 0.0).astype(BF16)


def main_kernel(
    groups, pieces, halo, dest, senders, receivers, place, all_dest, group_dest, line_receivers,
    part_there, nodes_there, edges, edge_in, edge_out, node_in, node_out, edge_gain, node_gain,
    coarse_out, fine_out,
    table, fine_wide, part, nodes, load_sems, hop, passed, near, mid, arrived, counts, pooled, coarse_part, coarse_hop, coarse_passed, coarse_near,
    coarse_in, ghosts, wide, rows, border, table_s, table_r, msg, send, land,
    f0, f1, p0, p1, e0, e1, a0, a1, b0, b1, g0, g1, h0, h1, i0, i1, i2, j0, j1, j2, k0, k1, k2,
):
    doms, size = mid.shape[0], mid.shape[1]
    quarter, border_size = coarse_in.shape[1], ghosts.shape[2]
    coarse_rows, count = 4 * quarter, edges.shape[0]
    net = Net(doms, groups)
    load_part = pltpu.make_async_copy(part_there, part, load_sems.at[0])
    load_nodes = pltpu.make_async_copy(nodes_there, nodes, load_sems.at[1])
    load_part.start()
    load_nodes.start()
    net.greet()
    premultiply(edges, edge_in[1, 2 * LANES :, :], msg)
    child_counts(all_dest, net.e * quarter, counts)
    pooled[...] = jnp.zeros_like(pooled)
    load_part.wait()
    load_nodes.wait()
    net.meet()

    reduce = Reduce(net, part, hop, passed, near, (f0, f1), groups // 2)
    pool = Exchange(
        net, net.behind,
        lambda t, peer: mid.at[t * net.per + lax.rem(peer, net.per)],
        lambda t: arrived.at[net.me],
        lambda t, l: arrived.at[net.ahead(t) + l],
        (i0, i1, i2),
    )
    span = net.per * size

    def use(c):
        units = (groups // 2 + c, c)
        for u in units:
            own = nodes[u * net.per : (u + 1) * net.per].reshape(span, LANES)
            result = node_mlp(own, reduce.value(pl.ds(u * span, span)), node_in[0], node_out[0], node_gain[0:1, :])
            mid[u * net.per : (u + 1) * net.per] = result.reshape(net.per, size, LANES)
        if c == 0:
            pool.own().start()
        for u in units:
            pool.send(u)

    reduce.run(use)

    def gathered(k, carry):
        c = groups // 2 - 1 - k // 2
        t = c + (1 - lax.rem(k, 2)) * (groups // 2)
        pool.receive(t)

        @pl.when(t == 0)
        def _():
            pool.own().wait()

        first = net.ahead(t)
        block = arrived[pl.ds(first, net.per)].reshape(span, LANES)
        index = group_dest[pl.ds(first // net.per, 1), :]
        for q in range(4):
            at = pl.ds(q * quarter, quarter)
            pooled[at, :] = pooled[at, :] + dot(one_hot(index, q * quarter, quarter), block)
        return carry

    lax.fori_loop(0, groups, gathered, 0)
    for owner in (net.opp, net.right, net.left, net.e):
        at = pl.ds(pl.multiple_of(owner * quarter, quarter), quarter)
        coarse_part[owner] = pooled[at, :].astype(BF16)
    pool.loop(lambda t: pool.each(t, lambda i: pool.copy(t, i).wait_send()))

    def spread(values):
        def got(owner, s):
            wide[pl.ds(pl.multiple_of(owner * quarter, quarter), quarter), :] = values[owner].astype(F32)

        return got

    reduce = Reduce(net, coarse_part, coarse_hop, coarse_passed, coarse_near, (p0, p1), p0.shape[1])
    reduce.run()
    mean = reduce.value(pl.ds(0, quarter)) / jnp.maximum(counts[...], 1.0)
    coarse_in[net.e] = mean.astype(BF16)
    Relay(net, coarse_in, (g0, g1), [quarter]).run(got=spread(coarse_in))
    gather_blocks(halo, lambda k: k, wide, rows, border, (0, doms))
    here = ghosts.at[net.e]
    exchange = Exchange(
        net, net.ahead,
        lambda t, peer: border.at[peer],
        lambda t: here.at[t * net.per + net.local],
        lambda t, l: here.at[t * net.per + l],
        (j0, j1, j2),
    )
    exchange.own().start()
    exchange.loop(exchange.send)
    w = edge_in[1]
    for q in range(4):
        table_r[pl.ds(q * quarter, quarter), :] = dot(coarse_in[q], w[LANES : 2 * LANES, :])
        table_s[pl.ds(q * quarter, quarter), :] = dot(coarse_in[q], w[0:LANES, :])

    def gather_near(at):
        for j in range(32):
            msg[pl.ds(at + j, 1), :] = msg[pl.ds(at + j, 1), :] + table_r[pl.ds(receivers[at + j], 1), :]

    row_loop(count, 32, gather_near)

    def ready(s):
        def run(t, carry):
            exchange.receive(t)
            return carry

        lax.fori_loop(s * (groups // 2), (s + 1) * (groups // 2), run, 0)
        if s == 0:
            exchange.own().wait()

    Relay(net, ghosts, (h0, h1), [doms // 2] * 2).run(ready)
    exchange.loop(lambda t: exchange.each(t, lambda i: exchange.copy(t, i).wait_send()))
    for owner in range(4):
        block = ghosts[owner].reshape(doms * border_size, LANES)
        at = pl.ds(coarse_rows + owner * doms * border_size, doms * border_size)
        table_s[at, :] = dot(block, w[0:LANES, :])

    def gather_far(at):
        for j in range(32):
            msg[pl.ds(at + j, 1), :] = msg[pl.ds(at + j, 1), :] + table_s[pl.ds(senders[at + j], 1), :]

    row_loop(count, 32, gather_far)
    edge_mlp(msg, edge_out[1], edge_gain[1:2, :], msg)
    high = msg[...].astype(BF16)
    low = (msg[...] - high.astype(F32)).astype(BF16)
    both = jnp.concatenate([high, low], axis=1)
    for owner in (net.opp, net.right, net.left, net.e):
        sums = dot(one_hot(line_receivers[...], owner * quarter, quarter), both)
        coarse_part[owner] = (sums[:, 0:LANES] + sums[:, LANES:]).astype(BF16)

    reduce = Reduce(net, coarse_part, coarse_hop, coarse_passed, coarse_near, (e0, e1), e0.shape[1])
    reduce.run()
    coarse_out[net.e] = node_mlp(
        coarse_in[net.e], reduce.value(pl.ds(0, quarter)), node_in[1], node_out[1], node_gain[1:2, :]
    )
    wide[pl.ds(coarse_rows, 8), :] = jnp.zeros((8, LANES), F32)
    Relay(net, coarse_out, (a0, a1), [quarter]).run(got=spread(coarse_out))
    back = Exchange(
        net, net.ahead,
        lambda t, peer: send.at[peer],
        lambda t: land.at[t * net.per + net.local],
        lambda t, l: land.at[t * net.per + l],
        (k0, k1, k2),
    )

    def start(t):
        gather_blocks(dest, lambda k: k, wide, rows, send, (net.ahead(t), net.per))
        back.send(t)

    back.loop(start)
    back.own().start()
    ends = [sum(pieces[:s]) for s in range(len(pieces) + 1)]

    def ready(s):
        def run(t, carry):
            back.receive(t)
            return carry

        lax.fori_loop(ends[s], ends[s + 1], run, 0)
        if s == 0:
            back.own().wait()
        block = slice(ends[s] * net.per, ends[s + 1] * net.per)
        table[net.e, block] = (land[block].astype(F32) + mid[block].astype(F32)).astype(BF16)

    relay = Relay(net, table, (b0, b1), [p * net.per for p in pieces])

    def got(owner, s):
        first, count = relay.range(s)
        at = pl.multiple_of(owner * (doms * size) + first * size, 16)
        block = table[owner, pl.ds(first, count)].reshape(count * size, LANES)
        fine_wide[pl.ds(at, count * size), :] = block.astype(F32)

    relay.run(ready, got=got)

    def pick(at):
        for half in (0, 64):
            for j in range(half, half + 64):
                rows[pl.ds(j, 1), :] = fine_wide[pl.ds(place[at + j], 1), :]
            fine_out[pl.ds(at + half, 64), :] = rows[half : half + 64, :].astype(BF16)

    row_loop(fine_out.shape[0], 128, pick)
    back.loop(lambda t: back.each(t, lambda i: back.copy(t, i).wait_send()))


def main_stage(groups, coarse_rows, ints, part, nodes, edges, weights, fine_rows, pieces=(2, 2, 2, 1, 1)):
    doms, size, _ = nodes.shape
    quarter = coarse_rows // 4
    border_size, count = ints[0].shape[1], edges.shape[0]
    vmem = pltpu.VMEM
    return pl.pallas_call(
        functools.partial(main_kernel, groups, pieces),
        out_shape=(
            jax.ShapeDtypeStruct((4, quarter, LANES), BF16),
            jax.ShapeDtypeStruct((fine_rows, LANES), BF16),
        ),
        in_specs=[SMEM] * 5 + [VMEM] * 3 + [ANY] * 2 + [VMEM] * 7,
        out_specs=(VMEM, VMEM),
        scratch_shapes=[
            vmem((4,) + nodes.shape, BF16),
            vmem((4 * doms * size, LANES), F32),
            vmem(part.shape, BF16),
            vmem(nodes.shape, BF16),
            pltpu.SemaphoreType.DMA((2,)),
        ]
        + reduce_scratch(part.shape[1], 1)[:3]
        + [
            vmem(nodes.shape, BF16),
            vmem(nodes.shape, BF16),
            vmem((quarter, LANES), F32),
            vmem((coarse_rows, LANES), F32),
            vmem((4, quarter, LANES), BF16),
        ]
        + reduce_scratch(quarter, 1)[:3]
        + [
            vmem((4, quarter, LANES), BF16),
            vmem((4, doms, border_size, LANES), BF16),
            vmem((coarse_rows + 8, LANES), F32),
            vmem((doms * size, LANES), F32),
            vmem((doms, border_size, LANES), BF16),
            vmem((coarse_rows + 4 * doms * border_size, LANES), F32),
            vmem((coarse_rows, LANES), F32),
            vmem((count, LANES), F32),
            vmem(nodes.shape, BF16),
            vmem(nodes.shape, BF16),
        ]
        + reduce_scratch(quarter, groups // 2)[3:]
        + reduce_scratch(quarter, 2)[3:]
        + reduce_scratch(quarter, 2)[3:]
        + relay_sems(1)
        + relay_sems(len(pieces))
        + relay_sems(1)
        + relay_sems(2)
        + exchange_sems(doms)
        + exchange_sems(doms)
        + exchange_sems(doms),
        compiler_params=comm_params(1),
        name="main_stage",
    )(*ints, part, nodes, edges, *weights)


def shards(groups, coarse_rows, *args):
    (
        fine_nodes, fine_edges, fine_senders, fine_receivers, fine_halo,
        coarse_edges, coarse_senders, coarse_receivers, coarse_halo,
        pool_send, pool_dest, unpool_slot,
        edge_in_weight, edge_out_weight, node_in_weight, node_out_weight, edge_gain, node_gain,
    ) = args
    e = lax.axis_index("edge")
    doms = fine_halo.shape[1]
    slots = pool_dest.shape[2]

    def quarter(lists):
        size = lists.shape[2] // 4
        return lax.dynamic_slice_in_dim(lists[0], e * size, size, axis=1)

    own, dest = quarter(pool_send), quarter(pool_dest)
    group_dest = dest.reshape(groups, -1)
    widths = (doms, fine_nodes.shape[0], fine_halo.shape[2], coarse_rows, coarse_halo.shape[2], slots)
    senders, far_senders, place = place_stage(groups, widths, fine_senders, coarse_senders, unpool_slot)

    msg, own_nodes = message_stage(
        doms, groups, quarter(fine_halo), own, senders, fine_receivers,
        fine_nodes, fine_edges, edge_in_weight, edge_out_weight, edge_gain,
    )
    part = sum_stage(fine_receivers, place, msg, doms * slots)
    ints = (
        quarter(coarse_halo), dest, far_senders, coarse_receivers, place,
        pool_dest[0], group_dest, coarse_receivers.reshape(1, -1),
    )
    weights = (edge_in_weight, edge_out_weight, node_in_weight, node_out_weight, edge_gain, node_gain)
    coarse_out, fine_out = main_stage(
        groups, coarse_rows, ints, part.reshape(4, -1, LANES), own_nodes, coarse_edges, weights, fine_nodes.shape[0]
    )
    return fine_out, coarse_out.reshape(-1, LANES)


def solution(mesh, groups=8, coarse_rows=2048):
    placed = (
        P("dom", None),
        P(("dom", "edge"), None),
        P(("dom", "edge")),
        P(("dom", "edge")),
        P("dom", None, None),
        P(("dom", "edge"), None),
        P(("dom", "edge")),
        P(("dom", "edge")),
        P("dom", None, None),
        P("dom", None, None),
        P("dom", None, None),
        P("dom"),
        P(),
        P(),
        P(),
        P(),
        P(),
        P(),
    )
    return jax.shard_map(
        functools.partial(shards, groups, coarse_rows),
        mesh=mesh,
        in_specs=placed,
        out_specs=(P("dom", None), P("dom", None)),
        check_vma=False,
    )
```

```python
import functools

import jax
import jax.numpy as jnp
from jax import lax
from jax.experimental import pallas as pl
from jax.experimental.pallas import tpu as pltpu
from jax.sharding import PartitionSpec as P

F32, BF16 = jnp.float32, jnp.bfloat16
VMEM = pl.BlockSpec(memory_space=pltpu.VMEM)
SMEM = pl.BlockSpec(memory_space=pltpu.SMEM)
ANY = pl.BlockSpec(memory_space=pl.ANY)
LANES = 128


def silu(v):
    return v / (1.0 + jnp.exp(-v))


def normed(v, gain):
    center = v - jnp.mean(v, axis=-1, keepdims=True)
    spread = jnp.mean(center * center, axis=-1, keepdims=True)
    return center * lax.rsqrt(spread + 1e-05) * gain


def dot(a, b):
    return jnp.dot(a, b, preferred_element_type=F32)


def node_mlp(rows, summed, w_in, w_out, gain):
    pre = dot(rows, w_in[0:LANES, :]) + dot(summed.astype(BF16), w_in[LANES : 2 * LANES, :])
    hidden = silu(pre).astype(BF16)
    return (rows.astype(F32) + normed(dot(hidden, w_out), gain)).astype(BF16)


def row_loop(total, step, body):
    def run(i, carry):
        body(pl.multiple_of(i * step, step))
        return carry

    lax.fori_loop(0, total // step, run, 0)


def widen(src, dst, step=512):
    def body(at):
        dst[pl.ds(at, step), :] = src[pl.ds(at, step), :].astype(F32)

    row_loop(src.shape[0], step, body)


def clear_all(accs, step=512):
    def body(at):
        for acc in accs:
            acc[pl.ds(at, step), :] = jnp.zeros((step, LANES), F32)

    row_loop(accs[0].shape[0] // step * step, step, body)


def add_rows(where, values, count, accs, unroll=32):
    def body(at):
        for j in range(unroll):
            acc, row = accs[j % len(accs)], where(at + j)
            acc[pl.ds(row, 1), :] = acc[pl.ds(row, 1), :] + values[pl.ds(at + j, 1), :]

    row_loop(count, unroll, body)


def sum_accs(accs, out, step=512):
    def body(at):
        value = accs[0][pl.ds(at, step), :]
        for acc in accs[1:]:
            value = value + acc[pl.ds(at, step), :]
        out[pl.ds(at, step), :] = value.astype(BF16)

    row_loop(out.shape[0], step, body)


def premultiply(rows, weight, dst, base=0, step=512):
    def body(at):
        dst[pl.ds(pl.multiple_of(base + at, step), step), :] = dot(rows[pl.ds(at, step), :], weight)

    row_loop(rows.shape[0], step, body)


def edge_mlp(msg, w_out, gain, out, step=512):
    def body(at):
        hidden = silu(msg[pl.ds(at, step), :]).astype(BF16)
        out[pl.ds(at, step), :] = normed(dot(hidden, w_out), gain)

    row_loop(msg.shape[0], step, body)


def sum_kernel(receivers, place, msg, out, held, total, sem_in, sem_out, *accs):
    load = pltpu.make_async_copy(msg, held, sem_in)
    load.start()
    clear_all(accs)
    load.wait()
    add_rows(lambda j: place[receivers[j]], held, held.shape[0], accs)
    size = out.shape[0] // 4

    def store(q):
        at = pl.ds(q * size, size)
        return pltpu.make_async_copy(total.at[at], out.at[at], sem_out.at[q])

    for q in range(4):
        at = pl.ds(q * size, size)
        sum_accs([acc.at[at] for acc in accs], total.at[at])
        store(q).start()
    for q in range(4):
        store(q).wait()


def sum_stage(receivers, place, msg, slots):
    return pl.pallas_call(
        sum_kernel,
        out_shape=jax.ShapeDtypeStruct((slots, LANES), BF16),
        in_specs=[SMEM, SMEM, ANY],
        out_specs=ANY,
        scratch_shapes=[
            pltpu.VMEM(msg.shape, F32),
            pltpu.VMEM((slots, LANES), BF16),
            pltpu.SemaphoreType.DMA,
            pltpu.SemaphoreType.DMA((4,)),
        ]
        + [pltpu.VMEM((slots, LANES), F32)] * 3,
        name="sum_stage",
    )(receivers, place, msg)


def place_kernel(groups, widths, senders, far_senders, slots, lists, out, far_out, place, cuts):
    me = lax.axis_index("dom")
    doms, rows, width, coarse_rows, coarse_width, slot_count = widths
    per = doms // groups

    def over(value, divisor):
        shift = (divisor & -divisor).bit_length() - 1
        left = divisor >> shift
        value = lax.shift_right_logical(value, shift)
        if left == 1:
            return value
        return lax.shift_right_logical(value * ((1 << 16) // left + 1), 16)

    def split(value, divisor):
        high = over(value, divisor)
        return high, value - high * divisor

    def nearby(p):
        group, local = split(p, per)
        away = me // per + groups - group
        away = jnp.where(away >= groups, away - groups, away)
        step = jnp.where(2 * away <= groups, jnp.maximum(2 * away - 1, 0), 2 * (groups - away))
        return step * per + local

    def moved(value, near, wide):
        size = wide // 4
        owner, slot = split(jnp.maximum(value - near, 0), wide)
        quarter, inner = split(slot, size)
        there = near + quarter * (doms * size) + nearby(owner) * size + inner
        return jnp.where(value < near, value, there)

    out[...] = moved(senders[...], rows, width)
    far_out[...] = moved(far_senders[...], coarse_rows, coarse_width)
    owner, slot = split(slots[...], slot_count)
    size = slot_count // 4
    quarter, inner = split(slot, size)
    place[...] = quarter * (doms * size) + nearby(owner) * size + inner

    e = lax.axis_index("edge")
    for whole, cut in zip(lists, cuts):
        axis = 0 if whole.shape[0] != cut.shape[0] else 1
        size = cut.shape[axis]
        pieces = [whole[q * size : (q + 1) * size] if axis == 0 else whole[:, q * size : (q + 1) * size] for q in range(4)]
        value = pieces[3]
        for q in range(3):
            value = jnp.where(e == q, pieces[q], value)
        cut[...] = value


def place_stage(groups, widths, ints, lists):
    shaped = [x.reshape(-1, LANES) for x in ints]
    cut_shapes = [
        tuple(n // 4 if i == axis else n for i, n in enumerate(whole.shape)) for whole, axis in lists
    ]
    shapes = [x.shape for x in shaped] + cut_shapes

    def kernel(*refs):
        k = 3 + len(lists)
        place_kernel(groups, widths, *refs[0:3], refs[3:k], *refs[k : k + 3], refs[k + 3 :])

    results = pl.pallas_call(
        kernel,
        out_shape=[jax.ShapeDtypeStruct(s, jnp.int32) for s in shapes],
        in_specs=[VMEM] * len(shapes),
        out_specs=[VMEM] * len(shapes),
        name="place_stage",
    )(*shaped, *(whole for whole, _ in lists))
    return [x.reshape(-1) for x in results[:3]] + list(results[3:])


class Net:
    def __init__(self, doms, groups):
        self.doms, self.groups, self.per = doms, groups, doms // groups
        self.me = lax.axis_index("dom")
        self.e = lax.axis_index("edge")
        self.group = self.me // self.per
        self.local = lax.rem(self.me, self.per)
        self.right = lax.rem(self.e + 1, 4)
        self.left = lax.rem(self.e + 3, 4)
        self.opp = lax.rem(self.e + 2, 4)

    def greet(self):
        sem = pltpu.get_barrier_semaphore()
        pl.semaphore_signal(sem, 1, device_id={"edge": self.right})
        pl.semaphore_signal(sem, 1, device_id={"edge": self.left})

        def signal(k, carry):
            pl.semaphore_signal(sem, 1, device_id={"dom": lax.rem(self.me + k, self.doms)})
            return carry

        lax.fori_loop(1, self.doms, signal, 0)

    def meet(self):
        pl.semaphore_wait(pltpu.get_barrier_semaphore(), self.doms + 1)

    def offset(self, t):
        odd = lax.rem(t, 2)
        return odd * ((t + 1) // 2) + (1 - odd) * lax.rem(self.groups - t // 2, self.groups)

    def ahead(self, t):
        return lax.rem(self.group + self.offset(t), self.groups) * self.per

    def behind(self, t):
        return lax.rem(self.group + self.groups - self.offset(t), self.groups) * self.per


class Exchange:
    def __init__(self, net, first, source, target, landed, sems):
        self.net, self.first, self.source, self.target, self.landed = net, first, source, target, landed
        self.send_sem, self.recv_sem, self.own_sem = sems

    def copy(self, t, i):
        net = self.net
        local = lax.rem(net.local + i, net.per)
        peer = self.first(t) + local
        return pltpu.make_async_remote_copy(
            src_ref=self.source(t, peer),
            dst_ref=self.target(t),
            send_sem=self.send_sem.at[t * net.per + local],
            recv_sem=self.recv_sem.at[t * net.per + net.local],
            device_id={"dom": peer},
        )

    def own(self):
        return pltpu.make_async_copy(self.source(0, self.net.me), self.target(0), self.own_sem)

    def each(self, t, body):
        def run(i, carry):
            body(i)
            return carry

        lax.fori_loop(jnp.where(t == 0, 1, 0), self.net.per, run, 0)

    def send(self, t):
        self.each(t, lambda i: self.copy(t, i).start())

    def receive(self, t):
        net = self.net

        def wait(i):
            local = lax.rem(net.local + i, net.per)
            pltpu.make_async_remote_copy(
                src_ref=self.landed(t, local),
                dst_ref=self.landed(t, local),
                send_sem=self.send_sem.at[t * net.per + local],
                recv_sem=self.recv_sem.at[t * net.per + local],
                device_id={"dom": self.first(t) + local},
            ).wait_recv()

        self.each(t, wait)

    def loop(self, body):
        def run(t, carry):
            body(t)
            return carry

        lax.fori_loop(0, self.net.groups, run, 0)

    def finish(self):
        self.own().wait()
        self.loop(lambda t: self.each(t, lambda i: self.copy(t, i).wait_send()))


def exchange_sems(doms):
    return [pltpu.SemaphoreType.DMA((doms,)), pltpu.SemaphoreType.DMA((doms,)), pltpu.SemaphoreType.DMA]


def edge_copy(src, dst, sems, which, slot, to):
    return pltpu.make_async_remote_copy(
        src_ref=src,
        dst_ref=dst,
        send_sem=sems[0].at[which, slot],
        recv_sem=sems[1].at[which, slot],
        device_id={"edge": to},
    )


class Relay:
    def __init__(self, net, out, sems, sizes):
        self.net, self.out, self.sems, self.sizes = net, out, sems, sizes
        self.pieces = len(sizes)

    def range(self, s):
        return sum(self.sizes[:s]), self.sizes[s]

    def copy(self, which, owner, s, half, to):
        first, size = self.range(s)
        if half is None:
            at = pl.ds(first, size)
        else:
            at = pl.ds(first + half * (size // 2), size // 2)
        piece = self.out.at[owner, at]
        return edge_copy(piece, piece, self.sems, which, s, to)

    def first(self, s):
        n = self.net
        self.copy(0, n.e, s, None, n.right).start()
        self.copy(1, n.e, s, None, n.left).start()

    def second(self, s):
        n = self.net
        self.copy(0, n.left, s, None, n.right).wait_recv()
        self.copy(2, n.left, s, 0, n.right).start()
        self.copy(1, n.right, s, None, n.left).wait_recv()
        self.copy(3, n.right, s, 1, n.left).start()

    def finish(self, s):
        n = self.net
        self.copy(2, n.opp, s, 0, n.right).wait_recv()
        self.copy(3, n.opp, s, 1, n.left).wait_recv()
        self.copy(0, n.e, s, None, n.right).wait_send()
        self.copy(1, n.e, s, None, n.left).wait_send()
        self.copy(2, n.left, s, 0, n.right).wait_send()
        self.copy(3, n.right, s, 1, n.left).wait_send()

    def rest(self, got):
        n = self.net
        for s in reversed(range(self.pieces)):
            got(n.e, s)
            self.second(s)
        for s in reversed(range(self.pieces)):
            got(n.left, s)
            got(n.right, s)
        for s in reversed(range(self.pieces)):
            self.finish(s)
            got(n.opp, s)

    def run(self, ready=lambda s: None, work=lambda s: None, got=lambda owner, s: None):
        n, last = self.net, self.pieces - 1
        for s in range(self.pieces + 1):
            if s <= last:
                ready(s)
                self.first(s)
            if s:
                self.second(s - 1)
            work(s)
            if s <= last:
                got(n.e, s)
            if s:
                got(n.left, s - 1)
                got(n.right, s - 1)
        for s in range(self.pieces):
            self.finish(s)
            got(n.opp, s)


def relay_sems(pieces):
    return [pltpu.SemaphoreType.DMA((4, pieces)), pltpu.SemaphoreType.DMA((4, pieces))]


class Reduce:
    def __init__(self, net, part, hop, passed, near, sems, chunks):
        self.net, self.part, self.hop, self.passed, self.near = net, part, hop, passed, near
        self.sems, self.chunks = sems, chunks
        self.half = part.shape[1] // 2
        self.size = self.half // chunks

    def h(self, c):
        return pl.ds(c * self.size, self.size)

    def a(self, c):
        return pl.ds(2 * c * self.size, self.size)

    def b(self, c):
        return pl.ds((2 * c + 1) * self.size, self.size)

    def hop_right(self, c):
        return edge_copy(self.part.at[self.net.opp, self.a(c)], self.hop.at[0, self.h(c)], self.sems, 0, c, self.net.right)

    def hop_left(self, c):
        return edge_copy(self.part.at[self.net.opp, self.b(c)], self.hop.at[1, self.h(c)], self.sems, 1, c, self.net.left)

    def raw_right(self, c):
        return edge_copy(self.part.at[self.net.right, self.b(c)], self.near.at[0, self.b(c)], self.sems, 2, c, self.net.right)

    def raw_left(self, c):
        return edge_copy(self.part.at[self.net.left, self.a(c)], self.near.at[1, self.a(c)], self.sems, 3, c, self.net.left)

    def sum_right(self, c):
        return edge_copy(self.passed.at[0, self.h(c)], self.near.at[0, self.a(c)], self.sems, 4, c, self.net.right)

    def sum_left(self, c):
        return edge_copy(self.passed.at[1, self.h(c)], self.near.at[1, self.b(c)], self.sems, 5, c, self.net.left)

    def loop(self, body):
        def run(c, carry):
            body(c)
            return carry

        lax.fori_loop(0, self.chunks, run, 0)

    def start(self, c):
        self.hop_right(c).start()
        self.hop_left(c).start()
        self.raw_right(c).start()
        self.raw_left(c).start()

    def through(self, c):
        net = self.net
        self.hop_right(c).wait_recv()
        self.passed[0, self.h(c)] = (
            self.hop[0, self.h(c)].astype(F32) + self.part[net.right, self.a(c)].astype(F32)
        ).astype(BF16)
        self.hop_left(c).wait_recv()
        self.passed[1, self.h(c)] = (
            self.hop[1, self.h(c)].astype(F32) + self.part[net.left, self.b(c)].astype(F32)
        ).astype(BF16)
        self.hop_right(c).wait_send()
        self.hop_left(c).wait_send()
        self.sum_right(c).start()
        self.sum_left(c).start()

    def finish(self, c):
        for copy in (self.raw_right(c), self.raw_left(c), self.sum_right(c), self.sum_left(c)):
            copy.wait()

    def run(self, use=lambda c: None, aside=lambda: None):
        order = list(reversed(range(self.chunks)))
        self.start(order[0])
        for k, c in enumerate(order):
            if k + 1 < self.chunks:
                self.start(order[k + 1])
            if k == 0:
                aside()
            self.through(c)
            if k:
                self.finish(order[k - 1])
                use(order[k - 1])
        self.finish(order[-1])
        use(order[-1])

    def value(self, rows):
        return (
            self.part[self.net.e, rows].astype(F32)
            + self.near[0, rows].astype(F32)
            + self.near[1, rows].astype(F32)
        )


def reduce_scratch(rows, chunks):
    return [
        pltpu.VMEM((2, rows // 2, LANES), BF16),
        pltpu.VMEM((2, rows // 2, LANES), BF16),
        pltpu.VMEM((2, rows, LANES), BF16),
        pltpu.SemaphoreType.DMA((6, chunks)),
        pltpu.SemaphoreType.DMA((6, chunks)),
    ]


def gather_blocks(index, base, table, rows, dst, blocks, turned=False):
    size = dst.shape[1]

    def body(i, carry):
        k = blocks[0] + i
        line, at = base(k), pl.multiple_of(k * size, size)
        for j in range(size):
            rows[pl.ds(at + j, 1), :] = table[pl.ds(index[j, line] if turned else index[line, j], 1), :]
        dst[k] = rows[pl.ds(at, size), :].astype(BF16)
        return carry

    lax.fori_loop(0, blocks[1], body, 0)


def message_kernel(
    groups, pieces, halo, senders, receivers, nodes, edges, w_in, w_out, gain,
    out, ghosts, wide, rows, send, from_rows, to_rows, s0, s1, s2, r0, r1,
):
    doms, size = ghosts.shape[1], ghosts.shape[2]
    count, near = edges.shape[0], nodes.shape[0]
    net = Net(doms, groups)
    net.greet()
    widen(nodes, wide)
    gather_blocks(halo, lambda k: k, wide, rows, send, (0, doms))
    net.meet()
    land = ghosts.at[net.e]
    exchange = Exchange(
        net, net.ahead,
        lambda t, peer: send.at[peer],
        lambda t: land.at[t * net.per + net.local],
        lambda t, l: land.at[t * net.per + l],
        (s0, s1, s2),
    )
    exchange.own().start()
    exchange.loop(exchange.send)

    def pick(index, dst):
        def body(at):
            for j in range(64):
                dst[pl.ds(at + j, 1), :] = wide[pl.ds(index[at + j], 1), :]

        row_loop(count, 64, body)

    pick(receivers, to_rows)
    w = w_in[0]

    def known(at):
        block = pl.ds(at, 512)
        to_rows[block, :] = dot(to_rows[block, :].astype(BF16), w[LANES : 2 * LANES, :]) + dot(
            edges[block, :], w[2 * LANES :, :]
        )

    each = groups // pieces

    def ready(s):
        def run(t, carry):
            exchange.receive(t)
            return carry

        lax.fori_loop(s * each, (s + 1) * each, run, 0)
        if s == 0:
            exchange.own().wait()

    def work(s):
        if s == 0:
            row_loop(count // 2, 512, known)
        if s == pieces:
            row_loop(count // 2, 512, lambda at: known(count // 2 + at))

    part = doms // pieces

    def got(owner, s):
        at = pl.multiple_of(near + owner * (doms * size) + s * part * size, 16)
        block = ghosts[owner, pl.ds(s * part, part)].reshape(part * size, LANES)
        wide[pl.ds(at, part * size), :] = block.astype(F32)

    Relay(net, ghosts, (r0, r1), [part] * pieces).run(ready, work, got)
    pick(senders, from_rows)

    def finish(at):
        block = pl.ds(at, 512)
        pre = dot(from_rows[block, :].astype(BF16), w[0:LANES, :]) + to_rows[block, :]
        out[block, :] = normed(dot(silu(pre).astype(BF16), w_out[0]), gain[0:1, :])

    row_loop(count, 512, finish)
    exchange.loop(lambda t: exchange.each(t, lambda i: exchange.copy(t, i).wait_send()))


def comm_params(collective_id):
    return pltpu.CompilerParams(collective_id=collective_id, has_side_effects=True)


def message_stage(doms, groups, halo, senders, receivers, nodes, edges, w_in, w_out, gain, pieces=2):
    size = halo.shape[1]
    near, count = nodes.shape[0], edges.shape[0]
    return pl.pallas_call(
        functools.partial(message_kernel, groups, pieces),
        out_shape=jax.ShapeDtypeStruct((count, LANES), F32),
        in_specs=[SMEM] * 3 + [VMEM] * 5,
        out_specs=VMEM,
        scratch_shapes=[
            pltpu.VMEM((4, doms, size, LANES), BF16),
            pltpu.VMEM((near + 4 * doms * size, LANES), F32),
            pltpu.VMEM((doms * size, LANES), F32),
            pltpu.VMEM((doms, size, LANES), BF16),
            pltpu.VMEM((count, LANES), F32),
            pltpu.VMEM((count, LANES), F32),
        ]
        + exchange_sems(doms)
        + relay_sems(pieces),
        compiler_params=comm_params(0),
        name="message_stage",
    )(halo, senders, receivers, nodes, edges, w_in, w_out, gain)


def child_counts(all_dest, first, counts, at, step):
    lines, width = all_dest.shape

    target = lax.broadcasted_iota(jnp.int32, (step, width), 0) + (first + at)

    def line(i, total):
        for j in range(4):
            hit = all_dest[pl.ds(i * 4 + j, 1), :] == target
            total = total + jnp.where(hit, 1.0, 0.0)
        return total

    total = lax.fori_loop(0, lines // 4, line, jnp.zeros((step, width), F32))
    counts[pl.ds(at, step), :] = jnp.broadcast_to(jnp.sum(total, axis=1, keepdims=True), (step, LANES))


def one_hot(index, first, rows):
    at = lax.broadcasted_iota(jnp.int32, (rows, index.shape[1]), 0) + first
    return jnp.where(at == index, 1.0, 0.0).astype(BF16)


def main_kernel(
    groups, pieces, halo, own, dest, senders, receivers, place, all_dest, group_dest, line_receivers,
    part_there, nodes_there, edges, edge_in, edge_out, node_in, node_out, edge_gain, node_gain,
    coarse_out, fine_out,
    table, fine_wide, part, fine_nodes, nodes, load_sems, hop, passed, near, mid, arrived, counts, pooled, coarse_part, coarse_hop, coarse_passed, coarse_near,
    coarse_in, ghosts, wide, rows, border, table_s, table_r, msg, send, land,
    f0, f1, p0, p1, e0, e1, a0, a1, b0, b1, g0, g1, h0, h1, i0, i1, i2, j0, j1, j2, k0, k1, k2,
):
    doms, size = mid.shape[0], mid.shape[1]
    quarter, border_size = coarse_in.shape[1], ghosts.shape[2]
    coarse_rows, count = 4 * quarter, edges.shape[0]
    net = Net(doms, groups)
    load_part = pltpu.make_async_copy(part_there, part, load_sems.at[0])
    load_nodes = pltpu.make_async_copy(nodes_there, fine_nodes, load_sems.at[1])
    load_nodes.start()
    load_part.start()
    net.greet()
    premultiply(edges, edge_in[1, 2 * LANES :, :], msg)
    load_nodes.wait()
    widen(fine_nodes, fine_wide)

    def line(k):
        return net.behind(k // net.per) + lax.rem(k, net.per)

    half = doms // 2
    gather_blocks(own, line, fine_wide, rows, nodes, (half, half))
    load_part.wait()
    net.meet()

    reduce = Reduce(net, part, hop, passed, near, (f0, f1), groups // 2)
    pool = Exchange(
        net, net.behind,
        lambda t, peer: mid.at[t * net.per + lax.rem(peer, net.per)],
        lambda t: arrived.at[net.me],
        lambda t, l: arrived.at[net.ahead(t) + l],
        (i0, i1, i2),
    )
    span = net.per * size

    def use(c):
        units = (2 * c + 1, 2 * c)
        for u in units:
            own = nodes[u * net.per : (u + 1) * net.per].reshape(span, LANES)
            result = node_mlp(own, reduce.value(pl.ds(u * span, span)), node_in[0], node_out[0], node_gain[0:1, :])
            mid[u * net.per : (u + 1) * net.per] = result.reshape(net.per, size, LANES)
        if c == 0:
            pool.own().start()
        for u in units:
            pool.send(u)
        step = 2 * quarter // groups
        child_counts(all_dest, net.e * quarter, counts, c * step, step)

    def aside():
        gather_blocks(own, line, fine_wide, rows, nodes, (0, half))
        pooled[...] = jnp.zeros_like(pooled)

    reduce.run(use, aside)

    def gathered(k, carry):
        t = groups - 1 - k
        pool.receive(t)

        @pl.when(t == 0)
        def _():
            pool.own().wait()

        first = net.ahead(t)
        block = arrived[pl.ds(first, net.per)].reshape(span, LANES)
        index = group_dest[pl.ds(first // net.per, 1), :]
        for q in range(4):
            at = pl.ds(q * quarter, quarter)
            pooled[at, :] = pooled[at, :] + dot(one_hot(index, q * quarter, quarter), block)
        return carry

    lax.fori_loop(0, groups, gathered, 0)
    for owner in (net.opp, net.right, net.left, net.e):
        at = pl.ds(pl.multiple_of(owner * quarter, quarter), quarter)
        coarse_part[owner] = pooled[at, :].astype(BF16)
    pool.loop(lambda t: pool.each(t, lambda i: pool.copy(t, i).wait_send()))

    def spread(values):
        def got(owner, s):
            at = pl.ds(pl.multiple_of(owner * quarter + s * share, share), share)
            wide[at, :] = values[owner, s * share : (s + 1) * share].astype(F32)

        return got

    reduce = Reduce(net, coarse_part, coarse_hop, coarse_passed, coarse_near, (p0, p1), p0.shape[1])
    chunks = p0.shape[1]
    share = quarter // chunks
    relay = Relay(net, coarse_in, (g0, g1), [share] * chunks)

    def mean(c):
        at = pl.ds(c * share, share)
        coarse_in[net.e, at] = (reduce.value(at) / jnp.maximum(counts[at, :], 1.0)).astype(BF16)
        relay.first(c)

    reduce.run(mean)
    relay.rest(spread(coarse_in))
    gather_blocks(halo, lambda k: k, wide, rows, border, (0, doms), True)
    here = ghosts.at[net.e]
    exchange = Exchange(
        net, net.ahead,
        lambda t, peer: border.at[peer],
        lambda t: here.at[t * net.per + net.local],
        lambda t, l: here.at[t * net.per + l],
        (j0, j1, j2),
    )
    exchange.own().start()
    exchange.loop(exchange.send)
    w = edge_in[1]
    for q in range(4):
        table_r[pl.ds(q * quarter, quarter), :] = dot(coarse_in[q], w[LANES : 2 * LANES, :])
        table_s[pl.ds(q * quarter, quarter), :] = dot(coarse_in[q], w[0:LANES, :])

    def gather_near(at):
        for j in range(32):
            msg[pl.ds(at + j, 1), :] = msg[pl.ds(at + j, 1), :] + table_r[pl.ds(receivers[at + j], 1), :]

    row_loop(count, 32, gather_near)

    def ready(s):
        def run(t, carry):
            exchange.receive(t)
            return carry

        lax.fori_loop(s * (groups // 2), (s + 1) * (groups // 2), run, 0)
        if s == 0:
            exchange.own().wait()

    Relay(net, ghosts, (h0, h1), [doms // 2] * 2).run(ready)
    exchange.loop(lambda t: exchange.each(t, lambda i: exchange.copy(t, i).wait_send()))
    for owner in range(4):
        block = ghosts[owner].reshape(doms * border_size, LANES)
        at = pl.ds(coarse_rows + owner * doms * border_size, doms * border_size)
        table_s[at, :] = dot(block, w[0:LANES, :])

    def gather_far(at):
        for j in range(32):
            msg[pl.ds(at + j, 1), :] = msg[pl.ds(at + j, 1), :] + table_s[pl.ds(senders[at + j], 1), :]

    row_loop(count, 32, gather_far)
    edge_mlp(msg, edge_out[1], edge_gain[1:2, :], msg)
    high = msg[...].astype(BF16)
    low = (msg[...] - high.astype(F32)).astype(BF16)
    both = jnp.concatenate([high, low], axis=1)
    for owner in (net.opp, net.right, net.left, net.e):
        sums = dot(one_hot(line_receivers[...], owner * quarter, quarter), both)
        coarse_part[owner] = (sums[:, 0:LANES] + sums[:, LANES:]).astype(BF16)

    reduce = Reduce(net, coarse_part, coarse_hop, coarse_passed, coarse_near, (e0, e1), e0.shape[1])
    wide[pl.ds(coarse_rows, 8), :] = jnp.zeros((8, LANES), F32)
    relay_out = Relay(net, coarse_out, (a0, a1), [share] * chunks)

    def updated(c):
        at = pl.ds(c * share, share)
        coarse_out[net.e, at] = node_mlp(
            coarse_in[net.e, at], reduce.value(at), node_in[1], node_out[1], node_gain[1:2, :]
        )
        relay_out.first(c)

    reduce.run(updated)
    relay_out.rest(spread(coarse_out))
    back = Exchange(
        net, net.ahead,
        lambda t, peer: send.at[peer],
        lambda t: land.at[t * net.per + net.local],
        lambda t, l: land.at[t * net.per + l],
        (k0, k1, k2),
    )

    def start(t):
        gather_blocks(dest, lambda k: k, wide, rows, send, (net.ahead(t), net.per))
        back.send(t)

    back.loop(start)
    back.own().start()
    ends = [sum(pieces[:s]) for s in range(len(pieces) + 1)]

    def ready(s):
        def run(t, carry):
            back.receive(t)
            return carry

        lax.fori_loop(ends[s], ends[s + 1], run, 0)
        if s == 0:
            back.own().wait()
        block = slice(ends[s] * net.per, ends[s + 1] * net.per)
        table[net.e, block] = (land[block].astype(F32) + mid[block].astype(F32)).astype(BF16)

    relay = Relay(net, table, (b0, b1), [p * net.per for p in pieces])

    def got(owner, s):
        first, count = relay.range(s)
        at = pl.multiple_of(owner * (doms * size) + first * size, 16)
        block = table[owner, pl.ds(first, count)].reshape(count * size, LANES)
        fine_wide[pl.ds(at, count * size), :] = block.astype(F32)

    relay.run(ready, got=got)

    def pick(at):
        for half in (0, 64):
            for j in range(half, half + 64):
                rows[pl.ds(j, 1), :] = fine_wide[pl.ds(place[at + j], 1), :]
            fine_out[pl.ds(at + half, 64), :] = rows[half : half + 64, :].astype(BF16)

    row_loop(fine_out.shape[0], 128, pick)
    back.loop(lambda t: back.each(t, lambda i: back.copy(t, i).wait_send()))


def main_stage(groups, coarse_rows, ints, part, fine_nodes, edges, weights, pieces=(2, 2, 2, 1, 1)):
    doms, size = ints[1].shape
    fine_rows = fine_nodes.shape[0]
    nodes = jax.ShapeDtypeStruct((doms, size, LANES), BF16)
    quarter = coarse_rows // 4
    border_size, count = ints[0].shape[0], edges.shape[0]
    vmem = pltpu.VMEM
    return pl.pallas_call(
        functools.partial(main_kernel, groups, pieces),
        out_shape=(
            jax.ShapeDtypeStruct((4, quarter, LANES), BF16),
            jax.ShapeDtypeStruct((fine_rows, LANES), BF16),
        ),
        in_specs=[SMEM] * 6 + [VMEM] * 3 + [ANY] * 2 + [VMEM] * 7,
        out_specs=(VMEM, VMEM),
        scratch_shapes=[
            vmem((4,) + nodes.shape, BF16),
            vmem((4 * doms * size, LANES), F32),
            vmem(part.shape, BF16),
            vmem(fine_nodes.shape, BF16),
            vmem(nodes.shape, BF16),
            pltpu.SemaphoreType.DMA((2,)),
        ]
        + reduce_scratch(part.shape[1], 1)[:3]
        + [
            vmem(nodes.shape, BF16),
            vmem(nodes.shape, BF16),
            vmem((quarter, LANES), F32),
            vmem((coarse_rows, LANES), F32),
            vmem((4, quarter, LANES), BF16),
        ]
        + reduce_scratch(quarter, 1)[:3]
        + [
            vmem((4, quarter, LANES), BF16),
            vmem((4, doms, border_size, LANES), BF16),
            vmem((coarse_rows + 8, LANES), F32),
            vmem((doms * size, LANES), F32),
            vmem((doms, border_size, LANES), BF16),
            vmem((coarse_rows + 4 * doms * border_size, LANES), F32),
            vmem((coarse_rows, LANES), F32),
            vmem((count, LANES), F32),
            vmem(nodes.shape, BF16),
            vmem(nodes.shape, BF16),
        ]
        + reduce_scratch(quarter, groups // 2)[3:]
        + reduce_scratch(quarter, 2)[3:]
        + reduce_scratch(quarter, 2)[3:]
        + relay_sems(2)
        + relay_sems(len(pieces))
        + relay_sems(2)
        + relay_sems(2)
        + exchange_sems(doms)
        + exchange_sems(doms)
        + exchange_sems(doms),
        compiler_params=comm_params(1),
        name="main_stage",
    )(*ints, part, fine_nodes, edges, *weights)


def shards(groups, coarse_rows, *args):
    (
        fine_nodes, fine_edges, fine_senders, fine_receivers, fine_halo,
        coarse_edges, coarse_senders, coarse_receivers, coarse_halo,
        pool_send, pool_dest, unpool_slot,
        edge_in_weight, edge_out_weight, node_in_weight, node_out_weight, edge_gain, node_gain,
    ) = args
    doms = fine_halo.shape[1]
    slots = pool_dest.shape[2]
    widths = (doms, fine_nodes.shape[0], fine_halo.shape[2], coarse_rows, coarse_halo.shape[2], slots)
    senders, far_senders, place, border, own, dest, far_border = place_stage(
        groups, widths, (fine_senders, coarse_senders, unpool_slot),
        ((fine_halo[0], 1), (pool_send[0], 1), (pool_dest[0], 1), (coarse_halo[0].T, 0)),
    )
    msg = message_stage(
        doms, groups, border, senders, fine_receivers,
        fine_nodes, fine_edges, edge_in_weight, edge_out_weight, edge_gain,
    )
    part = sum_stage(fine_receivers, place, msg, doms * slots)
    ints = (
        far_border, own, dest, far_senders, coarse_receivers, place,
        pool_dest[0], dest.reshape(groups, -1), coarse_receivers.reshape(1, -1),
    )
    weights = (edge_in_weight, edge_out_weight, node_in_weight, node_out_weight, edge_gain, node_gain)
    coarse_out, fine_out = main_stage(
        groups, coarse_rows, ints, part.reshape(4, -1, LANES), fine_nodes, coarse_edges, weights
    )
    return fine_out, coarse_out.reshape(-1, LANES)


def solution(mesh, groups=8, coarse_rows=2048):
    placed = (
        P("dom", None),
        P(("dom", "edge"), None),
        P(("dom", "edge")),
        P(("dom", "edge")),
        P("dom", None, None),
        P(("dom", "edge"), None),
        P(("dom", "edge")),
        P(("dom", "edge")),
        P("dom", None, None),
        P("dom", None, None),
        P("dom", None, None),
        P("dom"),
        P(),
        P(),
        P(),
        P(),
        P(),
        P(),
    )
    return jax.shard_map(
        functools.partial(shards, groups, coarse_rows),
        mesh=mesh,
        in_specs=placed,
        out_specs=(P("dom", None), P("dom", None)),
        check_vma=False,
    )
```

```python
import functools

import jax
import jax.numpy as jnp
from jax import lax
from jax.experimental import pallas as pl
from jax.experimental.pallas import tpu as pltpu
from jax.sharding import PartitionSpec as P

F32, BF16 = jnp.float32, jnp.bfloat16
VMEM = pl.BlockSpec(memory_space=pltpu.VMEM)
SMEM = pl.BlockSpec(memory_space=pltpu.SMEM)
ANY = pl.BlockSpec(memory_space=pl.ANY)
LANES = 128


def silu(v):
    return v / (1.0 + jnp.exp(-v))


def normed(v, gain):
    center = v - jnp.mean(v, axis=-1, keepdims=True)
    spread = jnp.mean(center * center, axis=-1, keepdims=True)
    return center * lax.rsqrt(spread + 1e-05) * gain


def dot(a, b):
    return jnp.dot(a, b, preferred_element_type=F32)


def node_mlp(rows, summed, w_in, w_out, gain):
    pre = dot(rows, w_in[0:LANES, :]) + dot(summed.astype(BF16), w_in[LANES : 2 * LANES, :])
    hidden = silu(pre).astype(BF16)
    return (rows.astype(F32) + normed(dot(hidden, w_out), gain)).astype(BF16)


def row_loop(total, step, body):
    def run(i, carry):
        body(pl.multiple_of(i * step, step))
        return carry

    lax.fori_loop(0, total // step, run, 0)


def widen(src, dst, step=512):
    def body(at):
        dst[pl.ds(at, step), :] = src[pl.ds(at, step), :].astype(F32)

    row_loop(src.shape[0], step, body)


def clear_all(accs, step=512):
    def body(at):
        for acc in accs:
            acc[pl.ds(at, step), :] = jnp.zeros((step, LANES), F32)

    row_loop(accs[0].shape[0] // step * step, step, body)


def add_rows(where, values, count, accs, unroll=32):
    def body(at):
        for j in range(unroll):
            acc, row = accs[j % len(accs)], where(at + j)
            acc[pl.ds(row, 1), :] = acc[pl.ds(row, 1), :] + values[pl.ds(at + j, 1), :]

    row_loop(count, unroll, body)


def sum_accs(accs, out, step=512):
    def body(at):
        value = accs[0][pl.ds(at, step), :]
        for acc in accs[1:]:
            value = value + acc[pl.ds(at, step), :]
        out[pl.ds(at, step), :] = value.astype(BF16)

    row_loop(out.shape[0], step, body)


def premultiply(rows, weight, dst, base=0, step=512):
    def body(at):
        dst[pl.ds(pl.multiple_of(base + at, step), step), :] = dot(rows[pl.ds(at, step), :], weight)

    row_loop(rows.shape[0], step, body)


def edge_mlp(msg, w_out, gain, out, step=512):
    def body(at):
        hidden = silu(msg[pl.ds(at, step), :]).astype(BF16)
        out[pl.ds(at, step), :] = normed(dot(hidden, w_out), gain)

    row_loop(msg.shape[0], step, body)


def sum_kernel(receivers, place, msg, out, held, total, sem_in, sem_out, *accs):
    load = pltpu.make_async_copy(msg, held, sem_in)
    load.start()
    clear_all(accs)
    load.wait()
    add_rows(lambda j: place[receivers[j]], held, held.shape[0], accs)
    size = out.shape[0] // 4

    def store(q):
        at = pl.ds(q * size, size)
        return pltpu.make_async_copy(total.at[at], out.at[at], sem_out.at[q])

    for q in range(4):
        at = pl.ds(q * size, size)
        sum_accs([acc.at[at] for acc in accs], total.at[at])
        if q:
            store(q - 1).start()
    store(3).start()
    for q in range(4):
        store(q).wait()


def sum_stage(receivers, place, msg, slots):
    return pl.pallas_call(
        sum_kernel,
        out_shape=jax.ShapeDtypeStruct((slots, LANES), BF16),
        in_specs=[SMEM, SMEM, ANY],
        out_specs=ANY,
        scratch_shapes=[
            pltpu.VMEM(msg.shape, F32),
            pltpu.VMEM((slots, LANES), BF16),
            pltpu.SemaphoreType.DMA,
            pltpu.SemaphoreType.DMA((4,)),
        ]
        + [pltpu.VMEM((slots, LANES), F32)] * 3,
        name="sum_stage",
    )(receivers, place, msg)


def place_kernel(groups, widths, senders, far_senders, slots, lists, out, far_out, place, lined, cuts):
    me = lax.axis_index("dom")
    doms, rows, width, coarse_rows, coarse_width, slot_count = widths
    per = doms // groups

    def over(value, divisor):
        shift = (divisor & -divisor).bit_length() - 1
        left = divisor >> shift
        value = lax.shift_right_logical(value, shift)
        if left == 1:
            return value
        return lax.shift_right_logical(value * ((1 << 16) // left + 1), 16)

    def split(value, divisor):
        high = over(value, divisor)
        return high, value - high * divisor

    def nearby(p):
        group, local = split(p, per)
        away = me // per + groups - group
        away = jnp.where(away >= groups, away - groups, away)
        step = jnp.where(2 * away <= groups, jnp.maximum(2 * away - 1, 0), 2 * (groups - away))
        return step * per + local

    def moved(value, near, wide):
        size = wide // 4
        owner, slot = split(jnp.maximum(value - near, 0), wide)
        quarter, inner = split(slot, size)
        there = near + quarter * (doms * size) + nearby(owner) * size + inner
        return jnp.where(value < near, value, there)

    out[...] = moved(senders[...], rows, width)
    far_out[...] = moved(far_senders[...], coarse_rows, coarse_width)
    owner, slot = split(slots[...], slot_count)
    size = slot_count // 4
    quarter, inner = split(slot, size)
    place[...] = quarter * (doms * size) + nearby(owner) * size + inner

    e = lax.axis_index("edge")
    for whole, cut in zip(lists, cuts):
        axis = 0 if whole.shape[0] != cut.shape[0] else 1
        size = cut.shape[axis]
        pieces = [whole[q * size : (q + 1) * size] if axis == 0 else whole[:, q * size : (q + 1) * size] for q in range(4)]
        value = pieces[3]
        for q in range(3):
            value = jnp.where(e == q, pieces[q], value)
        cut[...] = value
    dest = cuts[2]
    lined[...] = jnp.concatenate([dest[pl.ds(l, groups, stride=per), :] for l in range(per)], axis=1)


def place_stage(groups, widths, ints, lists):
    shaped = [x.reshape(-1, LANES) for x in ints]
    cut_shapes = [
        tuple(n // 4 if i == axis else n for i, n in enumerate(whole.shape)) for whole, axis in lists
    ]
    rows, size = cut_shapes[2]
    shapes = [x.shape for x in shaped] + [(groups, rows // groups * size)] + cut_shapes

    def kernel(*refs):
        k = 3 + len(lists)
        place_kernel(groups, widths, *refs[0:3], refs[3:k], *refs[k : k + 4], refs[k + 4 :])

    results = pl.pallas_call(
        kernel,
        out_shape=[jax.ShapeDtypeStruct(s, jnp.int32) for s in shapes],
        in_specs=[VMEM] * (3 + len(lists)),
        out_specs=[VMEM] * len(shapes),
        name="place_stage",
    )(*shaped, *(whole for whole, _ in lists))
    return [x.reshape(-1) for x in results[:3]] + list(results[3:])


class Net:
    def __init__(self, doms, groups):
        self.doms, self.groups, self.per = doms, groups, doms // groups
        self.me = lax.axis_index("dom")
        self.e = lax.axis_index("edge")
        self.group = self.me // self.per
        self.local = lax.rem(self.me, self.per)
        self.right = lax.rem(self.e + 1, 4)
        self.left = lax.rem(self.e + 3, 4)
        self.opp = lax.rem(self.e + 2, 4)

    def greet(self):
        sem = pltpu.get_barrier_semaphore()
        pl.semaphore_signal(sem, 1, device_id={"edge": self.right})
        pl.semaphore_signal(sem, 1, device_id={"edge": self.left})

        def signal(k, carry):
            pl.semaphore_signal(sem, 1, device_id={"dom": lax.rem(self.me + k, self.doms)})
            return carry

        lax.fori_loop(1, self.doms, signal, 0)

    def meet(self):
        pl.semaphore_wait(pltpu.get_barrier_semaphore(), self.doms + 1)

    def offset(self, t):
        odd = lax.rem(t, 2)
        return odd * ((t + 1) // 2) + (1 - odd) * lax.rem(self.groups - t // 2, self.groups)

    def ahead(self, t):
        return lax.rem(self.group + self.offset(t), self.groups) * self.per

    def behind(self, t):
        return lax.rem(self.group + self.groups - self.offset(t), self.groups) * self.per


class Exchange:
    def __init__(self, net, first, source, target, landed, sems):
        self.net, self.first, self.source, self.target, self.landed = net, first, source, target, landed
        self.send_sem, self.recv_sem, self.own_sem = sems

    def copy(self, t, i):
        net = self.net
        local = lax.rem(net.local + i, net.per)
        peer = self.first(t) + local
        return pltpu.make_async_remote_copy(
            src_ref=self.source(t, peer),
            dst_ref=self.target(t),
            send_sem=self.send_sem.at[t * net.per + local],
            recv_sem=self.recv_sem.at[t * net.per + net.local],
            device_id={"dom": peer},
        )

    def own(self):
        return pltpu.make_async_copy(self.source(0, self.net.me), self.target(0), self.own_sem)

    def each(self, t, body):
        def run(i, carry):
            body(i)
            return carry

        lax.fori_loop(jnp.where(t == 0, 1, 0), self.net.per, run, 0)

    def send(self, t):
        self.each(t, lambda i: self.copy(t, i).start())

    def receive(self, t):
        net = self.net

        def wait(i):
            local = lax.rem(net.local + i, net.per)
            pltpu.make_async_remote_copy(
                src_ref=self.landed(t, local),
                dst_ref=self.landed(t, local),
                send_sem=self.send_sem.at[t * net.per + local],
                recv_sem=self.recv_sem.at[t * net.per + local],
                device_id={"dom": self.first(t) + local},
            ).wait_recv()

        self.each(t, wait)

    def loop(self, body):
        def run(t, carry):
            body(t)
            return carry

        lax.fori_loop(0, self.net.groups, run, 0)

    def finish(self):
        self.own().wait()
        self.loop(lambda t: self.each(t, lambda i: self.copy(t, i).wait_send()))


def exchange_sems(doms):
    return [pltpu.SemaphoreType.DMA((doms,)), pltpu.SemaphoreType.DMA((doms,)), pltpu.SemaphoreType.DMA]


def edge_copy(src, dst, sems, which, slot, to):
    return pltpu.make_async_remote_copy(
        src_ref=src,
        dst_ref=dst,
        send_sem=sems[0].at[which, slot],
        recv_sem=sems[1].at[which, slot],
        device_id={"edge": to},
    )


class Relay:
    def __init__(self, net, out, sems, sizes):
        self.net, self.out, self.sems, self.sizes = net, out, sems, sizes
        self.pieces = len(sizes)

    def range(self, s):
        return sum(self.sizes[:s]), self.sizes[s]

    def copy(self, which, owner, s, half, to):
        first, size = self.range(s)
        if half is None:
            at = pl.ds(first, size)
        else:
            at = pl.ds(first + half * (size // 2), size // 2)
        piece = self.out.at[owner, at]
        return edge_copy(piece, piece, self.sems, which, s, to)

    def first(self, s):
        n = self.net
        self.copy(0, n.e, s, None, n.right).start()
        self.copy(1, n.e, s, None, n.left).start()

    def second(self, s):
        n = self.net
        self.copy(0, n.left, s, None, n.right).wait_recv()
        self.copy(2, n.left, s, 0, n.right).start()
        self.copy(1, n.right, s, None, n.left).wait_recv()
        self.copy(3, n.right, s, 1, n.left).start()

    def finish(self, s):
        n = self.net
        self.copy(2, n.opp, s, 0, n.right).wait_recv()
        self.copy(3, n.opp, s, 1, n.left).wait_recv()
        self.copy(0, n.e, s, None, n.right).wait_send()
        self.copy(1, n.e, s, None, n.left).wait_send()
        self.copy(2, n.left, s, 0, n.right).wait_send()
        self.copy(3, n.right, s, 1, n.left).wait_send()

    def rest(self, got):
        n = self.net
        for s in reversed(range(self.pieces)):
            got(n.e, s)
            self.second(s)
        for s in reversed(range(self.pieces)):
            got(n.left, s)
            got(n.right, s)
        for s in reversed(range(self.pieces)):
            self.finish(s)
            got(n.opp, s)

    def run(self, ready=lambda s: None, work=lambda s: None, got=lambda owner, s: None):
        n, last = self.net, self.pieces - 1
        for s in range(self.pieces + 1):
            if s <= last:
                ready(s)
                self.first(s)
            if s:
                self.second(s - 1)
            work(s)
            if s <= last:
                got(n.e, s)
            if s:
                got(n.left, s - 1)
                got(n.right, s - 1)
        for s in range(self.pieces):
            self.finish(s)
            got(n.opp, s)


def relay_sems(pieces):
    return [pltpu.SemaphoreType.DMA((4, pieces)), pltpu.SemaphoreType.DMA((4, pieces))]


class Reduce:
    def __init__(self, net, part, hop, passed, near, sems, chunks):
        self.net, self.part, self.hop, self.passed, self.near = net, part, hop, passed, near
        self.sems, self.chunks = sems, chunks
        self.half = part.shape[1] // 2
        self.size = self.half // chunks

    def h(self, c):
        return pl.ds(c * self.size, self.size)

    def a(self, c):
        return pl.ds(2 * c * self.size, self.size)

    def b(self, c):
        return pl.ds((2 * c + 1) * self.size, self.size)

    def hop_right(self, c):
        return edge_copy(self.part.at[self.net.opp, self.a(c)], self.hop.at[0, self.h(c)], self.sems, 0, c, self.net.right)

    def hop_left(self, c):
        return edge_copy(self.part.at[self.net.opp, self.b(c)], self.hop.at[1, self.h(c)], self.sems, 1, c, self.net.left)

    def raw_right(self, c):
        return edge_copy(self.part.at[self.net.right, self.b(c)], self.near.at[0, self.b(c)], self.sems, 2, c, self.net.right)

    def raw_left(self, c):
        return edge_copy(self.part.at[self.net.left, self.a(c)], self.near.at[1, self.a(c)], self.sems, 3, c, self.net.left)

    def sum_right(self, c):
        return edge_copy(self.passed.at[0, self.h(c)], self.near.at[0, self.a(c)], self.sems, 4, c, self.net.right)

    def sum_left(self, c):
        return edge_copy(self.passed.at[1, self.h(c)], self.near.at[1, self.b(c)], self.sems, 5, c, self.net.left)

    def loop(self, body):
        def run(c, carry):
            body(c)
            return carry

        lax.fori_loop(0, self.chunks, run, 0)

    def start(self, c):
        self.hop_right(c).start()
        self.hop_left(c).start()
        self.raw_right(c).start()
        self.raw_left(c).start()

    def through(self, c):
        net = self.net
        self.hop_right(c).wait_recv()
        self.passed[0, self.h(c)] = (
            self.hop[0, self.h(c)].astype(F32) + self.part[net.right, self.a(c)].astype(F32)
        ).astype(BF16)
        self.hop_left(c).wait_recv()
        self.passed[1, self.h(c)] = (
            self.hop[1, self.h(c)].astype(F32) + self.part[net.left, self.b(c)].astype(F32)
        ).astype(BF16)
        self.hop_right(c).wait_send()
        self.hop_left(c).wait_send()
        self.sum_right(c).start()
        self.sum_left(c).start()

    def finish(self, c):
        for copy in (self.raw_right(c), self.raw_left(c), self.sum_right(c), self.sum_left(c)):
            copy.wait()

    def run(self, use=lambda c: None, aside=lambda: None):
        order = list(reversed(range(self.chunks)))
        self.start(order[0])
        for k, c in enumerate(order):
            if k + 1 < self.chunks:
                self.start(order[k + 1])
            if k == 0:
                aside()
            self.through(c)
            if k:
                self.finish(order[k - 1])
                use(order[k - 1])
        self.finish(order[-1])
        use(order[-1])

    def value(self, rows):
        return (
            self.part[self.net.e, rows].astype(F32)
            + self.near[0, rows].astype(F32)
            + self.near[1, rows].astype(F32)
        )


def reduce_scratch(rows, chunks):
    return [
        pltpu.VMEM((2, rows // 2, LANES), BF16),
        pltpu.VMEM((2, rows // 2, LANES), BF16),
        pltpu.VMEM((2, rows, LANES), BF16),
        pltpu.SemaphoreType.DMA((6, chunks)),
        pltpu.SemaphoreType.DMA((6, chunks)),
    ]


def gather_blocks(index, base, table, rows, dst, blocks, turned=False):
    size = dst.shape[1]

    def body(i, carry):
        k = blocks[0] + i
        line, at = base(k), pl.multiple_of(k * size, size)
        for j in range(size):
            rows[pl.ds(at + j, 1), :] = table[pl.ds(index[j, line] if turned else index[line, j], 1), :]
        dst[k] = rows[pl.ds(at, size), :].astype(BF16)
        return carry

    lax.fori_loop(0, blocks[1], body, 0)


def message_kernel(
    groups, pieces, halo, senders, receivers, nodes, edges_there, w_in, w_out, gain,
    out, edges, load_sem, out_sem, ghosts, wide, rows, send, from_rows, to_rows, s0, s1, s2, r0, r1,
):
    doms, size = ghosts.shape[1], ghosts.shape[2]
    count, near = edges.shape[0], nodes.shape[0]
    net = Net(doms, groups)
    load = pltpu.make_async_copy(edges_there, edges, load_sem)
    load.start()
    net.greet()
    widen(nodes, wide)
    gather_blocks(halo, lambda k: k, wide, rows, send, (0, doms))
    load.wait()
    net.meet()
    land = ghosts.at[net.e]
    exchange = Exchange(
        net, net.ahead,
        lambda t, peer: send.at[peer],
        lambda t: land.at[t * net.per + net.local],
        lambda t, l: land.at[t * net.per + l],
        (s0, s1, s2),
    )
    exchange.own().start()
    exchange.loop(exchange.send)

    def pick(index, dst):
        def body(at):
            for j in range(64):
                dst[pl.ds(at + j, 1), :] = wide[pl.ds(index[at + j], 1), :]

        row_loop(count, 64, body)

    pick(receivers, to_rows)
    w = w_in[0]

    def known(at):
        block = pl.ds(at, 512)
        to_rows[block, :] = dot(to_rows[block, :].astype(BF16), w[LANES : 2 * LANES, :]) + dot(
            edges[block, :], w[2 * LANES :, :]
        )

    each = groups // pieces

    def ready(s):
        def run(t, carry):
            exchange.receive(t)
            return carry

        lax.fori_loop(s * each, (s + 1) * each, run, 0)
        if s == 0:
            exchange.own().wait()

    def work(s):
        if s == 0:
            row_loop(count // 2, 512, known)
        if s == pieces:
            row_loop(count // 2, 512, lambda at: known(count // 2 + at))

    part = doms // pieces

    def got(owner, s):
        at = pl.multiple_of(near + owner * (doms * size) + s * part * size, 16)
        block = ghosts[owner, pl.ds(s * part, part)].reshape(part * size, LANES)
        wide[pl.ds(at, part * size), :] = block.astype(F32)

    Relay(net, ghosts, (r0, r1), [part] * pieces).run(ready, work, got)
    pick(senders, from_rows)

    def store(k):
        block = pl.ds(pl.multiple_of(k * 512, 512), 512)
        return pltpu.make_async_copy(from_rows.at[block], out.at[block], out_sem.at[k])

    def finish(at):
        block = pl.ds(at, 512)
        pre = dot(from_rows[block, :].astype(BF16), w[0:LANES, :]) + to_rows[block, :]
        from_rows[block, :] = normed(dot(silu(pre).astype(BF16), w_out[0]), gain[0:1, :])

        @pl.when(at > 0)
        def _():
            store(at // 512 - 1).start()

    row_loop(count, 512, finish)
    store(count // 512 - 1).start()
    row_loop(count, 512, lambda at: store(at // 512).wait())
    exchange.loop(lambda t: exchange.each(t, lambda i: exchange.copy(t, i).wait_send()))


def comm_params(collective_id):
    return pltpu.CompilerParams(collective_id=collective_id, has_side_effects=True)


def message_stage(doms, groups, halo, senders, receivers, nodes, edges, w_in, w_out, gain, pieces=2):
    size = halo.shape[1]
    near, count = nodes.shape[0], edges.shape[0]
    return pl.pallas_call(
        functools.partial(message_kernel, groups, pieces),
        out_shape=jax.ShapeDtypeStruct((count, LANES), F32),
        in_specs=[SMEM] * 3 + [VMEM, ANY] + [VMEM] * 3,
        out_specs=ANY,
        scratch_shapes=[
            pltpu.VMEM(edges.shape, BF16),
            pltpu.SemaphoreType.DMA,
            pltpu.SemaphoreType.DMA((count // 512,)),
            pltpu.VMEM((4, doms, size, LANES), BF16),
            pltpu.VMEM((near + 4 * doms * size, LANES), F32),
            pltpu.VMEM((doms * size, LANES), F32),
            pltpu.VMEM((doms, size, LANES), BF16),
            pltpu.VMEM((count, LANES), F32),
            pltpu.VMEM((count, LANES), F32),
        ]
        + exchange_sems(doms)
        + relay_sems(pieces),
        compiler_params=comm_params(0),
        name="message_stage",
    )(halo, senders, receivers, nodes, edges, w_in, w_out, gain)


def child_counts(all_dest, first, counts, at, step):
    lines, width = all_dest.shape

    target = lax.broadcasted_iota(jnp.int32, (step, width), 0) + (first + at)

    def line(i, total):
        for j in range(4):
            hit = all_dest[pl.ds(i * 4 + j, 1), :] == target
            total = total + jnp.where(hit, 1.0, 0.0)
        return total

    total = lax.fori_loop(0, lines // 4, line, jnp.zeros((step, width), F32))
    counts[pl.ds(at, step), :] = jnp.broadcast_to(jnp.sum(total, axis=1, keepdims=True), (step, LANES))


def one_hot(index, first, rows):
    at = lax.broadcasted_iota(jnp.int32, (rows, index.shape[1]), 0) + first
    return jnp.where(at == index, 1.0, 0.0).astype(BF16)


def main_kernel(
    groups, pieces, halo, own, dest, senders, receivers, place, all_dest, group_dest, line_receivers,
    part_there, nodes_there, edges, edge_in, edge_out, node_in, node_out, edge_gain, node_gain,
    coarse_out, fine_out,
    table, fine_wide, part, fine_nodes, nodes, load_sems, hop, passed, near, mid, arrived, counts, pooled, coarse_part, coarse_hop, coarse_passed, coarse_near,
    coarse_in, ghosts, wide, rows, border, table_s, table_r, msg, send, land,
    f0, f1, p0, p1, e0, e1, a0, a1, b0, b1, g0, g1, h0, h1, i0, i1, i2, j0, j1, j2, k0, k1, k2,
):
    doms, size = mid.shape[0], mid.shape[1]
    quarter, border_size = coarse_in.shape[1], ghosts.shape[2]
    coarse_rows, count = 4 * quarter, edges.shape[0]
    net = Net(doms, groups)
    load_part = pltpu.make_async_copy(part_there, part, load_sems.at[0])
    load_nodes = pltpu.make_async_copy(nodes_there, fine_nodes, load_sems.at[1])
    load_nodes.start()
    load_part.start()
    net.greet()
    premultiply(edges, edge_in[1, 2 * LANES :, :], msg)
    load_nodes.wait()
    widen(fine_nodes, fine_wide)

    def line(k):
        return net.behind(k // net.per) + lax.rem(k, net.per)

    half = doms // 2
    gather_blocks(own, line, fine_wide, rows, nodes, (half, half))
    load_part.wait()
    net.meet()

    reduce = Reduce(net, part, hop, passed, near, (f0, f1), groups // 2)
    pool = Exchange(
        net, net.behind,
        lambda t, peer: mid.at[t * net.per + lax.rem(peer, net.per)],
        lambda t: arrived.at[net.me],
        lambda t, l: arrived.at[net.ahead(t) + l],
        (i0, i1, i2),
    )
    span = net.per * size

    def use(c):
        units = (2 * c + 1, 2 * c)
        for u in units:
            own = nodes[u * net.per : (u + 1) * net.per].reshape(span, LANES)
            result = node_mlp(own, reduce.value(pl.ds(u * span, span)), node_in[0], node_out[0], node_gain[0:1, :])
            mid[u * net.per : (u + 1) * net.per] = result.reshape(net.per, size, LANES)
        if c == 0:
            pool.own().start()
        for u in units:
            pool.send(u)
        step = 2 * quarter // groups
        child_counts(all_dest, net.e * quarter, counts, c * step, step)

    def aside():
        gather_blocks(own, line, fine_wide, rows, nodes, (0, half))
        pooled[...] = jnp.zeros_like(pooled)

    reduce.run(use, aside)

    def gathered(k, carry):
        t = groups - 1 - k
        pool.receive(t)

        @pl.when(t == 0)
        def _():
            pool.own().wait()

        first = net.ahead(t)
        block = arrived[pl.ds(first, net.per)].reshape(span, LANES)
        index = group_dest[pl.ds(first // net.per, 1), :]
        for q in range(4):
            at = pl.ds(q * quarter, quarter)
            pooled[at, :] = pooled[at, :] + dot(one_hot(index, q * quarter, quarter), block)
        return carry

    lax.fori_loop(0, groups, gathered, 0)
    for owner in (net.opp, net.right, net.left, net.e):
        at = pl.ds(pl.multiple_of(owner * quarter, quarter), quarter)
        coarse_part[owner] = pooled[at, :].astype(BF16)
    pool.loop(lambda t: pool.each(t, lambda i: pool.copy(t, i).wait_send()))

    def spread(values):
        def got(owner, s):
            at = pl.ds(pl.multiple_of(owner * quarter + s * share, share), share)
            wide[at, :] = values[owner, s * share : (s + 1) * share].astype(F32)

        return got

    reduce = Reduce(net, coarse_part, coarse_hop, coarse_passed, coarse_near, (p0, p1), p0.shape[1])
    chunks = p0.shape[1]
    share = quarter // chunks
    relay = Relay(net, coarse_in, (g0, g1), [share] * chunks)

    def mean(c):
        at = pl.ds(c * share, share)
        coarse_in[net.e, at] = (reduce.value(at) / jnp.maximum(counts[at, :], 1.0)).astype(BF16)
        relay.first(c)

    reduce.run(mean)
    relay.rest(spread(coarse_in))
    gather_blocks(halo, lambda k: k, wide, rows, border, (0, doms), True)
    here = ghosts.at[net.e]
    exchange = Exchange(
        net, net.ahead,
        lambda t, peer: border.at[peer],
        lambda t: here.at[t * net.per + net.local],
        lambda t, l: here.at[t * net.per + l],
        (j0, j1, j2),
    )
    exchange.own().start()
    exchange.loop(exchange.send)
    w = edge_in[1]
    for q in range(4):
        table_r[pl.ds(q * quarter, quarter), :] = dot(coarse_in[q], w[LANES : 2 * LANES, :])
        table_s[pl.ds(q * quarter, quarter), :] = dot(coarse_in[q], w[0:LANES, :])

    def gather_near(at):
        for j in range(32):
            msg[pl.ds(at + j, 1), :] = msg[pl.ds(at + j, 1), :] + table_r[pl.ds(receivers[at + j], 1), :]

    row_loop(count, 32, gather_near)

    def ready(s):
        def run(t, carry):
            exchange.receive(t)
            return carry

        lax.fori_loop(s * (groups // 2), (s + 1) * (groups // 2), run, 0)
        if s == 0:
            exchange.own().wait()

    Relay(net, ghosts, (h0, h1), [doms // 2] * 2).run(ready)
    exchange.loop(lambda t: exchange.each(t, lambda i: exchange.copy(t, i).wait_send()))
    for owner in range(4):
        block = ghosts[owner].reshape(doms * border_size, LANES)
        at = pl.ds(coarse_rows + owner * doms * border_size, doms * border_size)
        table_s[at, :] = dot(block, w[0:LANES, :])

    def gather_far(at):
        for j in range(32):
            msg[pl.ds(at + j, 1), :] = msg[pl.ds(at + j, 1), :] + table_s[pl.ds(senders[at + j], 1), :]

    row_loop(count, 32, gather_far)
    edge_mlp(msg, edge_out[1], edge_gain[1:2, :], msg)
    high = msg[...].astype(BF16)
    low = (msg[...] - high.astype(F32)).astype(BF16)
    both = jnp.concatenate([high, low], axis=1)
    for owner in (net.opp, net.right, net.left, net.e):
        sums = dot(one_hot(line_receivers[...], owner * quarter, quarter), both)
        coarse_part[owner] = (sums[:, 0:LANES] + sums[:, LANES:]).astype(BF16)

    reduce = Reduce(net, coarse_part, coarse_hop, coarse_passed, coarse_near, (e0, e1), e0.shape[1])
    wide[pl.ds(coarse_rows, 8), :] = jnp.zeros((8, LANES), F32)
    relay_out = Relay(net, coarse_out, (a0, a1), [share] * chunks)

    def updated(c):
        at = pl.ds(c * share, share)
        coarse_out[net.e, at] = node_mlp(
            coarse_in[net.e, at], reduce.value(at), node_in[1], node_out[1], node_gain[1:2, :]
        )
        relay_out.first(c)

    reduce.run(updated)
    relay_out.rest(spread(coarse_out))
    back = Exchange(
        net, net.ahead,
        lambda t, peer: send.at[peer],
        lambda t: land.at[t * net.per + net.local],
        lambda t, l: land.at[t * net.per + l],
        (k0, k1, k2),
    )

    def start(t):
        gather_blocks(dest, lambda k: k, wide, rows, send, (net.ahead(t), net.per))
        back.send(t)

    back.loop(start)
    back.own().start()
    ends = [sum(pieces[:s]) for s in range(len(pieces) + 1)]

    def ready(s):
        def run(t, carry):
            back.receive(t)
            return carry

        lax.fori_loop(ends[s], ends[s + 1], run, 0)
        if s == 0:
            back.own().wait()
        block = slice(ends[s] * net.per, ends[s + 1] * net.per)
        table[net.e, block] = (land[block].astype(F32) + mid[block].astype(F32)).astype(BF16)

    relay = Relay(net, table, (b0, b1), [p * net.per for p in pieces])

    def got(owner, s):
        first, count = relay.range(s)
        at = pl.multiple_of(owner * (doms * size) + first * size, 16)
        block = table[owner, pl.ds(first, count)].reshape(count * size, LANES)
        fine_wide[pl.ds(at, count * size), :] = block.astype(F32)

    relay.run(ready, got=got)

    def pick(at):
        for half in (0, 64):
            for j in range(half, half + 64):
                rows[pl.ds(j, 1), :] = fine_wide[pl.ds(place[at + j], 1), :]
            fine_out[pl.ds(at + half, 64), :] = rows[half : half + 64, :].astype(BF16)

    row_loop(fine_out.shape[0], 128, pick)
    back.loop(lambda t: back.each(t, lambda i: back.copy(t, i).wait_send()))


def main_stage(groups, coarse_rows, ints, part, fine_nodes, edges, weights, pieces=(2, 2, 2, 1, 1)):
    doms, size = ints[1].shape
    fine_rows = fine_nodes.shape[0]
    nodes = jax.ShapeDtypeStruct((doms, size, LANES), BF16)
    quarter = coarse_rows // 4
    border_size, count = ints[0].shape[0], edges.shape[0]
    vmem = pltpu.VMEM
    return pl.pallas_call(
        functools.partial(main_kernel, groups, pieces),
        out_shape=(
            jax.ShapeDtypeStruct((4, quarter, LANES), BF16),
            jax.ShapeDtypeStruct((fine_rows, LANES), BF16),
        ),
        in_specs=[SMEM] * 6 + [VMEM] * 3 + [ANY] * 2 + [VMEM] * 7,
        out_specs=(VMEM, VMEM),
        scratch_shapes=[
            vmem((4,) + nodes.shape, BF16),
            vmem((4 * doms * size, LANES), F32),
            vmem(part.shape, BF16),
            vmem(fine_nodes.shape, BF16),
            vmem(nodes.shape, BF16),
            pltpu.SemaphoreType.DMA((2,)),
        ]
        + reduce_scratch(part.shape[1], 1)[:3]
        + [
            vmem(nodes.shape, BF16),
            vmem(nodes.shape, BF16),
            vmem((quarter, LANES), F32),
            vmem((coarse_rows, LANES), F32),
            vmem((4, quarter, LANES), BF16),
        ]
        + reduce_scratch(quarter, 1)[:3]
        + [
            vmem((4, quarter, LANES), BF16),
            vmem((4, doms, border_size, LANES), BF16),
            vmem((coarse_rows + 8, LANES), F32),
            vmem((doms * size, LANES), F32),
            vmem((doms, border_size, LANES), BF16),
            vmem((coarse_rows + 4 * doms * border_size, LANES), F32),
            vmem((coarse_rows, LANES), F32),
            vmem((count, LANES), F32),
            vmem(nodes.shape, BF16),
            vmem(nodes.shape, BF16),
        ]
        + reduce_scratch(quarter, groups // 2)[3:]
        + reduce_scratch(quarter, 2)[3:]
        + reduce_scratch(quarter, 2)[3:]
        + relay_sems(2)
        + relay_sems(len(pieces))
        + relay_sems(2)
        + relay_sems(2)
        + exchange_sems(doms)
        + exchange_sems(doms)
        + exchange_sems(doms),
        compiler_params=comm_params(1),
        name="main_stage",
    )(*ints, part, fine_nodes, edges, *weights)


def shards(groups, coarse_rows, *args):
    (
        fine_nodes, fine_edges, fine_senders, fine_receivers, fine_halo,
        coarse_edges, coarse_senders, coarse_receivers, coarse_halo,
        pool_send, pool_dest, unpool_slot,
        edge_in_weight, edge_out_weight, node_in_weight, node_out_weight, edge_gain, node_gain,
    ) = args
    doms = fine_halo.shape[1]
    slots = pool_dest.shape[2]
    widths = (doms, fine_nodes.shape[0], fine_halo.shape[2], coarse_rows, coarse_halo.shape[2], slots)
    senders, far_senders, place, group_dest, border, own, dest, far_border = place_stage(
        groups, widths, (fine_senders, coarse_senders, unpool_slot),
        ((fine_halo[0], 1), (pool_send[0], 1), (pool_dest[0], 1), (coarse_halo[0].T, 0)),
    )
    msg = message_stage(
        doms, groups, border, senders, fine_receivers,
        fine_nodes, fine_edges, edge_in_weight, edge_out_weight, edge_gain,
    )
    part = sum_stage(fine_receivers, place, msg, doms * slots)
    ints = (
        far_border, own, dest, far_senders, coarse_receivers, place,
        pool_dest[0], group_dest, coarse_receivers.reshape(1, -1),
    )
    weights = (edge_in_weight, edge_out_weight, node_in_weight, node_out_weight, edge_gain, node_gain)
    coarse_out, fine_out = main_stage(
        groups, coarse_rows, ints, part.reshape(4, -1, LANES), fine_nodes, coarse_edges, weights
    )
    return fine_out, coarse_out.reshape(-1, LANES)


def solution(mesh, groups=8, coarse_rows=2048):
    placed = (
        P("dom", None),
        P(("dom", "edge"), None),
        P(("dom", "edge")),
        P(("dom", "edge")),
        P("dom", None, None),
        P(("dom", "edge"), None),
        P(("dom", "edge")),
        P(("dom", "edge")),
        P("dom", None, None),
        P("dom", None, None),
        P("dom", None, None),
        P("dom"),
        P(),
        P(),
        P(),
        P(),
        P(),
        P(),
    )
    return jax.shard_map(
        functools.partial(shards, groups, coarse_rows),
        mesh=mesh,
        in_specs=placed,
        out_specs=(P("dom", None), P("dom", None)),
        check_vma=False,
    )
```

```python
import functools

import jax
import jax.numpy as jnp
from jax import lax
from jax.experimental import pallas as pl
from jax.experimental.pallas import tpu as pltpu
from jax.sharding import PartitionSpec as P

F32, BF16 = jnp.float32, jnp.bfloat16
VMEM = pl.BlockSpec(memory_space=pltpu.VMEM)
SMEM = pl.BlockSpec(memory_space=pltpu.SMEM)
ANY = pl.BlockSpec(memory_space=pl.ANY)
LANES = 128


def silu(v):
    return v / (1.0 + jnp.exp(-v))


def normed(v, gain):
    center = v - jnp.mean(v, axis=-1, keepdims=True)
    spread = jnp.mean(center * center, axis=-1, keepdims=True)
    return center * lax.rsqrt(spread + 1e-05) * gain


def dot(a, b):
    return jnp.dot(a, b, preferred_element_type=F32)


def node_mlp(rows, summed, w_in, w_out, gain):
    pre = dot(rows, w_in[0:LANES, :]) + dot(summed.astype(BF16), w_in[LANES : 2 * LANES, :])
    hidden = silu(pre).astype(BF16)
    return (rows.astype(F32) + normed(dot(hidden, w_out), gain)).astype(BF16)


def row_loop(total, step, body):
    def run(i, carry):
        body(pl.multiple_of(i * step, step))
        return carry

    lax.fori_loop(0, total // step, run, 0)


def widen(src, dst, step=512):
    def body(at):
        dst[pl.ds(at, step), :] = src[pl.ds(at, step), :].astype(F32)

    row_loop(src.shape[0], step, body)


def clear_all(accs, step=512):
    def body(at):
        for acc in accs:
            acc[pl.ds(at, step), :] = jnp.zeros((step, LANES), F32)

    row_loop(accs[0].shape[0] // step * step, step, body)


def add_rows(where, values, count, accs, unroll=64):
    def body(at):
        for j in range(unroll):
            acc, row = accs[j % len(accs)], where(at + j)
            acc[pl.ds(row, 1), :] = acc[pl.ds(row, 1), :] + values[pl.ds(at + j, 1), :]

    row_loop(count, unroll, body)


def sum_accs(accs, out, step=512):
    def body(at):
        value = accs[0][pl.ds(at, step), :]
        for acc in accs[1:]:
            value = value + acc[pl.ds(at, step), :]
        out[pl.ds(at, step), :] = value.astype(BF16)

    row_loop(out.shape[0], step, body)


def premultiply(rows, weight, dst, base=0, step=512):
    def body(at):
        dst[pl.ds(pl.multiple_of(base + at, step), step), :] = dot(rows[pl.ds(at, step), :], weight)

    row_loop(rows.shape[0], step, body)


def edge_mlp(msg, w_out, gain, out, step=512):
    def body(at):
        hidden = silu(msg[pl.ds(at, step), :]).astype(BF16)
        out[pl.ds(at, step), :] = normed(dot(hidden, w_out), gain)

    row_loop(msg.shape[0], step, body)


def sum_kernel(receivers, place, msg, out, held, total, sem_in, sem_out, *accs):
    load = pltpu.make_async_copy(msg, held, sem_in)
    load.start()
    clear_all(accs)
    load.wait()
    add_rows(lambda j: place[receivers[j]], held, held.shape[0], accs)
    size = out.shape[0] // 4

    def store(q):
        at = pl.ds(q * size, size)
        return pltpu.make_async_copy(total.at[at], out.at[at], sem_out.at[q])

    for q in range(4):
        at = pl.ds(q * size, size)
        sum_accs([acc.at[at] for acc in accs], total.at[at])
        if q:
            store(q - 1).start()
    store(3).start()
    for q in range(4):
        store(q).wait()


def sum_stage(receivers, place, msg, slots):
    return pl.pallas_call(
        sum_kernel,
        out_shape=jax.ShapeDtypeStruct((slots, LANES), BF16),
        in_specs=[SMEM, SMEM, ANY],
        out_specs=ANY,
        scratch_shapes=[
            pltpu.VMEM(msg.shape, F32),
            pltpu.VMEM((slots, LANES), BF16),
            pltpu.SemaphoreType.DMA,
            pltpu.SemaphoreType.DMA((4,)),
        ]
        + [pltpu.VMEM((slots, LANES), F32)] * 4,
        name="sum_stage",
    )(receivers, place, msg)


def place_kernel(groups, widths, senders, far_senders, slots, lists, out, far_out, place, lined, cuts):
    me = lax.axis_index("dom")
    doms, rows, width, coarse_rows, coarse_width, slot_count = widths
    per = doms // groups

    def over(value, divisor):
        shift = (divisor & -divisor).bit_length() - 1
        left = divisor >> shift
        value = lax.shift_right_logical(value, shift)
        if left == 1:
            return value
        return lax.shift_right_logical(value * ((1 << 16) // left + 1), 16)

    def split(value, divisor):
        high = over(value, divisor)
        return high, value - high * divisor

    def nearby(p):
        group, local = split(p, per)
        away = me // per + groups - group
        away = jnp.where(away >= groups, away - groups, away)
        step = jnp.where(2 * away <= groups, jnp.maximum(2 * away - 1, 0), 2 * (groups - away))
        return step * per + local

    def moved(value, near, wide):
        size = wide // 4
        owner, slot = split(jnp.maximum(value - near, 0), wide)
        quarter, inner = split(slot, size)
        there = near + quarter * (doms * size) + nearby(owner) * size + inner
        return jnp.where(value < near, value, there)

    out[...] = moved(senders[...], rows, width)
    far_out[...] = moved(far_senders[...], coarse_rows, coarse_width)
    owner, slot = split(slots[...], slot_count)
    size = slot_count // 4
    quarter, inner = split(slot, size)
    place[...] = quarter * (doms * size) + nearby(owner) * size + inner

    e = lax.axis_index("edge")
    for whole, cut in zip(lists, cuts):
        axis = 0 if whole.shape[0] != cut.shape[0] else 1
        size = cut.shape[axis]
        pieces = [whole[q * size : (q + 1) * size] if axis == 0 else whole[:, q * size : (q + 1) * size] for q in range(4)]
        value = pieces[3]
        for q in range(3):
            value = jnp.where(e == q, pieces[q], value)
        cut[...] = value
    dest = cuts[2]
    lined[...] = jnp.concatenate([dest[pl.ds(l, groups, stride=per), :] for l in range(per)], axis=1)


def place_stage(groups, widths, ints, lists):
    shaped = [x.reshape(-1, LANES) for x in ints]
    cut_shapes = [
        tuple(n // 4 if i == axis else n for i, n in enumerate(whole.shape)) for whole, axis in lists
    ]
    rows, size = cut_shapes[2]
    shapes = [x.shape for x in shaped] + [(groups, rows // groups * size)] + cut_shapes

    def kernel(*refs):
        k = 3 + len(lists)
        place_kernel(groups, widths, *refs[0:3], refs[3:k], *refs[k : k + 4], refs[k + 4 :])

    results = pl.pallas_call(
        kernel,
        out_shape=[jax.ShapeDtypeStruct(s, jnp.int32) for s in shapes],
        in_specs=[VMEM] * (3 + len(lists)),
        out_specs=[VMEM] * len(shapes),
        name="place_stage",
    )(*shaped, *(whole for whole, _ in lists))
    return [x.reshape(-1) for x in results[:3]] + list(results[3:])


class Net:
    def __init__(self, doms, groups):
        self.doms, self.groups, self.per = doms, groups, doms // groups
        self.me = lax.axis_index("dom")
        self.e = lax.axis_index("edge")
        self.group = self.me // self.per
        self.local = lax.rem(self.me, self.per)
        self.right = lax.rem(self.e + 1, 4)
        self.left = lax.rem(self.e + 3, 4)
        self.opp = lax.rem(self.e + 2, 4)

    def greet(self):
        sem = pltpu.get_barrier_semaphore()
        pl.semaphore_signal(sem, 1, device_id={"edge": self.right})
        pl.semaphore_signal(sem, 1, device_id={"edge": self.left})

        def signal(k, carry):
            pl.semaphore_signal(sem, 1, device_id={"dom": lax.rem(self.me + k, self.doms)})
            return carry

        lax.fori_loop(1, self.doms, signal, 0)

    def meet(self):
        pl.semaphore_wait(pltpu.get_barrier_semaphore(), self.doms + 1)

    def offset(self, t):
        odd = lax.rem(t, 2)
        return odd * ((t + 1) // 2) + (1 - odd) * lax.rem(self.groups - t // 2, self.groups)

    def ahead(self, t):
        return lax.rem(self.group + self.offset(t), self.groups) * self.per

    def behind(self, t):
        return lax.rem(self.group + self.groups - self.offset(t), self.groups) * self.per


class Exchange:
    def __init__(self, net, first, source, target, landed, sems):
        self.net, self.first, self.source, self.target, self.landed = net, first, source, target, landed
        self.send_sem, self.recv_sem, self.own_sem = sems

    def copy(self, t, i):
        net = self.net
        local = lax.rem(net.local + i, net.per)
        peer = self.first(t) + local
        return pltpu.make_async_remote_copy(
            src_ref=self.source(t, peer),
            dst_ref=self.target(t),
            send_sem=self.send_sem.at[t * net.per + local],
            recv_sem=self.recv_sem.at[t * net.per + net.local],
            device_id={"dom": peer},
        )

    def own(self):
        return pltpu.make_async_copy(self.source(0, self.net.me), self.target(0), self.own_sem)

    def each(self, t, body):
        def run(i, carry):
            body(i)
            return carry

        lax.fori_loop(jnp.where(t == 0, 1, 0), self.net.per, run, 0)

    def send(self, t):
        self.each(t, lambda i: self.copy(t, i).start())

    def receive(self, t):
        net = self.net

        def wait(i):
            local = lax.rem(net.local + i, net.per)
            pltpu.make_async_remote_copy(
                src_ref=self.landed(t, local),
                dst_ref=self.landed(t, local),
                send_sem=self.send_sem.at[t * net.per + local],
                recv_sem=self.recv_sem.at[t * net.per + local],
                device_id={"dom": self.first(t) + local},
            ).wait_recv()

        self.each(t, wait)

    def loop(self, body):
        def run(t, carry):
            body(t)
            return carry

        lax.fori_loop(0, self.net.groups, run, 0)

    def finish(self):
        self.own().wait()
        self.loop(lambda t: self.each(t, lambda i: self.copy(t, i).wait_send()))


def exchange_sems(doms):
    return [pltpu.SemaphoreType.DMA((doms,)), pltpu.SemaphoreType.DMA((doms,)), pltpu.SemaphoreType.DMA]


def edge_copy(src, dst, sems, which, slot, to):
    return pltpu.make_async_remote_copy(
        src_ref=src,
        dst_ref=dst,
        send_sem=sems[0].at[which, slot],
        recv_sem=sems[1].at[which, slot],
        device_id={"edge": to},
    )


class Relay:
    def __init__(self, net, out, sems, sizes):
        self.net, self.out, self.sems, self.sizes = net, out, sems, sizes
        self.pieces = len(sizes)

    def range(self, s):
        return sum(self.sizes[:s]), self.sizes[s]

    def copy(self, which, owner, s, half, to):
        first, size = self.range(s)
        if half is None:
            at = pl.ds(first, size)
        else:
            at = pl.ds(first + half * (size // 2), size // 2)
        piece = self.out.at[owner, at]
        return edge_copy(piece, piece, self.sems, which, s, to)

    def first(self, s):
        n = self.net
        self.copy(0, n.e, s, None, n.right).start()
        self.copy(1, n.e, s, None, n.left).start()

    def second(self, s):
        n = self.net
        self.copy(0, n.left, s, None, n.right).wait_recv()
        self.copy(2, n.left, s, 0, n.right).start()
        self.copy(1, n.right, s, None, n.left).wait_recv()
        self.copy(3, n.right, s, 1, n.left).start()

    def finish(self, s):
        n = self.net
        self.copy(2, n.opp, s, 0, n.right).wait_recv()
        self.copy(3, n.opp, s, 1, n.left).wait_recv()
        self.copy(0, n.e, s, None, n.right).wait_send()
        self.copy(1, n.e, s, None, n.left).wait_send()
        self.copy(2, n.left, s, 0, n.right).wait_send()
        self.copy(3, n.right, s, 1, n.left).wait_send()

    def rest(self, got):
        n = self.net
        for s in reversed(range(self.pieces)):
            got(n.e, s)
            self.second(s)
        for s in reversed(range(self.pieces)):
            got(n.left, s)
            got(n.right, s)
        for s in reversed(range(self.pieces)):
            self.finish(s)
            got(n.opp, s)

    def run(self, ready=lambda s: None, work=lambda s: None, got=lambda owner, s: None):
        n, last = self.net, self.pieces - 1
        for s in range(self.pieces + 1):
            if s <= last:
                ready(s)
                self.first(s)
            if s:
                self.second(s - 1)
            work(s)
            if s <= last:
                got(n.e, s)
            if s:
                got(n.left, s - 1)
                got(n.right, s - 1)
        for s in range(self.pieces):
            self.finish(s)
            got(n.opp, s)


def relay_sems(pieces):
    return [pltpu.SemaphoreType.DMA((4, pieces)), pltpu.SemaphoreType.DMA((4, pieces))]


class Reduce:
    def __init__(self, net, part, hop, passed, near, sems, chunks):
        self.net, self.part, self.hop, self.passed, self.near = net, part, hop, passed, near
        self.sems, self.chunks = sems, chunks
        self.half = part.shape[1] // 2
        self.size = self.half // chunks

    def h(self, c):
        return pl.ds(c * self.size, self.size)

    def a(self, c):
        return pl.ds(2 * c * self.size, self.size)

    def b(self, c):
        return pl.ds((2 * c + 1) * self.size, self.size)

    def hop_right(self, c):
        return edge_copy(self.part.at[self.net.opp, self.a(c)], self.hop.at[0, self.h(c)], self.sems, 0, c, self.net.right)

    def hop_left(self, c):
        return edge_copy(self.part.at[self.net.opp, self.b(c)], self.hop.at[1, self.h(c)], self.sems, 1, c, self.net.left)

    def raw_right(self, c):
        return edge_copy(self.part.at[self.net.right, self.b(c)], self.near.at[0, self.b(c)], self.sems, 2, c, self.net.right)

    def raw_left(self, c):
        return edge_copy(self.part.at[self.net.left, self.a(c)], self.near.at[1, self.a(c)], self.sems, 3, c, self.net.left)

    def sum_right(self, c):
        return edge_copy(self.passed.at[0, self.h(c)], self.near.at[0, self.a(c)], self.sems, 4, c, self.net.right)

    def sum_left(self, c):
        return edge_copy(self.passed.at[1, self.h(c)], self.near.at[1, self.b(c)], self.sems, 5, c, self.net.left)

    def loop(self, body):
        def run(c, carry):
            body(c)
            return carry

        lax.fori_loop(0, self.chunks, run, 0)

    def start(self, c):
        self.hop_right(c).start()
        self.hop_left(c).start()
        self.raw_right(c).start()
        self.raw_left(c).start()

    def through(self, c):
        net = self.net
        self.hop_right(c).wait_recv()
        self.passed[0, self.h(c)] = (
            self.hop[0, self.h(c)].astype(F32) + self.part[net.right, self.a(c)].astype(F32)
        ).astype(BF16)
        self.hop_left(c).wait_recv()
        self.passed[1, self.h(c)] = (
            self.hop[1, self.h(c)].astype(F32) + self.part[net.left, self.b(c)].astype(F32)
        ).astype(BF16)
        self.hop_right(c).wait_send()
        self.hop_left(c).wait_send()
        self.sum_right(c).start()
        self.sum_left(c).start()

    def finish(self, c):
        for copy in (self.raw_right(c), self.raw_left(c), self.sum_right(c), self.sum_left(c)):
            copy.wait()

    def run(self, use=lambda c: None, aside=lambda: None):
        order = list(reversed(range(self.chunks)))
        self.start(order[0])
        for k, c in enumerate(order):
            if k + 1 < self.chunks:
                self.start(order[k + 1])
            if k == 0:
                aside()
            self.through(c)
            if k:
                self.finish(order[k - 1])
                use(order[k - 1])
        self.finish(order[-1])
        use(order[-1])

    def value(self, rows):
        return (
            self.part[self.net.e, rows].astype(F32)
            + self.near[0, rows].astype(F32)
            + self.near[1, rows].astype(F32)
        )


def reduce_scratch(rows, chunks):
    return [
        pltpu.VMEM((2, rows // 2, LANES), BF16),
        pltpu.VMEM((2, rows // 2, LANES), BF16),
        pltpu.VMEM((2, rows, LANES), BF16),
        pltpu.SemaphoreType.DMA((6, chunks)),
        pltpu.SemaphoreType.DMA((6, chunks)),
    ]


def gather_blocks(index, base, table, rows, dst, blocks, turned=False):
    size = dst.shape[1]

    def body(i, carry):
        k = blocks[0] + i
        line, at = base(k), pl.multiple_of(k * size, size)
        for j in range(size):
            rows[pl.ds(at + j, 1), :] = table[pl.ds(index[j, line] if turned else index[line, j], 1), :]
        dst[k] = rows[pl.ds(at, size), :].astype(BF16)
        return carry

    lax.fori_loop(0, blocks[1], body, 0)


def message_kernel(
    groups, pieces, halo, senders, receivers, nodes, edges_there, w_in, w_out, gain,
    out, edges, load_sem, out_sem, ghosts, wide, rows, send, from_rows, to_rows, s0, s1, s2, r0, r1,
):
    doms, size = ghosts.shape[1], ghosts.shape[2]
    count, near = edges.shape[0], nodes.shape[0]
    net = Net(doms, groups)
    load = pltpu.make_async_copy(edges_there, edges, load_sem)
    load.start()
    net.greet()
    widen(nodes, wide)
    gather_blocks(halo, lambda k: k, wide, rows, send, (0, doms))
    load.wait()
    net.meet()
    land = ghosts.at[net.e]
    exchange = Exchange(
        net, net.ahead,
        lambda t, peer: send.at[peer],
        lambda t: land.at[t * net.per + net.local],
        lambda t, l: land.at[t * net.per + l],
        (s0, s1, s2),
    )
    exchange.own().start()
    exchange.loop(exchange.send)

    def pick(index, dst):
        def body(at):
            for j in range(64):
                dst[pl.ds(at + j, 1), :] = wide[pl.ds(index[at + j], 1), :]

        row_loop(count, 64, body)

    pick(receivers, to_rows)
    w = w_in[0]

    def known(at):
        block = pl.ds(at, 512)
        to_rows[block, :] = dot(to_rows[block, :].astype(BF16), w[LANES : 2 * LANES, :]) + dot(
            edges[block, :], w[2 * LANES :, :]
        )

    each = groups // pieces

    def ready(s):
        def run(t, carry):
            exchange.receive(t)
            return carry

        lax.fori_loop(s * each, (s + 1) * each, run, 0)
        if s == 0:
            exchange.own().wait()

    def work(s):
        if s == 0:
            row_loop(count // 2, 512, known)
        if s == pieces:
            row_loop(count // 2, 512, lambda at: known(count // 2 + at))

    part = doms // pieces

    def got(owner, s):
        at = pl.multiple_of(near + owner * (doms * size) + s * part * size, 16)
        block = ghosts[owner, pl.ds(s * part, part)].reshape(part * size, LANES)
        wide[pl.ds(at, part * size), :] = block.astype(F32)

    Relay(net, ghosts, (r0, r1), [part] * pieces).run(ready, work, got)
    pick(senders, from_rows)

    def store(k):
        block = pl.ds(pl.multiple_of(k * 512, 512), 512)
        return pltpu.make_async_copy(from_rows.at[block], out.at[block], out_sem.at[k])

    def finish(at):
        block = pl.ds(at, 512)
        pre = dot(from_rows[block, :].astype(BF16), w[0:LANES, :]) + to_rows[block, :]
        from_rows[block, :] = normed(dot(silu(pre).astype(BF16), w_out[0]), gain[0:1, :])

        @pl.when(at > 0)
        def _():
            store(at // 512 - 1).start()

    row_loop(count, 512, finish)
    store(count // 512 - 1).start()
    row_loop(count, 512, lambda at: store(at // 512).wait())
    exchange.loop(lambda t: exchange.each(t, lambda i: exchange.copy(t, i).wait_send()))


def comm_params(collective_id):
    return pltpu.CompilerParams(collective_id=collective_id, has_side_effects=True)


def message_stage(doms, groups, halo, senders, receivers, nodes, edges, w_in, w_out, gain, pieces=2):
    size = halo.shape[1]
    near, count = nodes.shape[0], edges.shape[0]
    return pl.pallas_call(
        functools.partial(message_kernel, groups, pieces),
        out_shape=jax.ShapeDtypeStruct((count, LANES), F32),
        in_specs=[SMEM] * 3 + [VMEM, ANY] + [VMEM] * 3,
        out_specs=ANY,
        scratch_shapes=[
            pltpu.VMEM(edges.shape, BF16),
            pltpu.SemaphoreType.DMA,
            pltpu.SemaphoreType.DMA((count // 512,)),
            pltpu.VMEM((4, doms, size, LANES), BF16),
            pltpu.VMEM((near + 4 * doms * size, LANES), F32),
            pltpu.VMEM((doms * size, LANES), F32),
            pltpu.VMEM((doms, size, LANES), BF16),
            pltpu.VMEM((count, LANES), F32),
            pltpu.VMEM((count, LANES), F32),
        ]
        + exchange_sems(doms)
        + relay_sems(pieces),
        compiler_params=comm_params(0),
        name="message_stage",
    )(halo, senders, receivers, nodes, edges, w_in, w_out, gain)


def child_counts(all_dest, first, counts, at, step):
    lines, width = all_dest.shape

    target = lax.broadcasted_iota(jnp.int32, (step, width), 0) + (first + at)

    def line(i, total):
        for j in range(4):
            hit = all_dest[pl.ds(i * 4 + j, 1), :] == target
            total = total + jnp.where(hit, 1.0, 0.0)
        return total

    total = lax.fori_loop(0, lines // 4, line, jnp.zeros((step, width), F32))
    counts[pl.ds(at, step), :] = jnp.broadcast_to(jnp.sum(total, axis=1, keepdims=True), (step, LANES))


def one_hot(index, first, rows):
    at = lax.broadcasted_iota(jnp.int32, (rows, index.shape[1]), 0) + first
    return jnp.where(at == index, 1.0, 0.0).astype(BF16)


def main_kernel(
    groups, pieces, halo, own, dest, senders, receivers, place, all_dest, group_dest, line_receivers,
    part_there, nodes_there, edges, edge_in, edge_out, node_in, node_out, edge_gain, node_gain,
    coarse_out, fine_out,
    table, fine_wide, part, fine_nodes, nodes, load_sems, hop, passed, near, mid, arrived, counts, pooled, coarse_part, coarse_hop, coarse_passed, coarse_near,
    coarse_in, ghosts, wide, rows, border, table_s, table_r, msg, send, land,
    f0, f1, p0, p1, e0, e1, a0, a1, b0, b1, g0, g1, h0, h1, i0, i1, i2, j0, j1, j2, k0, k1, k2,
):
    doms, size = mid.shape[0], mid.shape[1]
    quarter, border_size = coarse_in.shape[1], ghosts.shape[2]
    coarse_rows, count = 4 * quarter, edges.shape[0]
    net = Net(doms, groups)
    load_part = pltpu.make_async_copy(part_there, part, load_sems.at[0])
    load_nodes = pltpu.make_async_copy(nodes_there, fine_nodes, load_sems.at[1])
    load_nodes.start()
    load_part.start()
    net.greet()
    premultiply(edges, edge_in[1, 2 * LANES :, :], msg)
    load_nodes.wait()
    widen(fine_nodes, fine_wide)

    def line(k):
        return net.behind(k // net.per) + lax.rem(k, net.per)

    half = doms // 2
    gather_blocks(own, line, fine_wide, rows, nodes, (half, half))
    load_part.wait()
    net.meet()

    reduce = Reduce(net, part, hop, passed, near, (f0, f1), groups // 2)
    pool = Exchange(
        net, net.behind,
        lambda t, peer: mid.at[t * net.per + lax.rem(peer, net.per)],
        lambda t: arrived.at[net.me],
        lambda t, l: arrived.at[net.ahead(t) + l],
        (i0, i1, i2),
    )
    span = net.per * size

    def use(c):
        units = (2 * c + 1, 2 * c)
        for u in units:
            own = nodes[u * net.per : (u + 1) * net.per].reshape(span, LANES)
            result = node_mlp(own, reduce.value(pl.ds(u * span, span)), node_in[0], node_out[0], node_gain[0:1, :])
            mid[u * net.per : (u + 1) * net.per] = result.reshape(net.per, size, LANES)
        if c == 0:
            pool.own().start()
        for u in units:
            pool.send(u)
        step = 2 * quarter // groups
        child_counts(all_dest, net.e * quarter, counts, c * step, step)

    def aside():
        gather_blocks(own, line, fine_wide, rows, nodes, (0, half))
        pooled[...] = jnp.zeros_like(pooled)

    reduce.run(use, aside)

    def gathered(k, carry):
        t = groups - 1 - k
        pool.receive(t)

        @pl.when(t == 0)
        def _():
            pool.own().wait()

        first = net.ahead(t)
        block = arrived[pl.ds(first, net.per)].reshape(span, LANES)
        index = group_dest[pl.ds(first // net.per, 1), :]
        for q in range(4):
            at = pl.ds(q * quarter, quarter)
            pooled[at, :] = pooled[at, :] + dot(one_hot(index, q * quarter, quarter), block)
        return carry

    lax.fori_loop(0, groups, gathered, 0)
    for owner in (net.opp, net.right, net.left, net.e):
        at = pl.ds(pl.multiple_of(owner * quarter, quarter), quarter)
        coarse_part[owner] = pooled[at, :].astype(BF16)
    pool.loop(lambda t: pool.each(t, lambda i: pool.copy(t, i).wait_send()))

    def spread(values):
        def got(owner, s):
            at = pl.ds(pl.multiple_of(owner * quarter + s * share, share), share)
            wide[at, :] = values[owner, s * share : (s + 1) * share].astype(F32)

        return got

    reduce = Reduce(net, coarse_part, coarse_hop, coarse_passed, coarse_near, (p0, p1), p0.shape[1])
    chunks = p0.shape[1]
    share = quarter // chunks
    relay = Relay(net, coarse_in, (g0, g1), [share] * chunks)

    def mean(c):
        at = pl.ds(c * share, share)
        coarse_in[net.e, at] = (reduce.value(at) / jnp.maximum(counts[at, :], 1.0)).astype(BF16)
        relay.first(c)

    reduce.run(mean)
    relay.rest(spread(coarse_in))
    gather_blocks(halo, lambda k: k, wide, rows, border, (0, doms), True)
    here = ghosts.at[net.e]
    exchange = Exchange(
        net, net.ahead,
        lambda t, peer: border.at[peer],
        lambda t: here.at[t * net.per + net.local],
        lambda t, l: here.at[t * net.per + l],
        (j0, j1, j2),
    )
    exchange.own().start()
    exchange.loop(exchange.send)
    w = edge_in[1]
    for q in range(4):
        table_r[pl.ds(q * quarter, quarter), :] = dot(coarse_in[q], w[LANES : 2 * LANES, :])
        table_s[pl.ds(q * quarter, quarter), :] = dot(coarse_in[q], w[0:LANES, :])

    def gather_near(at):
        for j in range(32):
            msg[pl.ds(at + j, 1), :] = msg[pl.ds(at + j, 1), :] + table_r[pl.ds(receivers[at + j], 1), :]

    row_loop(count, 32, gather_near)

    def ready(s):
        def run(t, carry):
            exchange.receive(t)
            return carry

        lax.fori_loop(s * (groups // 2), (s + 1) * (groups // 2), run, 0)
        if s == 0:
            exchange.own().wait()

    Relay(net, ghosts, (h0, h1), [doms // 2] * 2).run(ready)
    exchange.loop(lambda t: exchange.each(t, lambda i: exchange.copy(t, i).wait_send()))
    for owner in range(4):
        block = ghosts[owner].reshape(doms * border_size, LANES)
        at = pl.ds(coarse_rows + owner * doms * border_size, doms * border_size)
        table_s[at, :] = dot(block, w[0:LANES, :])

    def gather_far(at):
        for j in range(32):
            msg[pl.ds(at + j, 1), :] = msg[pl.ds(at + j, 1), :] + table_s[pl.ds(senders[at + j], 1), :]

    row_loop(count, 32, gather_far)
    edge_mlp(msg, edge_out[1], edge_gain[1:2, :], msg)
    high = msg[...].astype(BF16)
    low = (msg[...] - high.astype(F32)).astype(BF16)
    both = jnp.concatenate([high, low], axis=1)
    for owner in (net.opp, net.right, net.left, net.e):
        sums = dot(one_hot(line_receivers[...], owner * quarter, quarter), both)
        coarse_part[owner] = (sums[:, 0:LANES] + sums[:, LANES:]).astype(BF16)

    reduce = Reduce(net, coarse_part, coarse_hop, coarse_passed, coarse_near, (e0, e1), e0.shape[1])
    wide[pl.ds(coarse_rows, 8), :] = jnp.zeros((8, LANES), F32)
    relay_out = Relay(net, coarse_out, (a0, a1), [share] * chunks)

    def updated(c):
        at = pl.ds(c * share, share)
        coarse_out[net.e, at] = node_mlp(
            coarse_in[net.e, at], reduce.value(at), node_in[1], node_out[1], node_gain[1:2, :]
        )
        relay_out.first(c)

    reduce.run(updated)
    relay_out.rest(spread(coarse_out))
    back = Exchange(
        net, net.ahead,
        lambda t, peer: send.at[peer],
        lambda t: land.at[t * net.per + net.local],
        lambda t, l: land.at[t * net.per + l],
        (k0, k1, k2),
    )

    def start(t):
        gather_blocks(dest, lambda k: k, wide, rows, send, (net.ahead(t), net.per))
        back.send(t)

    back.loop(start)
    back.own().start()
    ends = [sum(pieces[:s]) for s in range(len(pieces) + 1)]

    def ready(s):
        def run(t, carry):
            back.receive(t)
            return carry

        lax.fori_loop(ends[s], ends[s + 1], run, 0)
        if s == 0:
            back.own().wait()
        block = slice(ends[s] * net.per, ends[s + 1] * net.per)
        table[net.e, block] = (land[block].astype(F32) + mid[block].astype(F32)).astype(BF16)

    relay = Relay(net, table, (b0, b1), [p * net.per for p in pieces])

    def got(owner, s):
        first, count = relay.range(s)
        at = pl.multiple_of(owner * (doms * size) + first * size, 16)
        block = table[owner, pl.ds(first, count)].reshape(count * size, LANES)
        fine_wide[pl.ds(at, count * size), :] = block.astype(F32)

    relay.run(ready, got=got)

    def pick(at):
        for half in (0, 64):
            for j in range(half, half + 64):
                rows[pl.ds(j, 1), :] = fine_wide[pl.ds(place[at + j], 1), :]
            fine_out[pl.ds(at + half, 64), :] = rows[half : half + 64, :].astype(BF16)

    row_loop(fine_out.shape[0], 128, pick)
    back.loop(lambda t: back.each(t, lambda i: back.copy(t, i).wait_send()))


def main_stage(groups, coarse_rows, ints, part, fine_nodes, edges, weights, pieces=(2, 2, 2, 1, 1)):
    doms, size = ints[1].shape
    fine_rows = fine_nodes.shape[0]
    nodes = jax.ShapeDtypeStruct((doms, size, LANES), BF16)
    quarter = coarse_rows // 4
    border_size, count = ints[0].shape[0], edges.shape[0]
    vmem = pltpu.VMEM
    return pl.pallas_call(
        functools.partial(main_kernel, groups, pieces),
        out_shape=(
            jax.ShapeDtypeStruct((4, quarter, LANES), BF16),
            jax.ShapeDtypeStruct((fine_rows, LANES), BF16),
        ),
        in_specs=[SMEM] * 6 + [VMEM] * 3 + [ANY] * 2 + [VMEM] * 7,
        out_specs=(VMEM, VMEM),
        scratch_shapes=[
            vmem((4,) + nodes.shape, BF16),
            vmem((4 * doms * size, LANES), F32),
            vmem(part.shape, BF16),
            vmem(fine_nodes.shape, BF16),
            vmem(nodes.shape, BF16),
            pltpu.SemaphoreType.DMA((2,)),
        ]
        + reduce_scratch(part.shape[1], 1)[:3]
        + [
            vmem(nodes.shape, BF16),
            vmem(nodes.shape, BF16),
            vmem((quarter, LANES), F32),
            vmem((coarse_rows, LANES), F32),
            vmem((4, quarter, LANES), BF16),
        ]
        + reduce_scratch(quarter, 1)[:3]
        + [
            vmem((4, quarter, LANES), BF16),
            vmem((4, doms, border_size, LANES), BF16),
            vmem((coarse_rows + 8, LANES), F32),
            vmem((doms * size, LANES), F32),
            vmem((doms, border_size, LANES), BF16),
            vmem((coarse_rows + 4 * doms * border_size, LANES), F32),
            vmem((coarse_rows, LANES), F32),
            vmem((count, LANES), F32),
            vmem(nodes.shape, BF16),
            vmem(nodes.shape, BF16),
        ]
        + reduce_scratch(quarter, groups // 2)[3:]
        + reduce_scratch(quarter, 2)[3:]
        + reduce_scratch(quarter, 2)[3:]
        + relay_sems(2)
        + relay_sems(len(pieces))
        + relay_sems(2)
        + relay_sems(2)
        + exchange_sems(doms)
        + exchange_sems(doms)
        + exchange_sems(doms),
        compiler_params=comm_params(1),
        name="main_stage",
    )(*ints, part, fine_nodes, edges, *weights)


def shards(groups, coarse_rows, *args):
    (
        fine_nodes, fine_edges, fine_senders, fine_receivers, fine_halo,
        coarse_edges, coarse_senders, coarse_receivers, coarse_halo,
        pool_send, pool_dest, unpool_slot,
        edge_in_weight, edge_out_weight, node_in_weight, node_out_weight, edge_gain, node_gain,
    ) = args
    doms = fine_halo.shape[1]
    slots = pool_dest.shape[2]
    widths = (doms, fine_nodes.shape[0], fine_halo.shape[2], coarse_rows, coarse_halo.shape[2], slots)
    senders, far_senders, place, group_dest, border, own, dest, far_border = place_stage(
        groups, widths, (fine_senders, coarse_senders, unpool_slot),
        ((fine_halo[0], 1), (pool_send[0], 1), (pool_dest[0], 1), (coarse_halo[0].T, 0)),
    )
    msg = message_stage(
        doms, groups, border, senders, fine_receivers,
        fine_nodes, fine_edges, edge_in_weight, edge_out_weight, edge_gain,
    )
    part = sum_stage(fine_receivers, place, msg, doms * slots)
    ints = (
        far_border, own, dest, far_senders, coarse_receivers, place,
        pool_dest[0], group_dest, coarse_receivers.reshape(1, -1),
    )
    weights = (edge_in_weight, edge_out_weight, node_in_weight, node_out_weight, edge_gain, node_gain)
    coarse_out, fine_out = main_stage(
        groups, coarse_rows, ints, part.reshape(4, -1, LANES), fine_nodes, coarse_edges, weights
    )
    return fine_out, coarse_out.reshape(-1, LANES)


def solution(mesh, groups=8, coarse_rows=2048):
    placed = (
        P("dom", None),
        P(("dom", "edge"), None),
        P(("dom", "edge")),
        P(("dom", "edge")),
        P("dom", None, None),
        P(("dom", "edge"), None),
        P(("dom", "edge")),
        P(("dom", "edge")),
        P("dom", None, None),
        P("dom", None, None),
        P("dom", None, None),
        P("dom"),
        P(),
        P(),
        P(),
        P(),
        P(),
        P(),
    )
    return jax.shard_map(
        functools.partial(shards, groups, coarse_rows),
        mesh=mesh,
        in_specs=placed,
        out_specs=(P("dom", None), P("dom", None)),
        check_vma=False,
    )
```
